32 devices in a mesh: row: 16 (over z, y, core), col: 2 (over x).
Axes of the slice: x: 2, y: 2, z: 4, core: 2. Of those that a mesh axis runs over, the one named last changes fastest.
Arguments:
- start_block: float32 [4096, 256], P(('row', 'col')), may hold values from -6 to 6
- tiles: bfloat16 [16, 2, 14, 128, 128], P('row', 'col'), may hold values from -0.125 to 0.125
- tile_rows: int32 [16, 2, 14], P('row', 'col'), may hold values from -1 to 31, as said below
- tile_cols: int32 [16, 2, 14], P('row', 'col'), may hold values from -1 to 31, as said below
- bounds: float32 [3], replicated, may hold values from -2.6 to 2.6, as said below
Outputs:
- filtered: float32 [4096, 256], P(('row', 'col'))
The draws below stay inside these ranges and needn't reach their ends.
Inputs may be any that keep to these rules, and one draw needn't show every extreme that they name: Vector rows form blocks of 128 rows, one block a device, in row+col order. On the device at grid row r and grid column c, a live slot names a block row held by one of the devices (r, any column) and a block column held by one of the devices (any row, c). Live slots come first; each device has 1 to 14 live slots, and one device has exactly 14 in every draw. No block position is named twice, and the mirror of a named position is never named unless it lies on the diagonal. tile_rows and tile_cols are -1 together. `tile_cols`: same slots as tile_rows. bounds[0] < bounds[1] < bounds[2].
All inputs are finite; a program needn't handle non-finite values.
Results may differ from the reference program's by a relative error of at most 0.0042.
Values may be sent and summed in bfloat16 or wider, within the bound.
A program may use at most 64 MiB of HBM per device.

```python
import jax
import jax.numpy as jnp
from jax import lax

K = 256
TILE = 128
BLK_DEV = 1
TILES_DEV = 14
DEGREE = 4
ORDER = 4096
N_ROW = 16
N_COL = 2


def tile_pattern(key):
    base = jax.random.fold_in(key, 7)
    group_count = N_ROW * N_COL
    near_count = N_COL * BLK_DEV
    far_count = N_ROW * BLK_DEV
    positions = near_count * far_count
    shape = (N_ROW, N_COL, near_count, far_count)
    row_grid = lax.broadcasted_iota(jnp.int32, shape, 0)
    col_grid = lax.broadcasted_iota(jnp.int32, shape, 1)
    near_grid = lax.broadcasted_iota(jnp.int32, shape, 2)
    far_grid = lax.broadcasted_iota(jnp.int32, shape, 3)
    glob_i = row_grid * near_count + near_grid
    glob_j = (far_grid // BLK_DEV * N_COL + col_grid) * BLK_DEV + far_grid % BLK_DEV
    parity = (glob_i + glob_j) % 2
    keep = (glob_i == glob_j) | (glob_i < glob_j) & (parity == 0) | (glob_i > glob_j) & (parity == 1)
    upper = max(2, (1 << 30) // positions)
    flat_index = near_grid * far_count + far_grid
    scores = jax.random.randint(jax.random.fold_in(base, 1), shape, 0, upper) * positions + flat_index
    scores = jnp.where(keep, scores, -1).reshape(N_ROW, N_COL, positions)
    chosen_scores, chosen = lax.top_k(scores, TILES_DEV)
    chosen = chosen.astype(jnp.int32)
    counts = jax.random.randint(jax.random.fold_in(base, 2), (N_ROW, N_COL), TILES_DEV // 8, TILES_DEV + 1)
    full_device = jax.random.randint(jax.random.fold_in(base, 3), (), 0, group_count)
    device_ids = lax.broadcasted_iota(jnp.int32, (N_ROW, N_COL), 0) * N_COL + lax.broadcasted_iota(jnp.int32, (N_ROW, N_COL), 1)
    counts = jnp.where(device_ids == full_device, TILES_DEV, counts)
    slot_shape = (N_ROW, N_COL, TILES_DEV)
    slot_ids = lax.broadcasted_iota(jnp.int32, slot_shape, 2)
    alive = slot_ids < counts[:, :, None]
    near_sel = chosen // far_count
    far_sel = chosen % far_count
    row_slot = lax.broadcasted_iota(jnp.int32, slot_shape, 0)
    col_slot = lax.broadcasted_iota(jnp.int32, slot_shape, 1)
    glob_rows = row_slot * near_count + near_sel
    glob_cols = (far_sel // BLK_DEV * N_COL + col_slot) * BLK_DEV + far_sel % BLK_DEV
    return (jnp.where(alive, glob_rows, -1), jnp.where(alive, glob_cols, -1))


def draw_tile_rows(key, part):
    return tile_pattern(key)[0]


def draw_tile_cols(key, part):
    return tile_pattern(key)[1]


def draw_bounds(key, part):
    uniform_part = jax.random.uniform(jax.random.fold_in(key, 11), (3,), jnp.float32)
    lowest = jnp.array([-2.6, -1.2, 2.3], jnp.float32)
    spread = jnp.array([0.3, 0.4, 0.3], jnp.float32)
    return lowest + uniform_part * spread


def block_levels(key, dims, shards, smallest, high):
    def one(dim, shards_of):
        heights = jax.random.uniform(jax.random.fold_in(jax.random.fold_in(key, 6), dim), (shards_of,), jnp.float32, smallest / len(shards), high / len(shards))
        return jnp.repeat(jnp.exp(heights), dims[dim] // shards_of).reshape((-1,) + (1,) * (len(dims) - dim - 1))

    factor_of = one(*shards[0])
    for cut in shards[1:]:
        factor_of = factor_of * one(*cut)
    return factor_of


def gaussian(own_key, shape, scale, limit, pieces=(), kind=jnp.bfloat16):
    result = jax.random.normal(own_key, shape, jnp.float32) * scale
    if len(pieces) > 0:
        result = block_levels(own_key, shape, pieces, -0.22, 0.18) * result
    return jnp.clip(result, min=-limit, max=limit).astype(kind)


def setup_inputs(seed: int = 0) -> dict:
    key_list = jax.random.split(jax.random.key(seed), 6)
    return {
        "start_block": gaussian(key_list[0], (ORDER, K), 1.0, 6.0, ((0, 32),), jnp.float32),
        "tiles": gaussian(key_list[1], (N_ROW, N_COL, TILES_DEV, TILE, TILE), (TILE * 9 * TILES_DEV // (8 * BLK_DEV)) ** -0.5, 0.125, ((0, 16), (1, 2))),
        "tile_rows": draw_tile_rows(jax.random.fold_in(key_list[5], 71), 0),
        "tile_cols": draw_tile_cols(jax.random.fold_in(key_list[5], 71), 0),
        "bounds": draw_bounds(jax.random.fold_in(key_list[5], 71), 0),
    }


def apply_matrix(vectors, tiles, tile_rows, tile_cols):
    block_count = N_ROW * N_COL * BLK_DEV
    group_count = N_ROW * N_COL
    low_vectors = lax.optimization_barrier(vectors.astype(jnp.bfloat16))
    blocks_f = low_vectors.astype(jnp.float32).reshape(block_count, TILE, K)
    tile_sets = tiles.reshape(group_count, TILES_DEV, TILE, TILE)
    row_sets = tile_rows.reshape(group_count, TILES_DEV)
    col_sets = tile_cols.reshape(group_count, TILES_DEV)

    def one_group(accum, item):
        tile_mats, rows_here, cols_here = item
        tile_f = tile_mats.astype(jnp.float32)
        is_live = rows_here >= 0
        rows_safe = jnp.maximum(rows_here, 0)
        cols_safe = jnp.maximum(cols_here, 0)
        forward = jnp.einsum('txy,tyk->txk', tile_f, blocks_f[cols_safe], precision=lax.Precision.HIGHEST)
        backward = jnp.einsum('tyx,tyk->txk', tile_f, blocks_f[rows_safe], precision=lax.Precision.HIGHEST)
        accum = accum.at[jnp.where(is_live, rows_here, block_count)].add(forward, mode="drop")
        accum = accum.at[jnp.where(is_live, cols_here, block_count)].add(backward, mode="drop")
        return accum, None

    start = jnp.zeros((block_count, TILE, K), jnp.float32)
    accum, _ = lax.scan(one_group, start, (tile_sets, row_sets, col_sets))
    return accum.reshape(block_count * TILE, K)


def reference(start_block, tiles, tile_rows, tile_cols, bounds):
    half_width = (bounds[2] - bounds[1]) * 0.5
    center = (bounds[2] + bounds[1]) * 0.5
    sigma_one = half_width / (bounds[0] - center)
    previous = start_block
    current = (apply_matrix(start_block, tiles, tile_rows, tile_cols) - center * start_block) * (sigma_one / half_width)
    sigma = sigma_one
    for turn_index in range(DEGREE - 1):
        sigma_next = 1.0 / (2.0 / sigma_one - sigma)
        product = apply_matrix(current, tiles, tile_rows, tile_cols)
        following = (product - center * current) * (2.0 * sigma_next / half_width) - (sigma * sigma_next) * previous
        previous = current
        current = following
        sigma = sigma_next
    return current
```

```python
import functools
import math

import jax
import jax.numpy as jnp
from jax import lax
from jax.experimental import pallas as pl
from jax.experimental.pallas import tpu as pltpu
from jax.sharding import PartitionSpec as P

DEGREE = 4
CHAINS = 2
LAG = 0
PARTS = 2
ROOM = 48 * 1024 * 1024
MESH = pl.DeviceIdType.MESH


def wide_kernel(
    far, near, slots, tile, width,
    rows_ref, cols_ref, bounds_ref, start_ref, tiles_ref, out_ref,
    placed, owned, mirror, window, diagonal, low, partial, arrived, mine, state,
    tile_send, tile_recv, low_send, low_recv, part_send, part_recv,
):
    chips = far // 2
    tall = far // 4
    count = far * near
    cut = width // CHAINS
    row = lax.axis_index("row")
    col = lax.axis_index("col")
    me = row * near + col
    core = row % 2
    mid = row // 2 % 2
    high = row // 4

    def spot(high_at, mid_at, core_at):
        return core_at * chips + high_at * 2 + mid_at

    def row_of(high_at, mid_at, core_at):
        return (high_at * 2 + mid_at) * 2 + core_at

    own_spot = spot(high, mid, core)

    barrier = pltpu.get_barrier_semaphore()

    def greet(step, carry):
        other = (me + step) % count
        pl.semaphore_signal(
            barrier, inc=1, device_id=(other // near, other % near), device_id_type=MESH
        )
        return carry

    lax.fori_loop(1, count, greet, 0)

    line = (1, cut)
    lowest = jnp.full(line, bounds_ref[0], jnp.float32)
    lower = jnp.full(line, bounds_ref[1], jnp.float32)
    upper = jnp.full(line, bounds_ref[2], jnp.float32)
    half_width = (upper - lower) * 0.5
    center = (upper + lower) * 0.5
    sigma_one = half_width / (lowest - center)

    def columns(chain):
        return slice(chain * cut, (chain + 1) * cut)

    for chain in range(CHAINS):
        low[0, chain, own_spot] = start_ref[:, columns(chain)].astype(jnp.bfloat16)

    for slot in range(slots):
        placed[slot] = tiles_ref[slot]
    placed[slots] = jnp.zeros((tile, tile), jnp.bfloat16)
    places = []
    for slot in range(slots):
        glob_row = rows_ref[slot]
        glob_col = cols_ref[slot]
        place = (glob_col // near) * near + (glob_row - row * near)
        places.append(jnp.where(glob_row >= 0, place, -1))

    def put(position, carry):
        chosen = jnp.int32(slots)
        for slot in range(slots):
            chosen = jnp.where(places[slot] == position, slot, chosen)
        owned[position] = placed[chosen]
        return carry

    lax.fori_loop(0, count, put, 0)
    diagonal[...] = owned[me]
    mirror[me] = diagonal[...]
    owned[me] = jnp.zeros((tile, tile), jnp.bfloat16)

    pl.semaphore_wait(barrier, count - 1)

    flip = high >= tall // 2
    near_end = jnp.where(flip, tall - 1 - high, high)

    def along(position):
        return jnp.where(flip, tall - 1 - position, position)

    def ranked(index):
        return index + jnp.where(index >= near_end, 1, 0)

    def send_low(step, chain, place, target_row):
        pltpu.make_async_remote_copy(
            src_ref=low.at[step, chain, place],
            dst_ref=low.at[step, chain, place],
            send_sem=low_send.at[step, chain],
            recv_sem=low_recv.at[step, chain, place],
            device_id=(target_row, col),
            device_id_type=MESH,
        ).start()

    def await_low(step, chain, place):
        here = low.at[step, chain, place]
        pltpu.make_async_copy(here, here, low_recv.at[step, chain, place]).wait()

    def begin(step, chain):
        send_low(step, chain, own_spot, row_of(high, 1 - mid, core))
        for index in range(tall - 1):
            send_low(step, chain, own_spot, row_of(along(ranked(index)), mid, core))
        send_low(step, chain, own_spot, row_of(high, mid, 1 - core))

    def forward_line(step, chain):
        for index in range(tall - 1):
            place = spot(along(ranked(index)), mid, core)
            await_low(step, chain, place)
            send_low(step, chain, place, row_of(high, 1 - mid, core))
            send_low(step, chain, place, row_of(high, mid, 1 - core))

    def forward_mid(step, chain):
        for index in range(tall):
            source = high if index == 0 else along(ranked(index - 1))
            place = spot(source, 1 - mid, core)
            await_low(step, chain, place)
            send_low(step, chain, place, row_of(high, mid, 1 - core))

    def await_core(step, chain):
        for offset in range(tall):
            for mid_at in range(2):
                await_low(step, chain, spot((high + offset) % tall, mid_at, 1 - core))

    def send_tiles(high_at):
        inner = me % (4 * near)

        def send_tile(offset, carry):
            other = high_at * (4 * near) + (inner + offset) % (4 * near)
            pltpu.make_async_remote_copy(
                src_ref=owned.at[other],
                dst_ref=mirror.at[me],
                send_sem=tile_send,
                recv_sem=tile_recv.at[row],
                device_id=(other // near, other % near),
                device_id_type=MESH,
            ).start()
            return carry

        return send_tile

    def send_group(index):
        if index < 0:
            lax.fori_loop(1, 4 * near, send_tiles(high), 0)
        else:
            lax.fori_loop(0, 4 * near, send_tiles(along(ranked(index))), 0)

    def build(step, carry):
        source = (row + far - step) % far
        base = source * near
        group = mirror.at[pl.ds(base, near)]
        pltpu.make_async_copy(group, group, tile_recv.at[source]).wait()
        fill(source)
        return carry

    def fill(source):
        lanes = (source % 2) * chips + source // 2
        lanes = pl.ds(pl.multiple_of(lanes * tile, tile), tile)
        for near_at in range(near):
            index = source * near + near_at
            window[near_at * tile : (near_at + 1) * tile, lanes] = (
                owned[index] + mirror[index].T
            )

    def multiply(step, chain, near_at):
        total = jnp.zeros((tile, cut), jnp.float32)
        matrix = window[pl.ds(pl.multiple_of(near_at * tile, tile), tile), :]
        vectors = low[step, chain].reshape(far * tile, cut)
        return total + jnp.dot(matrix, vectors, preferred_element_type=jnp.float32)

    def product(step, chain):
        for offset in range(1, near):
            other = (col + offset) % near
            partial[step, chain, other] = multiply(step, chain, other)
            pltpu.make_async_remote_copy(
                src_ref=partial.at[step, chain, other],
                dst_ref=arrived.at[step, chain, col],
                send_sem=part_send.at[step, chain],
                recv_sem=part_recv.at[step, chain, col],
                device_id=(row, other),
                device_id_type=MESH,
            ).start()
        mine[chain] = multiply(step, chain, col) + jnp.dot(
            diagonal[...], low[step, chain, own_spot], preferred_element_type=jnp.float32
        )

    def finish(step, chain, sigma):
        total = mine[chain]
        for offset in range(1, near):
            other = (col + offset) % near
            here = arrived.at[step, chain, other]
            pltpu.make_async_copy(here, here, part_recv.at[step, chain, other]).wait()
            total = total + arrived[step, chain, other]
        where = columns(chain)
        current = start_ref[:, where] if step == 0 else state[step - 1, :, where]
        if step == 0:
            following = (total - center * current) * (sigma_one / half_width)
            sigma_next = sigma_one
        else:
            before = start_ref[:, where] if step == 1 else state[step - 2, :, where]
            sigma_next = 1.0 / (2.0 / sigma_one - sigma)
            following = (total - center * current) * (
                2.0 * sigma_next / half_width
            ) - (sigma * sigma_next) * before
        if step == DEGREE - 1:
            out_ref[:, where] = following
        else:
            low[step + 1, chain, own_spot] = following.astype(jnp.bfloat16)
            begin(step + 1, chain)
            state[step, :, where] = following
        return sigma_next

    for chain in range(CHAINS):
        begin(0, chain)
    groups = list(range(tall - 2, -2, -1))
    for index in groups:
        send_group(index)
    for chain in range(CHAINS):
        forward_line(0, chain)
    for chain in range(CHAINS):
        forward_mid(0, chain)

    if near > 1:
        group = mirror.at[pl.ds(row * near, near - 1)]
        pltpu.make_async_copy(group, group, tile_recv.at[row]).wait()
    fill(row)
    lax.fori_loop(1, far, build, 0)

    sigmas = [sigma_one] * CHAINS

    def phase(chain, index):
        step, part = index // 4, index % 4
        if part == 0:
            forward_line(step, chain)
        elif part == 1:
            forward_mid(step, chain)
        elif part == 2:
            await_core(step, chain)
            product(step, chain)
        else:
            sigmas[chain] = finish(step, chain, sigmas[chain])

    for index in range(2, 4 * DEGREE + LAG * (CHAINS - 1)):
        for chain in range(CHAINS):
            own_index = index - LAG * chain
            if 2 <= own_index < 4 * DEGREE:
                phase(chain, own_index)

    group = owned.at[pl.ds(0, count - 1)]
    pltpu.make_async_copy(group, group, tile_send).wait()
    for step in range(DEGREE):
        for chain in range(CHAINS):
            group = low.at[step, chain, pl.ds(0, far - 1)]
            pltpu.make_async_copy(group, group, low_send.at[step, chain]).wait()
            if near > 1:
                group = partial.at[step, chain, pl.ds(0, near - 1)]
                pltpu.make_async_copy(group, group, part_send.at[step, chain]).wait()


def plane_kernel(
    tall, near, slots, tile, width,
    rows_ref, cols_ref, bounds_ref, start_ref, tiles_ref, out_ref,
    placed, owned, direct, mirror, forward, backward, give, take, low,
    part_out, part_in, mine, state, last, last_in,
    near_tiles_send, far_tiles_send, core_tiles_send, core_far_send,
    near_tiles_recv, far_tiles_recv, core_tiles_recv, core_far_recv,
    give_send, give_recv, low_send, line_send, low_recv, line_recv,
    part_send, back_send, part_recv, back_recv, last_send, last_recv,
):
    far = 4 * tall
    count = far * near
    plane = 2 * near
    line = tall // 2
    half = width // 2
    cut = half // PARTS
    pair = 2 * tile
    row = lax.axis_index("row")
    col = lax.axis_index("col")
    core = row % 2
    mid = row // 2 % 2
    high = row // 4
    here = mid * near + col

    def device(high_at, mid_at, core_at, col_at):
        return ((high_at * 2 + mid_at) * 2 + core_at, col_at)

    def beside(offset):
        other = (here + offset) % plane
        return device(high, other // near, core, other % near)

    partner = device(high, mid, 1 - core, col)

    from_ok = [high != 2 * m for m in range(line)]
    from_at = [
        jnp.where(high < 2 * m, high + tall - 2 * m, high - 2 * m - 1) for m in range(line)
    ]
    into_ok = [high != tall - 1 - 2 * m for m in range(line)]
    into_at = [
        jnp.where(high >= tall - 2 * m, high - tall + 2 * m, high + 2 * m + 1)
        for m in range(line)
    ]

    def copy(src, dst, send, recv, to):
        pltpu.make_async_remote_copy(
            src_ref=src, dst_ref=dst, send_sem=send, recv_sem=recv,
            device_id=to, device_id_type=MESH,
        ).start()

    def wait(ref, sem):
        pltpu.make_async_copy(ref, ref, sem).wait()

    barrier = pltpu.get_barrier_semaphore()

    def greet(step, carry):
        other = (row // 2 * near + col + step) % (far // 2 * near)
        pl.semaphore_signal(
            barrier, inc=1, device_id=(other // near * 2 + core, other % near),
            device_id_type=MESH,
        )
        return carry

    lax.fori_loop(1, far // 2 * near, greet, 0)
    pl.semaphore_signal(barrier, inc=1, device_id=partner, device_id_type=MESH)

    span = (1, pair)
    lowest = jnp.full(span, bounds_ref[0], jnp.float32)
    lower = jnp.full(span, bounds_ref[1], jnp.float32)
    upper = jnp.full(span, bounds_ref[2], jnp.float32)
    half_width = (upper - lower) * 0.5
    center = (upper + lower) * 0.5
    sigma_one = half_width / (lowest - center)

    def lanes(at, size):
        return pl.ds(pl.multiple_of(at * size, size), size)

    give[...] = start_ref[:, lanes(1 - core, half)].T
    kept = start_ref[:, lanes(core, half)].T
    for chain in range(PARTS):
        state[0, chain, :, lanes(core, tile)] = kept[chain * cut : (chain + 1) * cut]

    for slot in range(slots):
        placed[slot] = tiles_ref[slot]
    placed[slots] = jnp.zeros((tile, tile), jnp.bfloat16)
    places = []
    for slot in range(slots):
        glob_row = rows_ref[slot]
        glob_col = cols_ref[slot]
        place = (glob_col // near) * near + (glob_row - row * near)
        places.append(jnp.where(glob_row >= 0, place, -1))

    def put(position, carry):
        chosen = jnp.int32(slots)
        for slot in range(slots):
            chosen = jnp.where(places[slot] == position, slot, chosen)
        owned[position // near, position % near] = placed[chosen]
        return carry

    lax.fori_loop(0, count, put, 0)

    def owned_at(high_at, mid_at):
        return pl.ds((high_at * 2 + mid_at) * 2, 2)

    direct[0, mid, core] = owned[owned_at(high, mid)]
    for m in range(line):

        @pl.when(from_ok[m])
        def _(m=m):
            direct[1 + m, mid, core] = owned[owned_at(from_at[m], mid)]

        @pl.when(jnp.logical_not(from_ok[m]))
        def _(m=m):
            forward[:, (1 + m) * pair : (2 + m) * pair] = jnp.zeros(
                (plane * pair, pair), jnp.bfloat16
            )
            backward[(1 + m) * pair : (2 + m) * pair, :] = jnp.zeros(
                (pair, plane * pair), jnp.bfloat16
            )
            for step in range(DEGREE):
                for chain in range(PARTS):
                    low[step, chain, plane + m] = jnp.zeros((cut, pair), jnp.bfloat16)

        @pl.when(jnp.logical_not(into_ok[m]))
        def _(m=m):
            for step in range(DEGREE):
                for chain in range(PARTS):
                    part_in[step, chain, plane - 1 + m] = jnp.zeros((cut, pair), jnp.bfloat16)

    pl.semaphore_wait(barrier, far // 2 * near)

    copy(give, take, give_send, give_recv, partner)
    for m in reversed(range(line)):

        @pl.when(into_ok[m])
        def _(m=m):
            for offset in range(near):
                other = (col + offset) % near
                copy(
                    owned.at[pl.ds(into_at[m] * 4, 4), other], mirror.at[m, core, col],
                    far_tiles_send.at[m], far_tiles_recv.at[m, col],
                    device(into_at[m], mid, core, other),
                )

    def each_slot(act):
        act(0, high)
        for m in range(line):

            @pl.when(from_ok[m])
            def _(m=m):
                act(1 + m, from_at[m])

    def send_near(slot, high_at):
        copy(
            owned.at[owned_at(high_at, 1 - mid)], direct.at[slot, mid, core],
            near_tiles_send.at[slot], near_tiles_recv.at[slot],
            device(high, 1 - mid, core, col),
        )
        copy(
            owned.at[owned_at(high_at, mid)], direct.at[slot, mid, core],
            core_tiles_send.at[slot, 0], core_tiles_recv.at[slot, 0], partner,
        )

    each_slot(send_near)

    def begin(step, chain):
        own = low.at[step, chain, 0]
        for m in reversed(range(line)):

            @pl.when(into_ok[m])
            def _(m=m):
                copy(
                    own, low.at[step, chain, plane + m],
                    line_send.at[step, chain, m], line_recv.at[step, chain, m],
                    device(into_at[m], mid, core, col),
                )

        for offset in range(1, plane):
            copy(
                own, low.at[step, chain, plane - offset],
                low_send.at[step, chain], low_recv.at[step, chain], beside(offset),
            )

    wait(take, give_recv)
    for chain in range(PARTS):
        state[0, chain, :, lanes(1 - core, tile)] = take[chain * cut : (chain + 1) * cut, :]
        low[0, chain, 0] = state[0, chain].astype(jnp.bfloat16)
        begin(0, chain)

    def pass_near(slot, high_at):
        block = direct.at[slot, 1 - mid, core]
        wait(block, near_tiles_recv.at[slot])
        copy(
            block, block, core_tiles_send.at[slot, 1], core_tiles_recv.at[slot, 1], partner
        )

    each_slot(pass_near)

    def pass_far(m, offset):
        other = (col + offset) % near
        block = mirror.at[m, core, other]
        wait(block, far_tiles_recv.at[m, other])
        copy(block, block, core_far_send.at[m, other], core_far_recv.at[m, other], partner)

    for m in range(line):

        @pl.when(from_ok[m])
        def _(m=m):
            for offset in range(near):
                pass_far(m, offset)

    def spots(index, slot):
        mid_at = index // (4 * near)
        core_at = index // (2 * near) % 2
        other_core = index // near % 2
        col_at = index % near
        offset = (mid_at * near + col_at + plane - here) % plane
        inner = pl.ds(pl.multiple_of((offset * 2 + core_at) * tile, tile), tile)
        outer = pl.ds(pl.multiple_of((slot * 2 + other_core) * tile, tile), tile)
        return mid_at, core_at, other_core, col_at, inner, outer

    def fill_own(index, carry):
        mid_at, core_at, other_core, col_at, inner, outer = spots(index, 0)
        block = direct[0, mid_at, core_at, other_core, col_at]
        forward[inner, outer] = block
        backward[outer, inner] = block.T
        return carry

    def fill_far(m):
        def fill(index, carry):
            mid_at, core_at, other_core, col_at, inner, outer = spots(index, 1 + m)
            block = direct[1 + m, mid_at, core_at, other_core, col_at]
            other = mirror[m, other_core, col_at, mid_at * 2 + core_at]
            forward[inner, outer] = block + other.T
            backward[outer, inner] = block.T + other
            return carry

        return fill

    def await_near(slot, high_at):
        wait(direct.at[slot, mid, 1 - core], core_tiles_recv.at[slot, 0])
        wait(direct.at[slot, 1 - mid, 1 - core], core_tiles_recv.at[slot, 1])

    blocks = 8 * near
    await_near(0, high)
    lax.fori_loop(0, blocks, fill_own, 0)
    for m in range(line):

        @pl.when(from_ok[m])
        def _(m=m):
            await_near(1 + m, from_at[m])
            for other in range(near):
                wait(mirror.at[m, 1 - core, other], core_far_recv.at[m, other])
            lax.fori_loop(0, blocks, fill_far(m), 0)

    def product(step, chain):
        wait(low.at[step, chain, pl.ds(1, plane - 1)], low_recv.at[step, chain])
        total = jnp.zeros((cut, (1 + line) * pair), jnp.float32)
        for offset in range(plane):
            total = total + jnp.dot(
                low[step, chain, offset], forward[offset * pair : (offset + 1) * pair, :],
                preferred_element_type=jnp.float32,
            )
        kept = total[:, :pair]
        for m in range(line):
            at = plane - 1 + m
            part_out[step, chain, at] = total[:, (1 + m) * pair : (2 + m) * pair].astype(
                jnp.bfloat16
            )
        for m in reversed(range(line)):

            @pl.when(from_ok[m])
            def _(m=m):
                at = plane - 1 + m
                copy(
                    part_out.at[step, chain, at], part_in.at[step, chain, at],
                    back_send.at[step, chain, m], back_recv.at[step, chain, m],
                    device(from_at[m], mid, core, col),
                )

        for m in range(line):

            @pl.when(from_ok[m])
            def _(m=m):
                wait(low.at[step, chain, plane + m], line_recv.at[step, chain, m])

        total = jnp.dot(
            low[step, chain, 0], backward[:pair, :], preferred_element_type=jnp.float32
        )
        for m in range(line):
            total = total + jnp.dot(
                low[step, chain, plane + m], backward[(1 + m) * pair : (2 + m) * pair, :],
                preferred_element_type=jnp.float32,
            )
        mine[chain] = kept + total[:, :pair]
        for offset in range(1, plane):
            part_out[step, chain, offset - 1] = total[
                :, offset * pair : (offset + 1) * pair
            ].astype(jnp.bfloat16)
            copy(
                part_out.at[step, chain, offset - 1],
                part_in.at[step, chain, plane - offset - 1],
                part_send.at[step, chain], part_recv.at[step, chain], beside(offset),
            )

    def finish(step, chain, sigma):
        wait(part_in.at[step, chain, pl.ds(0, plane - 1)], part_recv.at[step, chain])
        for m in range(line):

            @pl.when(into_ok[m])
            def _(m=m):
                wait(part_in.at[step, chain, plane - 1 + m], back_recv.at[step, chain, m])

        total = mine[chain]
        for at in range(plane - 1 + line):
            total = total + part_in[step, chain, at].astype(jnp.float32)
        current = state[step, chain]
        if step == 0:
            sigma_next = sigma_one
            following = (total - center * current) * (sigma_one / half_width)
        else:
            sigma_next = 1.0 / (2.0 / sigma_one - sigma)
            following = (total - center * current) * (
                2.0 * sigma_next / half_width
            ) - (sigma * sigma_next) * state[step - 1, chain]
        if step == DEGREE - 1:
            last[chain] = following
            copy(
                last.at[chain, :, lanes(1 - core, tile)], last_in.at[chain],
                last_send.at[chain], last_recv.at[chain], partner,
            )
        else:
            low[step + 1, chain, 0] = following.astype(jnp.bfloat16)
            begin(step + 1, chain)
            state[step + 1, chain] = following
        return sigma_next

    sigmas = [sigma_one] * PARTS
    for step in range(DEGREE):
        for chain in range(PARTS):
            product(step, chain)
        for chain in range(PARTS):
            sigmas[chain] = finish(step, chain, sigmas[chain])

    own = last[:, :, lanes(core, tile)].reshape(half, tile)
    out_ref[:, lanes(core, half)] = own.T
    for chain in range(PARTS):
        wait(last_in.at[chain], last_recv.at[chain])
    out_ref[:, lanes(1 - core, half)] = last_in[...].reshape(half, tile).T

    wait(give, give_send)
    for chain in range(PARTS):
        wait(last_in.at[chain], last_send.at[chain])

    def close_near(slot, high_at):
        block = direct.at[slot, mid, core]
        wait(block, near_tiles_send.at[slot])
        wait(block, core_tiles_send.at[slot, 0])
        wait(block, core_tiles_send.at[slot, 1])

    each_slot(close_near)
    for m in range(line):

        @pl.when(from_ok[m])
        def _(m=m):
            for other in range(near):
                wait(mirror.at[m, core, other], core_far_send.at[m, other])
            for step in range(DEGREE):
                for chain in range(PARTS):
                    wait(part_out.at[step, chain, plane - 1 + m], back_send.at[step, chain, m])

        @pl.when(into_ok[m])
        def _(m=m):
            wait(mirror.at[m, core], far_tiles_send.at[m])
            for step in range(DEGREE):
                for chain in range(PARTS):
                    wait(low.at[step, chain, 0], line_send.at[step, chain, m])

    for step in range(DEGREE):
        for chain in range(PARTS):
            wait(low.at[step, chain, pl.ds(1, plane - 1)], low_send.at[step, chain])
            wait(part_out.at[step, chain, pl.ds(0, plane - 1)], part_send.at[step, chain])


def plane_scratch(tall, near, slots, tile, width):
    far = 4 * tall
    plane = 2 * near
    line = tall // 2
    half = width // 2
    cut = half // PARTS
    pair = 2 * tile
    bf16, f32 = jnp.bfloat16, jnp.float32
    memory = [
        ((slots + 1, tile, tile), bf16),
        ((far, near, tile, tile), bf16),
        ((1 + line, 2, 2, 2, near, tile, tile), bf16),
        ((line, 2, near, 4, tile, tile), bf16),
        ((plane * pair, (1 + line) * pair), bf16),
        (((1 + line) * pair, plane * pair), bf16),
        ((half, tile), f32),
        ((half, tile), f32),
        ((DEGREE, PARTS, plane + line, cut, pair), bf16),
        ((DEGREE, PARTS, plane - 1 + line, cut, pair), bf16),
        ((DEGREE, PARTS, plane - 1 + line, cut, pair), bf16),
        ((PARTS, cut, pair), f32),
        ((DEGREE, PARTS, cut, pair), f32),
        ((PARTS, cut, pair), f32),
        ((PARTS, cut, tile), f32),
    ]
    chains = (DEGREE, PARTS)
    semaphores = [
        (1 + line,), (line,), (1 + line, 2), (line, near),
        (1 + line,), (line, near), (1 + line, 2), (line, near),
        (), (), chains, (*chains, line), chains, (*chains, line),
        chains, (*chains, line), chains, (*chains, line), (PARTS,), (PARTS,),
    ]
    size = sum(math.prod(shape) * jnp.dtype(kind).itemsize for shape, kind in memory)
    shapes = [pltpu.VMEM(shape, kind) for shape, kind in memory]
    return size, shapes + [pltpu.SemaphoreType.DMA(shape) for shape in semaphores]


def wide_scratch(far, near, slots, tile, width):
    count = far * near
    cut = width // CHAINS
    return [
        pltpu.VMEM((slots + 1, tile, tile), jnp.bfloat16),
        pltpu.VMEM((count, tile, tile), jnp.bfloat16),
        pltpu.VMEM((count, tile, tile), jnp.bfloat16),
        pltpu.VMEM((near * tile, far * tile), jnp.bfloat16),
        pltpu.VMEM((tile, tile), jnp.bfloat16),
        pltpu.VMEM((DEGREE, CHAINS, far, tile, cut), jnp.bfloat16),
        pltpu.VMEM((DEGREE, CHAINS, near, tile, cut), jnp.float32),
        pltpu.VMEM((DEGREE, CHAINS, near, tile, cut), jnp.float32),
        pltpu.VMEM((CHAINS, tile, cut), jnp.float32),
        pltpu.VMEM((DEGREE, tile, width), jnp.float32),
        pltpu.SemaphoreType.DMA(()),
        pltpu.SemaphoreType.DMA((far,)),
        pltpu.SemaphoreType.DMA((DEGREE, CHAINS)),
        pltpu.SemaphoreType.DMA((DEGREE, CHAINS, far)),
        pltpu.SemaphoreType.DMA((DEGREE, CHAINS)),
        pltpu.SemaphoreType.DMA((DEGREE, CHAINS, near)),
    ]


def local(start_block, tiles, tile_rows, tile_cols, bounds):
    tall, width = start_block.shape
    tile = tiles.shape[-1]
    slots = tiles.shape[2]
    far = lax.axis_size("row")
    near = lax.axis_size("col")
    assert tall == tile and far % 4 == 0
    smem = pl.BlockSpec(memory_space=pltpu.SMEM)
    vmem = pl.BlockSpec(memory_space=pltpu.VMEM)
    body = functools.partial(wide_kernel, far, near, slots, tile, width)
    scratch = wide_scratch(far, near, slots, tile, width)
    if far % 8 == 0:
        size, shapes = plane_scratch(far // 4, near, slots, tile, width)
        if size <= ROOM:
            body = functools.partial(plane_kernel, far // 4, near, slots, tile, width)
            scratch = shapes
    return pl.pallas_call(
        body,
        out_shape=jax.ShapeDtypeStruct((tall, width), jnp.float32),
        in_specs=[smem, smem, smem, vmem, vmem],
        out_specs=vmem,
        scratch_shapes=scratch,
        compiler_params=pltpu.CompilerParams(
            collective_id=0, has_side_effects=True, vmem_limit_bytes=60 * 1024 * 1024
        ),
    )(
        tile_rows.reshape(slots),
        tile_cols.reshape(slots),
        bounds,
        start_block,
        tiles.reshape(slots, tile, tile),
    )


def solution(mesh):
    placed = (
        P(("row", "col"), None),
        P("row", "col", None, None, None),
        P("row", "col", None),
        P("row", "col", None),
        P(),
    )
    return jax.shard_map(
        local, mesh=mesh, in_specs=placed, out_specs=P(("row", "col"), None), check_vma=False
    )
```

```python
import functools
import math

import jax
import jax.numpy as jnp
from jax import lax
from jax.experimental import pallas as pl
from jax.experimental.pallas import tpu as pltpu
from jax.sharding import PartitionSpec as P

DEGREE = 4
CHAINS = 2
LAG = 0
PARTS = 4
ROOM = 48 * 1024 * 1024
MESH = pl.DeviceIdType.MESH


def wide_kernel(
    far, near, slots, tile, width,
    rows_ref, cols_ref, bounds_ref, start_ref, tiles_ref, out_ref,
    placed, owned, mirror, window, diagonal, low, partial, arrived, mine, state,
    tile_send, tile_recv, low_send, low_recv, part_send, part_recv,
):
    chips = far // 2
    tall = far // 4
    count = far * near
    cut = width // CHAINS
    row = lax.axis_index("row")
    col = lax.axis_index("col")
    me = row * near + col
    core = row % 2
    mid = row // 2 % 2
    high = row // 4

    def spot(high_at, mid_at, core_at):
        return core_at * chips + high_at * 2 + mid_at

    def row_of(high_at, mid_at, core_at):
        return (high_at * 2 + mid_at) * 2 + core_at

    own_spot = spot(high, mid, core)

    barrier = pltpu.get_barrier_semaphore()

    def greet(step, carry):
        other = (me + step) % count
        pl.semaphore_signal(
            barrier, inc=1, device_id=(other // near, other % near), device_id_type=MESH
        )
        return carry

    lax.fori_loop(1, count, greet, 0)

    line = (1, cut)
    lowest = jnp.full(line, bounds_ref[0], jnp.float32)
    lower = jnp.full(line, bounds_ref[1], jnp.float32)
    upper = jnp.full(line, bounds_ref[2], jnp.float32)
    half_width = (upper - lower) * 0.5
    center = (upper + lower) * 0.5
    sigma_one = half_width / (lowest - center)

    def columns(chain):
        return slice(chain * cut, (chain + 1) * cut)

    for chain in range(CHAINS):
        low[0, chain, own_spot] = start_ref[:, columns(chain)].astype(jnp.bfloat16)

    for slot in range(slots):
        placed[slot] = tiles_ref[slot]
    placed[slots] = jnp.zeros((tile, tile), jnp.bfloat16)
    places = []
    for slot in range(slots):
        glob_row = rows_ref[slot]
        glob_col = cols_ref[slot]
        place = (glob_col // near) * near + (glob_row - row * near)
        places.append(jnp.where(glob_row >= 0, place, -1))

    def put(position, carry):
        chosen = jnp.int32(slots)
        for slot in range(slots):
            chosen = jnp.where(places[slot] == position, slot, chosen)
        owned[position] = placed[chosen]
        return carry

    lax.fori_loop(0, count, put, 0)
    diagonal[...] = owned[me]
    mirror[me] = diagonal[...]
    owned[me] = jnp.zeros((tile, tile), jnp.bfloat16)

    pl.semaphore_wait(barrier, count - 1)

    flip = high >= tall // 2
    near_end = jnp.where(flip, tall - 1 - high, high)

    def along(position):
        return jnp.where(flip, tall - 1 - position, position)

    def ranked(index):
        return index + jnp.where(index >= near_end, 1, 0)

    def send_low(step, chain, place, target_row):
        pltpu.make_async_remote_copy(
            src_ref=low.at[step, chain, place],
            dst_ref=low.at[step, chain, place],
            send_sem=low_send.at[step, chain],
            recv_sem=low_recv.at[step, chain, place],
            device_id=(target_row, col),
            device_id_type=MESH,
        ).start()

    def await_low(step, chain, place):
        here = low.at[step, chain, place]
        pltpu.make_async_copy(here, here, low_recv.at[step, chain, place]).wait()

    def begin(step, chain):
        send_low(step, chain, own_spot, row_of(high, 1 - mid, core))
        for index in range(tall - 1):
            send_low(step, chain, own_spot, row_of(along(ranked(index)), mid, core))
        send_low(step, chain, own_spot, row_of(high, mid, 1 - core))

    def forward_line(step, chain):
        for index in range(tall - 1):
            place = spot(along(ranked(index)), mid, core)
            await_low(step, chain, place)
            send_low(step, chain, place, row_of(high, 1 - mid, core))
            send_low(step, chain, place, row_of(high, mid, 1 - core))

    def forward_mid(step, chain):
        for index in range(tall):
            source = high if index == 0 else along(ranked(index - 1))
            place = spot(source, 1 - mid, core)
            await_low(step, chain, place)
            send_low(step, chain, place, row_of(high, mid, 1 - core))

    def await_core(step, chain):
        for offset in range(tall):
            for mid_at in range(2):
                await_low(step, chain, spot((high + offset) % tall, mid_at, 1 - core))

    def send_tiles(high_at):
        inner = me % (4 * near)

        def send_tile(offset, carry):
            other = high_at * (4 * near) + (inner + offset) % (4 * near)
            pltpu.make_async_remote_copy(
                src_ref=owned.at[other],
                dst_ref=mirror.at[me],
                send_sem=tile_send,
                recv_sem=tile_recv.at[row],
                device_id=(other // near, other % near),
                device_id_type=MESH,
            ).start()
            return carry

        return send_tile

    def send_group(index):
        if index < 0:
            lax.fori_loop(1, 4 * near, send_tiles(high), 0)
        else:
            lax.fori_loop(0, 4 * near, send_tiles(along(ranked(index))), 0)

    def build(step, carry):
        source = (row + far - step) % far
        base = source * near
        group = mirror.at[pl.ds(base, near)]
        pltpu.make_async_copy(group, group, tile_recv.at[source]).wait()
        fill(source)
        return carry

    def fill(source):
        lanes = (source % 2) * chips + source // 2
        lanes = pl.ds(pl.multiple_of(lanes * tile, tile), tile)
        for near_at in range(near):
            index = source * near + near_at
            window[near_at * tile : (near_at + 1) * tile, lanes] = (
                owned[index] + mirror[index].T
            )

    def multiply(step, chain, near_at):
        total = jnp.zeros((tile, cut), jnp.float32)
        matrix = window[pl.ds(pl.multiple_of(near_at * tile, tile), tile), :]
        vectors = low[step, chain].reshape(far * tile, cut)
        return total + jnp.dot(matrix, vectors, preferred_element_type=jnp.float32)

    def product(step, chain):
        for offset in range(1, near):
            other = (col + offset) % near
            partial[step, chain, other] = multiply(step, chain, other)
            pltpu.make_async_remote_copy(
                src_ref=partial.at[step, chain, other],
                dst_ref=arrived.at[step, chain, col],
                send_sem=part_send.at[step, chain],
                recv_sem=part_recv.at[step, chain, col],
                device_id=(row, other),
                device_id_type=MESH,
            ).start()
        mine[chain] = multiply(step, chain, col) + jnp.dot(
            diagonal[...], low[step, chain, own_spot], preferred_element_type=jnp.float32
        )

    def finish(step, chain, sigma):
        total = mine[chain]
        for offset in range(1, near):
            other = (col + offset) % near
            here = arrived.at[step, chain, other]
            pltpu.make_async_copy(here, here, part_recv.at[step, chain, other]).wait()
            total = total + arrived[step, chain, other]
        where = columns(chain)
        current = start_ref[:, where] if step == 0 else state[step - 1, :, where]
        if step == 0:
            following = (total - center * current) * (sigma_one / half_width)
            sigma_next = sigma_one
        else:
            before = start_ref[:, where] if step == 1 else state[step - 2, :, where]
            sigma_next = 1.0 / (2.0 / sigma_one - sigma)
            following = (total - center * current) * (
                2.0 * sigma_next / half_width
            ) - (sigma * sigma_next) * before
        if step == DEGREE - 1:
            out_ref[:, where] = following
        else:
            low[step + 1, chain, own_spot] = following.astype(jnp.bfloat16)
            begin(step + 1, chain)
            state[step, :, where] = following
        return sigma_next

    for chain in range(CHAINS):
        begin(0, chain)
    groups = list(range(tall - 2, -2, -1))
    for index in groups:
        send_group(index)
    for chain in range(CHAINS):
        forward_line(0, chain)
    for chain in range(CHAINS):
        forward_mid(0, chain)

    if near > 1:
        group = mirror.at[pl.ds(row * near, near - 1)]
        pltpu.make_async_copy(group, group, tile_recv.at[row]).wait()
    fill(row)
    lax.fori_loop(1, far, build, 0)

    sigmas = [sigma_one] * CHAINS

    def phase(chain, index):
        step, part = index // 4, index % 4
        if part == 0:
            forward_line(step, chain)
        elif part == 1:
            forward_mid(step, chain)
        elif part == 2:
            await_core(step, chain)
            product(step, chain)
        else:
            sigmas[chain] = finish(step, chain, sigmas[chain])

    for index in range(2, 4 * DEGREE + LAG * (CHAINS - 1)):
        for chain in range(CHAINS):
            own_index = index - LAG * chain
            if 2 <= own_index < 4 * DEGREE:
                phase(chain, own_index)

    group = owned.at[pl.ds(0, count - 1)]
    pltpu.make_async_copy(group, group, tile_send).wait()
    for step in range(DEGREE):
        for chain in range(CHAINS):
            group = low.at[step, chain, pl.ds(0, far - 1)]
            pltpu.make_async_copy(group, group, low_send.at[step, chain]).wait()
            if near > 1:
                group = partial.at[step, chain, pl.ds(0, near - 1)]
                pltpu.make_async_copy(group, group, part_send.at[step, chain]).wait()


def plane_kernel(
    tall, near, slots, tile, width,
    rows_ref, cols_ref, bounds_ref, start_ref, tiles_ref, out_ref,
    placed, owned, direct, mirror, forward, backward, give, take, low,
    part_out, part_in, mine, state, last, last_in, start, row_of, col_of, limits, load,
    near_tiles_send, far_tiles_send, core_tiles_send, core_far_send,
    near_tiles_recv, far_tiles_recv, core_tiles_recv, core_far_recv,
    give_send, give_recv, low_send, line_send, low_recv, line_recv,
    part_send, back_send, part_recv, back_recv, last_send, last_recv,
):
    far = 4 * tall
    count = far * near
    plane = 2 * near
    line = tall // 2
    half = width // 2
    cut = half // PARTS
    pair = 2 * tile
    row = lax.axis_index("row")
    col = lax.axis_index("col")
    core = row % 2
    mid = row // 2 % 2
    high = row // 4
    here = mid * near + col

    def device(high_at, mid_at, core_at, col_at):
        return ((high_at * 2 + mid_at) * 2 + core_at, col_at)

    def beside(offset):
        other = (here + offset) % plane
        return device(high, other // near, core, other % near)

    partner = device(high, mid, 1 - core, col)

    from_ok = [high != 2 * m for m in range(line)]
    from_at = [
        jnp.where(high < 2 * m, high + tall - 2 * m, high - 2 * m - 1) for m in range(line)
    ]
    into_ok = [high != tall - 1 - 2 * m for m in range(line)]
    into_at = [
        jnp.where(high >= tall - 2 * m, high - tall + 2 * m, high + 2 * m + 1)
        for m in range(line)
    ]

    def copy(src, dst, send, recv, to):
        pltpu.make_async_remote_copy(
            src_ref=src, dst_ref=dst, send_sem=send, recv_sem=recv,
            device_id=to, device_id_type=MESH,
        ).start()

    def wait(ref, sem):
        pltpu.make_async_copy(ref, ref, sem).wait()

    barrier = pltpu.get_barrier_semaphore()

    def greet(step, carry):
        other = (row // 2 * near + col + step) % (far // 2 * near)
        pl.semaphore_signal(
            barrier, inc=1, device_id=(other // near * 2 + core, other % near),
            device_id_type=MESH,
        )
        return carry

    lax.fori_loop(1, far // 2 * near, greet, 0)
    pl.semaphore_signal(barrier, inc=1, device_id=partner, device_id_type=MESH)

    loads = [
        pltpu.make_async_copy(src, dst, load.at[index])
        for index, (src, dst) in enumerate(
            [
                (rows_ref, row_of),
                (cols_ref, col_of),
                (bounds_ref, limits),
                (start_ref, start),
                (tiles_ref, placed.at[pl.ds(0, slots)]),
            ]
        )
    ]
    for item in loads:
        item.start()
    placed[slots] = jnp.zeros((tile, tile), jnp.bfloat16)
    for item in loads[:4]:
        item.wait()

    span = (1, pair)
    lowest = jnp.full(span, limits[0], jnp.float32)
    lower = jnp.full(span, limits[1], jnp.float32)
    upper = jnp.full(span, limits[2], jnp.float32)
    half_width = (upper - lower) * 0.5
    center = (upper + lower) * 0.5
    sigma_one = half_width / (lowest - center)

    def lanes(at, size):
        return pl.ds(pl.multiple_of(at * size, size), size)

    give[...] = start[:, lanes(1 - core, half)].T
    kept = start[:, lanes(core, half)].T
    for chain in range(PARTS):
        state[0, chain, :, lanes(core, tile)] = kept[chain * cut : (chain + 1) * cut]

    places = []
    for slot in range(slots):
        glob_row = row_of[slot]
        glob_col = col_of[slot]
        place = (glob_col // near) * near + (glob_row - row * near)
        places.append(jnp.where(glob_row >= 0, place, -1))

    def put(position, carry):
        chosen = jnp.int32(slots)
        for slot in range(slots):
            chosen = jnp.where(places[slot] == position, slot, chosen)
        owned[position // near, position % near] = placed[chosen]
        return carry

    loads[4].wait()
    lax.fori_loop(0, count, put, 0)

    def owned_at(high_at, mid_at):
        return pl.ds((high_at * 2 + mid_at) * 2, 2)

    direct[0, mid, core] = owned[owned_at(high, mid)]
    for m in range(line):

        @pl.when(from_ok[m])
        def _(m=m):
            direct[1 + m, mid, core] = owned[owned_at(from_at[m], mid)]

        @pl.when(jnp.logical_not(from_ok[m]))
        def _(m=m):
            forward[:, (1 + m) * pair : (2 + m) * pair] = jnp.zeros(
                (plane * pair, pair), jnp.bfloat16
            )
            backward[(1 + m) * pair : (2 + m) * pair, :] = jnp.zeros(
                (pair, plane * pair), jnp.bfloat16
            )
            for step in range(DEGREE):
                for chain in range(PARTS):
                    low[step, chain, plane + m] = jnp.zeros((cut, pair), jnp.bfloat16)

        @pl.when(jnp.logical_not(into_ok[m]))
        def _(m=m):
            for step in range(DEGREE):
                for chain in range(PARTS):
                    part_in[step, chain, plane - 1 + m] = jnp.zeros((cut, pair), jnp.bfloat16)

    pl.semaphore_wait(barrier, far // 2 * near)

    copy(give, take, give_send, give_recv, partner)
    for m in reversed(range(line)):

        @pl.when(into_ok[m])
        def _(m=m):
            for offset in range(near):
                other = (col + offset) % near
                copy(
                    owned.at[pl.ds(into_at[m] * 4, 4), other], mirror.at[m, core, col],
                    far_tiles_send.at[m], far_tiles_recv.at[m, col],
                    device(into_at[m], mid, core, other),
                )

    def each_slot(act):
        act(0, high)
        for m in reversed(range(line)):

            @pl.when(from_ok[m])
            def _(m=m):
                act(1 + m, from_at[m])

    def send_near(slot, high_at):
        copy(
            owned.at[owned_at(high_at, 1 - mid)], direct.at[slot, mid, core],
            near_tiles_send.at[slot], near_tiles_recv.at[slot],
            device(high, 1 - mid, core, col),
        )
        copy(
            owned.at[owned_at(high_at, mid)], direct.at[slot, mid, core],
            core_tiles_send.at[slot, 0], core_tiles_recv.at[slot, 0], partner,
        )

    each_slot(send_near)

    def begin(step, chain):
        own = low.at[step, chain, 0]
        for m in reversed(range(line)):

            @pl.when(into_ok[m])
            def _(m=m):
                copy(
                    own, low.at[step, chain, plane + m],
                    line_send.at[step, chain, m], line_recv.at[step, chain, m],
                    device(into_at[m], mid, core, col),
                )

        for offset in range(1, plane):
            copy(
                own, low.at[step, chain, plane - offset],
                low_send.at[step, chain], low_recv.at[step, chain], beside(offset),
            )

    wait(take, give_recv)
    for chain in range(PARTS):
        state[0, chain, :, lanes(1 - core, tile)] = take[chain * cut : (chain + 1) * cut, :]
        low[0, chain, 0] = state[0, chain].astype(jnp.bfloat16)
        begin(0, chain)

    def pass_near(slot, high_at):
        block = direct.at[slot, 1 - mid, core]
        wait(block, near_tiles_recv.at[slot])
        copy(
            block, block, core_tiles_send.at[slot, 1], core_tiles_recv.at[slot, 1], partner
        )

    def pass_far(m, offset):
        other = (col + offset) % near
        block = mirror.at[m, core, other]
        wait(block, far_tiles_recv.at[m, other])
        copy(block, block, core_far_send.at[m, other], core_far_recv.at[m, other], partner)

    def spots(slot, mid_at, core_at, other_core, col_at):
        offset = (mid_at * near + col_at + plane - here) % plane
        inner = pl.ds(pl.multiple_of((offset * 2 + core_at) * tile, tile), tile)
        outer = pl.ds(pl.multiple_of((slot * 2 + other_core) * tile, tile), tile)
        return inner, outer

    def fill_near(slot, mid_at, core_at):
        def fill(index, carry):
            other_core, col_at = index // near, index % near
            inner, outer = spots(slot, mid_at, core_at, other_core, col_at)
            block = direct[slot, mid_at, core_at, other_core, col_at]
            forward[inner, outer] = block
            backward[outer, inner] = block.T
            return carry

        lax.fori_loop(0, 2 * near, fill, 0, unroll=2)

    def fill_slot(slot, high_at):
        fill_near(slot, mid, core)
        fill_near(slot, 1 - mid, core)
        wait(direct.at[slot, mid, 1 - core], core_tiles_recv.at[slot, 0])
        fill_near(slot, mid, 1 - core)
        wait(direct.at[slot, 1 - mid, 1 - core], core_tiles_recv.at[slot, 1])
        fill_near(slot, 1 - mid, 1 - core)

    def fill_far(m, offset, other_core):
        col_at = (col + offset) % near

        def fill(index, carry):
            inner, outer = spots(1 + m, index // 2, index % 2, other_core, col_at)
            block = mirror[m, other_core, col_at, index]
            forward[inner, outer] += block.T
            backward[outer, inner] += block
            return carry

        lax.fori_loop(0, 4, fill, 0, unroll=2)

    def fill_pair(m, offset):
        fill_far(m, offset, core)
        other = (col + offset) % near
        wait(mirror.at[m, 1 - core, other], core_far_recv.at[m, other])
        fill_far(m, offset, 1 - core)

    def when_from(m, act):
        @pl.when(from_ok[m])
        def _():
            act()

    pass_near(0, high)
    order = list(reversed(range(line)))
    for place, m in enumerate(order):
        for offset in range(near):
            when_from(m, lambda m=m, offset=offset: pass_far(m, offset))
            if offset == 0:
                when_from(m, lambda m=m: pass_near(1 + m, from_at[m]))
                if place == 0:
                    fill_slot(0, high)
        if place + 1 < line:
            when_from(m, lambda m=m: fill_slot(1 + m, from_at[m]))
            for offset in range(near):
                when_from(m, lambda m=m, offset=offset: fill_pair(m, offset))
        else:
            when_from(m, lambda m=m: fill_slot(1 + m, from_at[m]))
    for offset in range(near):
        when_from(order[-1], lambda offset=offset: fill_pair(order[-1], offset))

    def product(step, chain):
        wait(low.at[step, chain, pl.ds(1, plane - 1)], low_recv.at[step, chain])
        total = jnp.zeros((cut, (1 + line) * pair), jnp.float32)
        for offset in range(plane):
            total = total + jnp.dot(
                low[step, chain, offset], forward[offset * pair : (offset + 1) * pair, :],
                preferred_element_type=jnp.float32,
            )
        kept = total[:, :pair]
        for m in range(line):
            at = plane - 1 + m
            part_out[step, chain, at] = total[:, (1 + m) * pair : (2 + m) * pair].astype(
                jnp.bfloat16
            )
        for m in reversed(range(line)):

            @pl.when(from_ok[m])
            def _(m=m):
                at = plane - 1 + m
                copy(
                    part_out.at[step, chain, at], part_in.at[step, chain, at],
                    back_send.at[step, chain, m], back_recv.at[step, chain, m],
                    device(from_at[m], mid, core, col),
                )

        for m in range(line):

            @pl.when(from_ok[m])
            def _(m=m):
                wait(low.at[step, chain, plane + m], line_recv.at[step, chain, m])

        total = jnp.dot(
            low[step, chain, 0], backward[:pair, :], preferred_element_type=jnp.float32
        )
        for m in range(line):
            total = total + jnp.dot(
                low[step, chain, plane + m], backward[(1 + m) * pair : (2 + m) * pair, :],
                preferred_element_type=jnp.float32,
            )
        mine[chain] = kept + total[:, :pair]
        for offset in range(1, plane):
            part_out[step, chain, offset - 1] = total[
                :, offset * pair : (offset + 1) * pair
            ].astype(jnp.bfloat16)
            copy(
                part_out.at[step, chain, offset - 1],
                part_in.at[step, chain, plane - offset - 1],
                part_send.at[step, chain], part_recv.at[step, chain], beside(offset),
            )

    def finish(step, chain, sigma):
        wait(part_in.at[step, chain, pl.ds(0, plane - 1)], part_recv.at[step, chain])
        for m in range(line):

            @pl.when(into_ok[m])
            def _(m=m):
                wait(part_in.at[step, chain, plane - 1 + m], back_recv.at[step, chain, m])

        total = mine[chain]
        for at in range(plane - 1 + line):
            total = total + part_in[step, chain, at].astype(jnp.float32)
        current = state[step, chain]
        if step == 0:
            sigma_next = sigma_one
            following = (total - center * current) * (sigma_one / half_width)
        else:
            sigma_next = 1.0 / (2.0 / sigma_one - sigma)
            following = (total - center * current) * (
                2.0 * sigma_next / half_width
            ) - (sigma * sigma_next) * state[step - 1, chain]
        if step == DEGREE - 1:
            last[chain] = following
            copy(
                last.at[chain, :, lanes(1 - core, tile)], last_in.at[chain],
                last_send.at[chain], last_recv.at[chain], partner,
            )
        else:
            low[step + 1, chain, 0] = following.astype(jnp.bfloat16)
            begin(step + 1, chain)
            state[step + 1, chain] = following
        return sigma_next

    sigmas = [sigma_one] * PARTS
    for step in range(DEGREE):
        for chain in range(PARTS):
            product(step, chain)
        for chain in range(PARTS):
            sigmas[chain] = finish(step, chain, sigmas[chain])

    own = last[:, :, lanes(core, tile)].reshape(half, tile)
    out_ref[:, lanes(core, half)] = own.T
    for chain in range(PARTS):
        wait(last_in.at[chain], last_recv.at[chain])
    out_ref[:, lanes(1 - core, half)] = last_in[...].reshape(half, tile).T

    wait(give, give_send)
    for chain in range(PARTS):
        wait(last_in.at[chain], last_send.at[chain])

    def close_near(slot, high_at):
        block = direct.at[slot, mid, core]
        wait(block, near_tiles_send.at[slot])
        wait(block, core_tiles_send.at[slot, 0])
        wait(block, core_tiles_send.at[slot, 1])

    each_slot(close_near)
    for m in range(line):

        @pl.when(from_ok[m])
        def _(m=m):
            for other in range(near):
                wait(mirror.at[m, core, other], core_far_send.at[m, other])
            for step in range(DEGREE):
                for chain in range(PARTS):
                    wait(part_out.at[step, chain, plane - 1 + m], back_send.at[step, chain, m])

        @pl.when(into_ok[m])
        def _(m=m):
            wait(mirror.at[m, core], far_tiles_send.at[m])
            for step in range(DEGREE):
                for chain in range(PARTS):
                    wait(low.at[step, chain, 0], line_send.at[step, chain, m])

    for step in range(DEGREE):
        for chain in range(PARTS):
            wait(low.at[step, chain, pl.ds(1, plane - 1)], low_send.at[step, chain])
            wait(part_out.at[step, chain, pl.ds(0, plane - 1)], part_send.at[step, chain])


def plane_scratch(tall, near, slots, tile, width):
    far = 4 * tall
    plane = 2 * near
    line = tall // 2
    half = width // 2
    cut = half // PARTS
    pair = 2 * tile
    bf16, f32 = jnp.bfloat16, jnp.float32
    memory = [
        ((slots + 1, tile, tile), bf16),
        ((far, near, tile, tile), bf16),
        ((1 + line, 2, 2, 2, near, tile, tile), bf16),
        ((line, 2, near, 4, tile, tile), bf16),
        ((plane * pair, (1 + line) * pair), bf16),
        (((1 + line) * pair, plane * pair), bf16),
        ((half, tile), f32),
        ((half, tile), f32),
        ((DEGREE, PARTS, plane + line, cut, pair), bf16),
        ((DEGREE, PARTS, plane - 1 + line, cut, pair), bf16),
        ((DEGREE, PARTS, plane - 1 + line, cut, pair), bf16),
        ((PARTS, cut, pair), f32),
        ((DEGREE, PARTS, cut, pair), f32),
        ((PARTS, cut, pair), f32),
        ((PARTS, cut, tile), f32),
        ((tile, width), f32),
    ]
    chains = (DEGREE, PARTS)
    semaphores = [
        (1 + line,), (line,), (1 + line, 2), (line, near),
        (1 + line,), (line, near), (1 + line, 2), (line, near),
        (), (), chains, (*chains, line), chains, (*chains, line),
        chains, (*chains, line), chains, (*chains, line), (PARTS,), (PARTS,),
    ]
    size = sum(math.prod(shape) * jnp.dtype(kind).itemsize for shape, kind in memory)
    shapes = [pltpu.VMEM(shape, kind) for shape, kind in memory]
    shapes += [
        pltpu.SMEM((slots,), jnp.int32),
        pltpu.SMEM((slots,), jnp.int32),
        pltpu.SMEM((3,), jnp.float32),
        pltpu.SemaphoreType.DMA((5,)),
    ]
    return size, shapes + [pltpu.SemaphoreType.DMA(shape) for shape in semaphores]


def wide_scratch(far, near, slots, tile, width):
    count = far * near
    cut = width // CHAINS
    return [
        pltpu.VMEM((slots + 1, tile, tile), jnp.bfloat16),
        pltpu.VMEM((count, tile, tile), jnp.bfloat16),
        pltpu.VMEM((count, tile, tile), jnp.bfloat16),
        pltpu.VMEM((near * tile, far * tile), jnp.bfloat16),
        pltpu.VMEM((tile, tile), jnp.bfloat16),
        pltpu.VMEM((DEGREE, CHAINS, far, tile, cut), jnp.bfloat16),
        pltpu.VMEM((DEGREE, CHAINS, near, tile, cut), jnp.float32),
        pltpu.VMEM((DEGREE, CHAINS, near, tile, cut), jnp.float32),
        pltpu.VMEM((CHAINS, tile, cut), jnp.float32),
        pltpu.VMEM((DEGREE, tile, width), jnp.float32),
        pltpu.SemaphoreType.DMA(()),
        pltpu.SemaphoreType.DMA((far,)),
        pltpu.SemaphoreType.DMA((DEGREE, CHAINS)),
        pltpu.SemaphoreType.DMA((DEGREE, CHAINS, far)),
        pltpu.SemaphoreType.DMA((DEGREE, CHAINS)),
        pltpu.SemaphoreType.DMA((DEGREE, CHAINS, near)),
    ]


def local(start_block, tiles, tile_rows, tile_cols, bounds):
    tall, width = start_block.shape
    tile = tiles.shape[-1]
    slots = tiles.shape[2]
    far = lax.axis_size("row")
    near = lax.axis_size("col")
    assert tall == tile and far % 4 == 0
    smem = pl.BlockSpec(memory_space=pltpu.SMEM)
    vmem = pl.BlockSpec(memory_space=pltpu.VMEM)
    body = functools.partial(wide_kernel, far, near, slots, tile, width)
    scratch = wide_scratch(far, near, slots, tile, width)
    in_specs = [smem, smem, smem, vmem, vmem]
    if far % 8 == 0:
        size, shapes = plane_scratch(far // 4, near, slots, tile, width)
        if size <= ROOM:
            body = functools.partial(plane_kernel, far // 4, near, slots, tile, width)
            scratch = shapes
            in_specs = [pl.BlockSpec(memory_space=pl.ANY)] * 5
    return pl.pallas_call(
        body,
        out_shape=jax.ShapeDtypeStruct((tall, width), jnp.float32),
        in_specs=in_specs,
        out_specs=vmem,
        scratch_shapes=scratch,
        compiler_params=pltpu.CompilerParams(
            collective_id=0, has_side_effects=True, vmem_limit_bytes=60 * 1024 * 1024
        ),
    )(
        tile_rows.reshape(slots),
        tile_cols.reshape(slots),
        bounds,
        start_block,
        tiles.reshape(slots, tile, tile),
    )


def solution(mesh):
    placed = (
        P(("row", "col"), None),
        P("row", "col", None, None, None),
        P("row", "col", None),
        P("row", "col", None),
        P(),
    )
    return jax.shard_map(
        local, mesh=mesh, in_specs=placed, out_specs=P(("row", "col"), None), check_vma=False
    )
```

```python
import functools
import math

import jax
import jax.numpy as jnp
from jax import lax
from jax.experimental import pallas as pl
from jax.experimental.pallas import tpu as pltpu
from jax.sharding import PartitionSpec as P

DEGREE = 4
CHAINS = 2
LAG = 0
PARTS = 4
ROOM = 48 * 1024 * 1024
MESH = pl.DeviceIdType.MESH


def wide_kernel(
    far, near, slots, tile, width,
    rows_ref, cols_ref, bounds_ref, start_ref, tiles_ref, out_ref,
    placed, owned, mirror, window, diagonal, low, partial, arrived, mine, state,
    tile_send, tile_recv, low_send, low_recv, part_send, part_recv,
):
    chips = far // 2
    tall = far // 4
    count = far * near
    cut = width // CHAINS
    row = lax.axis_index("row")
    col = lax.axis_index("col")
    me = row * near + col
    core = row % 2
    mid = row // 2 % 2
    high = row // 4

    def spot(high_at, mid_at, core_at):
        return core_at * chips + high_at * 2 + mid_at

    def row_of(high_at, mid_at, core_at):
        return (high_at * 2 + mid_at) * 2 + core_at

    own_spot = spot(high, mid, core)

    barrier = pltpu.get_barrier_semaphore()

    def greet(step, carry):
        other = (me + step) % count
        pl.semaphore_signal(
            barrier, inc=1, device_id=(other // near, other % near), device_id_type=MESH
        )
        return carry

    lax.fori_loop(1, count, greet, 0)

    line = (1, cut)
    lowest = jnp.full(line, bounds_ref[0], jnp.float32)
    lower = jnp.full(line, bounds_ref[1], jnp.float32)
    upper = jnp.full(line, bounds_ref[2], jnp.float32)
    half_width = (upper - lower) * 0.5
    center = (upper + lower) * 0.5
    sigma_one = half_width / (lowest - center)

    def columns(chain):
        return slice(chain * cut, (chain + 1) * cut)

    for chain in range(CHAINS):
        low[0, chain, own_spot] = start_ref[:, columns(chain)].astype(jnp.bfloat16)

    for slot in range(slots):
        placed[slot] = tiles_ref[slot]
    placed[slots] = jnp.zeros((tile, tile), jnp.bfloat16)
    places = []
    for slot in range(slots):
        glob_row = rows_ref[slot]
        glob_col = cols_ref[slot]
        place = (glob_col // near) * near + (glob_row - row * near)
        places.append(jnp.where(glob_row >= 0, place, -1))

    def put(position, carry):
        chosen = jnp.int32(slots)
        for slot in range(slots):
            chosen = jnp.where(places[slot] == position, slot, chosen)
        owned[position] = placed[chosen]
        return carry

    lax.fori_loop(0, count, put, 0)
    diagonal[...] = owned[me]
    mirror[me] = diagonal[...]
    owned[me] = jnp.zeros((tile, tile), jnp.bfloat16)

    pl.semaphore_wait(barrier, count - 1)

    flip = high >= tall // 2
    near_end = jnp.where(flip, tall - 1 - high, high)

    def along(position):
        return jnp.where(flip, tall - 1 - position, position)

    def ranked(index):
        return index + jnp.where(index >= near_end, 1, 0)

    def send_low(step, chain, place, target_row):
        pltpu.make_async_remote_copy(
            src_ref=low.at[step, chain, place],
            dst_ref=low.at[step, chain, place],
            send_sem=low_send.at[step, chain],
            recv_sem=low_recv.at[step, chain, place],
            device_id=(target_row, col),
            device_id_type=MESH,
        ).start()

    def await_low(step, chain, place):
        here = low.at[step, chain, place]
        pltpu.make_async_copy(here, here, low_recv.at[step, chain, place]).wait()

    def begin(step, chain):
        send_low(step, chain, own_spot, row_of(high, 1 - mid, core))
        for index in range(tall - 1):
            send_low(step, chain, own_spot, row_of(along(ranked(index)), mid, core))
        send_low(step, chain, own_spot, row_of(high, mid, 1 - core))

    def forward_line(step, chain):
        for index in range(tall - 1):
            place = spot(along(ranked(index)), mid, core)
            await_low(step, chain, place)
            send_low(step, chain, place, row_of(high, 1 - mid, core))
            send_low(step, chain, place, row_of(high, mid, 1 - core))

    def forward_mid(step, chain):
        for index in range(tall):
            source = high if index == 0 else along(ranked(index - 1))
            place = spot(source, 1 - mid, core)
            await_low(step, chain, place)
            send_low(step, chain, place, row_of(high, mid, 1 - core))

    def await_core(step, chain):
        for offset in range(tall):
            for mid_at in range(2):
                await_low(step, chain, spot((high + offset) % tall, mid_at, 1 - core))

    def send_tiles(high_at):
        inner = me % (4 * near)

        def send_tile(offset, carry):
            other = high_at * (4 * near) + (inner + offset) % (4 * near)
            pltpu.make_async_remote_copy(
                src_ref=owned.at[other],
                dst_ref=mirror.at[me],
                send_sem=tile_send,
                recv_sem=tile_recv.at[row],
                device_id=(other // near, other % near),
                device_id_type=MESH,
            ).start()
            return carry

        return send_tile

    def send_group(index):
        if index < 0:
            lax.fori_loop(1, 4 * near, send_tiles(high), 0)
        else:
            lax.fori_loop(0, 4 * near, send_tiles(along(ranked(index))), 0)

    def build(step, carry):
        source = (row + far - step) % far
        base = source * near
        group = mirror.at[pl.ds(base, near)]
        pltpu.make_async_copy(group, group, tile_recv.at[source]).wait()
        fill(source)
        return carry

    def fill(source):
        lanes = (source % 2) * chips + source // 2
        lanes = pl.ds(pl.multiple_of(lanes * tile, tile), tile)
        for near_at in range(near):
            index = source * near + near_at
            window[near_at * tile : (near_at + 1) * tile, lanes] = (
                owned[index] + mirror[index].T
            )

    def multiply(step, chain, near_at):
        total = jnp.zeros((tile, cut), jnp.float32)
        matrix = window[pl.ds(pl.multiple_of(near_at * tile, tile), tile), :]
        vectors = low[step, chain].reshape(far * tile, cut)
        return total + jnp.dot(matrix, vectors, preferred_element_type=jnp.float32)

    def product(step, chain):
        for offset in range(1, near):
            other = (col + offset) % near
            partial[step, chain, other] = multiply(step, chain, other)
            pltpu.make_async_remote_copy(
                src_ref=partial.at[step, chain, other],
                dst_ref=arrived.at[step, chain, col],
                send_sem=part_send.at[step, chain],
                recv_sem=part_recv.at[step, chain, col],
                device_id=(row, other),
                device_id_type=MESH,
            ).start()
        mine[chain] = multiply(step, chain, col) + jnp.dot(
            diagonal[...], low[step, chain, own_spot], preferred_element_type=jnp.float32
        )

    def finish(step, chain, sigma):
        total = mine[chain]
        for offset in range(1, near):
            other = (col + offset) % near
            here = arrived.at[step, chain, other]
            pltpu.make_async_copy(here, here, part_recv.at[step, chain, other]).wait()
            total = total + arrived[step, chain, other]
        where = columns(chain)
        current = start_ref[:, where] if step == 0 else state[step - 1, :, where]
        if step == 0:
            following = (total - center * current) * (sigma_one / half_width)
            sigma_next = sigma_one
        else:
            before = start_ref[:, where] if step == 1 else state[step - 2, :, where]
            sigma_next = 1.0 / (2.0 / sigma_one - sigma)
            following = (total - center * current) * (
                2.0 * sigma_next / half_width
            ) - (sigma * sigma_next) * before
        if step == DEGREE - 1:
            out_ref[:, where] = following
        else:
            low[step + 1, chain, own_spot] = following.astype(jnp.bfloat16)
            begin(step + 1, chain)
            state[step, :, where] = following
        return sigma_next

    for chain in range(CHAINS):
        begin(0, chain)
    groups = list(range(tall - 2, -2, -1))
    for index in groups:
        send_group(index)
    for chain in range(CHAINS):
        forward_line(0, chain)
    for chain in range(CHAINS):
        forward_mid(0, chain)

    if near > 1:
        group = mirror.at[pl.ds(row * near, near - 1)]
        pltpu.make_async_copy(group, group, tile_recv.at[row]).wait()
    fill(row)
    lax.fori_loop(1, far, build, 0)

    sigmas = [sigma_one] * CHAINS

    def phase(chain, index):
        step, part = index // 4, index % 4
        if part == 0:
            forward_line(step, chain)
        elif part == 1:
            forward_mid(step, chain)
        elif part == 2:
            await_core(step, chain)
            product(step, chain)
        else:
            sigmas[chain] = finish(step, chain, sigmas[chain])

    for index in range(2, 4 * DEGREE + LAG * (CHAINS - 1)):
        for chain in range(CHAINS):
            own_index = index - LAG * chain
            if 2 <= own_index < 4 * DEGREE:
                phase(chain, own_index)

    group = owned.at[pl.ds(0, count - 1)]
    pltpu.make_async_copy(group, group, tile_send).wait()
    for step in range(DEGREE):
        for chain in range(CHAINS):
            group = low.at[step, chain, pl.ds(0, far - 1)]
            pltpu.make_async_copy(group, group, low_send.at[step, chain]).wait()
            if near > 1:
                group = partial.at[step, chain, pl.ds(0, near - 1)]
                pltpu.make_async_copy(group, group, part_send.at[step, chain]).wait()


def plane_kernel(
    tall, near, slots, tile, width,
    rows_ref, cols_ref, bounds_ref, start_ref, tiles_ref, out_ref,
    placed, owned, direct, mirror, forward, backward, give, take, low,
    part_out, part_in, mine, state, last, last_in, start, row_of, col_of, limits, load,
    near_tiles_send, far_tiles_send, core_tiles_send, core_far_send,
    near_tiles_recv, far_tiles_recv, core_tiles_recv, core_far_recv,
    give_send, give_recv, low_send, line_send, low_recv, line_recv,
    part_send, back_send, part_recv, back_recv, last_send, last_recv,
):
    far = 4 * tall
    count = far * near
    plane = 2 * near
    line = tall // 2
    half = width // 2
    cut = half // PARTS
    pair = 2 * tile
    row = lax.axis_index("row")
    col = lax.axis_index("col")
    core = row % 2
    mid = row // 2 % 2
    high = row // 4
    here = mid * near + col

    def device(high_at, mid_at, core_at, col_at):
        return ((high_at * 2 + mid_at) * 2 + core_at, col_at)

    def beside(offset):
        other = (here + offset) % plane
        return device(high, other // near, core, other % near)

    partner = device(high, mid, 1 - core, col)

    from_ok = [high != 2 * m for m in range(line)]
    from_at = [
        jnp.where(high < 2 * m, high + tall - 2 * m, high - 2 * m - 1) for m in range(line)
    ]
    into_ok = [high != tall - 1 - 2 * m for m in range(line)]
    into_at = [
        jnp.where(high >= tall - 2 * m, high - tall + 2 * m, high + 2 * m + 1)
        for m in range(line)
    ]

    def copy(src, dst, send, recv, to):
        pltpu.make_async_remote_copy(
            src_ref=src, dst_ref=dst, send_sem=send, recv_sem=recv,
            device_id=to, device_id_type=MESH,
        ).start()

    def wait(ref, sem):
        pltpu.make_async_copy(ref, ref, sem).wait()

    barrier = pltpu.get_barrier_semaphore()

    def greet(step, carry):
        other = (row // 2 * near + col + step) % (far // 2 * near)
        pl.semaphore_signal(
            barrier, inc=1, device_id=(other // near * 2 + core, other % near),
            device_id_type=MESH,
        )
        return carry

    lax.fori_loop(1, far // 2 * near, greet, 0)
    pl.semaphore_signal(barrier, inc=1, device_id=partner, device_id_type=MESH)

    loads = [
        pltpu.make_async_copy(src, dst, load.at[index])
        for index, (src, dst) in enumerate(
            [
                (rows_ref, row_of),
                (cols_ref, col_of),
                (bounds_ref, limits),
                (start_ref, start),
                (tiles_ref, placed.at[pl.ds(0, slots)]),
            ]
        )
    ]
    for item in loads:
        item.start()
    placed[slots] = jnp.zeros((tile, tile), jnp.bfloat16)
    for item in loads[:4]:
        item.wait()

    span = (1, pair)
    lowest = jnp.full(span, limits[0], jnp.float32)
    lower = jnp.full(span, limits[1], jnp.float32)
    upper = jnp.full(span, limits[2], jnp.float32)
    half_width = (upper - lower) * 0.5
    center = (upper + lower) * 0.5
    sigma_one = half_width / (lowest - center)

    def lanes(at, size):
        return pl.ds(pl.multiple_of(at * size, size), size)

    give[...] = start[:, lanes(1 - core, half)].T
    kept = start[:, lanes(core, half)].T
    for chain in range(PARTS):
        state[0, chain, :, lanes(core, tile)] = kept[chain * cut : (chain + 1) * cut]

    places = []
    for slot in range(slots):
        glob_row = row_of[slot]
        glob_col = col_of[slot]
        place = (glob_col // near) * near + (glob_row - row * near)
        places.append(jnp.where(glob_row >= 0, place, -1))

    def put(position, carry):
        chosen = jnp.int32(slots)
        for slot in range(slots):
            chosen = jnp.where(places[slot] == position, slot, chosen)
        owned[position // near, position % near] = placed[chosen]
        return carry

    loads[4].wait()
    lax.fori_loop(0, count, put, 0)

    def owned_at(high_at, mid_at):
        return pl.ds((high_at * 2 + mid_at) * 2, 2)

    direct[0, mid, core] = owned[owned_at(high, mid)]
    for m in range(line):

        @pl.when(from_ok[m])
        def _(m=m):
            direct[1 + m, mid, core] = owned[owned_at(from_at[m], mid)]

        @pl.when(jnp.logical_not(from_ok[m]))
        def _(m=m):
            forward[:, (1 + m) * pair : (2 + m) * pair] = jnp.zeros(
                (plane * pair, pair), jnp.bfloat16
            )
            backward[(1 + m) * pair : (2 + m) * pair, :] = jnp.zeros(
                (pair, plane * pair), jnp.bfloat16
            )
            for step in range(DEGREE):
                for chain in range(PARTS):
                    low[step, chain, plane + m] = jnp.zeros((cut, pair), jnp.bfloat16)

        @pl.when(jnp.logical_not(into_ok[m]))
        def _(m=m):
            for step in range(DEGREE):
                for chain in range(PARTS):
                    part_in[step, chain, plane - 1 + m] = jnp.zeros((cut, pair), jnp.bfloat16)

    pl.semaphore_wait(barrier, far // 2 * near)

    copy(give, take, give_send, give_recv, partner)
    for m in reversed(range(line)):

        @pl.when(into_ok[m])
        def _(m=m):
            for offset in range(near):
                other = (col + offset) % near
                copy(
                    owned.at[pl.ds(into_at[m] * 4, 4), other], mirror.at[m, core, col],
                    far_tiles_send.at[m], far_tiles_recv.at[m, col],
                    device(into_at[m], mid, core, other),
                )

    def each_slot(act):
        act(0, high)
        for m in reversed(range(line)):

            @pl.when(from_ok[m])
            def _(m=m):
                act(1 + m, from_at[m])

    def send_near(slot, high_at):
        copy(
            owned.at[owned_at(high_at, 1 - mid)], direct.at[slot, mid, core],
            near_tiles_send.at[slot], near_tiles_recv.at[slot],
            device(high, 1 - mid, core, col),
        )
        copy(
            owned.at[owned_at(high_at, mid)], direct.at[slot, mid, core],
            core_tiles_send.at[slot, 0], core_tiles_recv.at[slot, 0], partner,
        )

    each_slot(send_near)

    def begin(step, chain):
        own = low.at[step, chain, 0]
        for m in reversed(range(line)):

            @pl.when(into_ok[m])
            def _(m=m):
                copy(
                    own, low.at[step, chain, plane + m],
                    line_send.at[step, chain, m], line_recv.at[step, chain, m],
                    device(into_at[m], mid, core, col),
                )

        for offset in range(1, plane):
            copy(
                own, low.at[step, chain, plane - offset],
                low_send.at[step, chain], low_recv.at[step, chain], beside(offset),
            )

    wait(take, give_recv)
    for chain in range(PARTS):
        state[0, chain, :, lanes(1 - core, tile)] = take[chain * cut : (chain + 1) * cut, :]
        low[0, chain, 0] = state[0, chain].astype(jnp.bfloat16)
        begin(0, chain)

    def pass_near(slot, high_at):
        block = direct.at[slot, 1 - mid, core]
        wait(block, near_tiles_recv.at[slot])
        copy(
            block, block, core_tiles_send.at[slot, 1], core_tiles_recv.at[slot, 1], partner
        )

    def pass_far(m, offset):
        other = (col + offset) % near
        block = mirror.at[m, core, other]
        wait(block, far_tiles_recv.at[m, other])
        copy(block, block, core_far_send.at[m, other], core_far_recv.at[m, other], partner)

    def spots(slot, mid_at, core_at, other_core, col_at):
        offset = (mid_at * near + col_at + plane - here) % plane
        inner = pl.ds(pl.multiple_of((offset * 2 + core_at) * tile, tile), tile)
        outer = pl.ds(pl.multiple_of((slot * 2 + other_core) * tile, tile), tile)
        return inner, outer

    def fill_near(slot, mid_at, core_at):
        def fill(index, carry):
            other_core, col_at = index // near, index % near
            inner, outer = spots(slot, mid_at, core_at, other_core, col_at)
            block = direct[slot, mid_at, core_at, other_core, col_at]
            forward[inner, outer] = block
            backward[outer, inner] = block.T
            return carry

        lax.fori_loop(0, 2 * near, fill, 0, unroll=2)

    def fill_slot(slot, high_at):
        fill_near(slot, mid, core)
        fill_near(slot, 1 - mid, core)
        wait(direct.at[slot, mid, 1 - core], core_tiles_recv.at[slot, 0])
        fill_near(slot, mid, 1 - core)
        wait(direct.at[slot, 1 - mid, 1 - core], core_tiles_recv.at[slot, 1])
        fill_near(slot, 1 - mid, 1 - core)

    def fill_far(m, offset, other_core):
        col_at = (col + offset) % near

        def fill(index, carry):
            inner, outer = spots(1 + m, index // 2, index % 2, other_core, col_at)
            block = mirror[m, other_core, col_at, index]
            forward[inner, outer] += block.T
            backward[outer, inner] += block
            return carry

        lax.fori_loop(0, 4, fill, 0, unroll=2)

    def fill_pair(m, offset):
        fill_far(m, offset, core)
        other = (col + offset) % near
        wait(mirror.at[m, 1 - core, other], core_far_recv.at[m, other])
        fill_far(m, offset, 1 - core)

    def when_from(m, act):
        @pl.when(from_ok[m])
        def _():
            act()

    pass_near(0, high)
    order = list(reversed(range(line)))
    for place, m in enumerate(order):
        for offset in range(near):
            when_from(m, lambda m=m, offset=offset: pass_far(m, offset))
            if offset == 0:
                when_from(m, lambda m=m: pass_near(1 + m, from_at[m]))
                if place == 0:
                    fill_slot(0, high)
        if place + 1 < line:
            when_from(m, lambda m=m: fill_slot(1 + m, from_at[m]))
            for offset in range(near):
                when_from(m, lambda m=m, offset=offset: fill_pair(m, offset))
        else:
            when_from(m, lambda m=m: fill_slot(1 + m, from_at[m]))
    for offset in range(near):
        when_from(order[-1], lambda offset=offset: fill_pair(order[-1], offset))

    def product(step, chain):
        wait(low.at[step, chain, pl.ds(1, plane - 1)], low_recv.at[step, chain])
        vectors = jnp.concatenate([low[step, chain, at] for at in range(plane)], axis=1)
        total = jnp.dot(vectors, forward[...], preferred_element_type=jnp.float32)
        kept = total[:, :pair]
        for m in range(line):
            at = plane - 1 + m
            part_out[step, chain, at] = total[:, (1 + m) * pair : (2 + m) * pair].astype(
                jnp.bfloat16
            )
        for m in reversed(range(line)):

            @pl.when(from_ok[m])
            def _(m=m):
                at = plane - 1 + m
                copy(
                    part_out.at[step, chain, at], part_in.at[step, chain, at],
                    back_send.at[step, chain, m], back_recv.at[step, chain, m],
                    device(from_at[m], mid, core, col),
                )

        for m in range(line):

            @pl.when(from_ok[m])
            def _(m=m):
                wait(low.at[step, chain, plane + m], line_recv.at[step, chain, m])

        vectors = jnp.concatenate(
            [low[step, chain, at] for at in [0, *range(plane, plane + line)]], axis=1
        )
        total = jnp.dot(vectors, backward[...], preferred_element_type=jnp.float32)
        mine[chain] = kept + total[:, :pair]
        for offset in range(1, plane):
            part_out[step, chain, offset - 1] = total[
                :, offset * pair : (offset + 1) * pair
            ].astype(jnp.bfloat16)
            copy(
                part_out.at[step, chain, offset - 1],
                part_in.at[step, chain, plane - offset - 1],
                part_send.at[step, chain], part_recv.at[step, chain], beside(offset),
            )

    def finish(step, chain, sigma):
        wait(part_in.at[step, chain, pl.ds(0, plane - 1)], part_recv.at[step, chain])
        for m in range(line):

            @pl.when(into_ok[m])
            def _(m=m):
                wait(part_in.at[step, chain, plane - 1 + m], back_recv.at[step, chain, m])

        total = mine[chain]
        for at in range(plane - 1 + line):
            total = total + part_in[step, chain, at].astype(jnp.float32)
        current = state[step, chain]
        if step == 0:
            sigma_next = sigma_one
            following = (total - center * current) * (sigma_one / half_width)
        else:
            sigma_next = 1.0 / (2.0 / sigma_one - sigma)
            following = (total - center * current) * (
                2.0 * sigma_next / half_width
            ) - (sigma * sigma_next) * state[step - 1, chain]
        if step == DEGREE - 1:
            last[chain] = following
            copy(
                last.at[chain, :, lanes(1 - core, tile)], last_in.at[chain],
                last_send.at[chain], last_recv.at[chain], partner,
            )
        else:
            low[step + 1, chain, 0] = following.astype(jnp.bfloat16)
            begin(step + 1, chain)
            state[step + 1, chain] = following
        return sigma_next

    sigmas = [sigma_one] * PARTS
    for step in range(DEGREE):
        for chain in range(PARTS):
            product(step, chain)
        for chain in range(PARTS):
            sigmas[chain] = finish(step, chain, sigmas[chain])

    own = last[:, :, lanes(core, tile)].reshape(half, tile)
    out_ref[:, lanes(core, half)] = own.T
    for chain in range(PARTS):
        wait(last_in.at[chain], last_recv.at[chain])
    out_ref[:, lanes(1 - core, half)] = last_in[...].reshape(half, tile).T

    wait(give, give_send)
    for chain in range(PARTS):
        wait(last_in.at[chain], last_send.at[chain])

    def close_near(slot, high_at):
        block = direct.at[slot, mid, core]
        wait(block, near_tiles_send.at[slot])
        wait(block, core_tiles_send.at[slot, 0])
        wait(block, core_tiles_send.at[slot, 1])

    each_slot(close_near)
    for m in range(line):

        @pl.when(from_ok[m])
        def _(m=m):
            for other in range(near):
                wait(mirror.at[m, core, other], core_far_send.at[m, other])
            for step in range(DEGREE):
                for chain in range(PARTS):
                    wait(part_out.at[step, chain, plane - 1 + m], back_send.at[step, chain, m])

        @pl.when(into_ok[m])
        def _(m=m):
            wait(mirror.at[m, core], far_tiles_send.at[m])
            for step in range(DEGREE):
                for chain in range(PARTS):
                    wait(low.at[step, chain, 0], line_send.at[step, chain, m])

    for step in range(DEGREE):
        for chain in range(PARTS):
            wait(low.at[step, chain, pl.ds(1, plane - 1)], low_send.at[step, chain])
            wait(part_out.at[step, chain, pl.ds(0, plane - 1)], part_send.at[step, chain])


def plane_scratch(tall, near, slots, tile, width):
    far = 4 * tall
    plane = 2 * near
    line = tall // 2
    half = width // 2
    cut = half // PARTS
    pair = 2 * tile
    bf16, f32 = jnp.bfloat16, jnp.float32
    memory = [
        ((slots + 1, tile, tile), bf16),
        ((far, near, tile, tile), bf16),
        ((1 + line, 2, 2, 2, near, tile, tile), bf16),
        ((line, 2, near, 4, tile, tile), bf16),
        ((plane * pair, (1 + line) * pair), bf16),
        (((1 + line) * pair, plane * pair), bf16),
        ((half, tile), f32),
        ((half, tile), f32),
        ((DEGREE, PARTS, plane + line, cut, pair), bf16),
        ((DEGREE, PARTS, plane - 1 + line, cut, pair), bf16),
        ((DEGREE, PARTS, plane - 1 + line, cut, pair), bf16),
        ((PARTS, cut, pair), f32),
        ((DEGREE, PARTS, cut, pair), f32),
        ((PARTS, cut, pair), f32),
        ((PARTS, cut, tile), f32),
        ((tile, width), f32),
    ]
    chains = (DEGREE, PARTS)
    semaphores = [
        (1 + line,), (line,), (1 + line, 2), (line, near),
        (1 + line,), (line, near), (1 + line, 2), (line, near),
        (), (), chains, (*chains, line), chains, (*chains, line),
        chains, (*chains, line), chains, (*chains, line), (PARTS,), (PARTS,),
    ]
    size = sum(math.prod(shape) * jnp.dtype(kind).itemsize for shape, kind in memory)
    shapes = [pltpu.VMEM(shape, kind) for shape, kind in memory]
    shapes += [
        pltpu.SMEM((slots,), jnp.int32),
        pltpu.SMEM((slots,), jnp.int32),
        pltpu.SMEM((3,), jnp.float32),
        pltpu.SemaphoreType.DMA((5,)),
    ]
    return size, shapes + [pltpu.SemaphoreType.DMA(shape) for shape in semaphores]


def wide_scratch(far, near, slots, tile, width):
    count = far * near
    cut = width // CHAINS
    return [
        pltpu.VMEM((slots + 1, tile, tile), jnp.bfloat16),
        pltpu.VMEM((count, tile, tile), jnp.bfloat16),
        pltpu.VMEM((count, tile, tile), jnp.bfloat16),
        pltpu.VMEM((near * tile, far * tile), jnp.bfloat16),
        pltpu.VMEM((tile, tile), jnp.bfloat16),
        pltpu.VMEM((DEGREE, CHAINS, far, tile, cut), jnp.bfloat16),
        pltpu.VMEM((DEGREE, CHAINS, near, tile, cut), jnp.float32),
        pltpu.VMEM((DEGREE, CHAINS, near, tile, cut), jnp.float32),
        pltpu.VMEM((CHAINS, tile, cut), jnp.float32),
        pltpu.VMEM((DEGREE, tile, width), jnp.float32),
        pltpu.SemaphoreType.DMA(()),
        pltpu.SemaphoreType.DMA((far,)),
        pltpu.SemaphoreType.DMA((DEGREE, CHAINS)),
        pltpu.SemaphoreType.DMA((DEGREE, CHAINS, far)),
        pltpu.SemaphoreType.DMA((DEGREE, CHAINS)),
        pltpu.SemaphoreType.DMA((DEGREE, CHAINS, near)),
    ]


def local(start_block, tiles, tile_rows, tile_cols, bounds):
    tall, width = start_block.shape
    tile = tiles.shape[-1]
    slots = tiles.shape[2]
    far = lax.axis_size("row")
    near = lax.axis_size("col")
    assert tall == tile and far % 4 == 0
    smem = pl.BlockSpec(memory_space=pltpu.SMEM)
    vmem = pl.BlockSpec(memory_space=pltpu.VMEM)
    body = functools.partial(wide_kernel, far, near, slots, tile, width)
    scratch = wide_scratch(far, near, slots, tile, width)
    in_specs = [smem, smem, smem, vmem, vmem]
    if far % 8 == 0:
        size, shapes = plane_scratch(far // 4, near, slots, tile, width)
        if size <= ROOM:
            body = functools.partial(plane_kernel, far // 4, near, slots, tile, width)
            scratch = shapes
            in_specs = [pl.BlockSpec(memory_space=pl.ANY)] * 5
    return pl.pallas_call(
        body,
        out_shape=pltpu.VMEM((tall, width), jnp.float32),
        in_specs=in_specs,
        out_specs=vmem,
        scratch_shapes=scratch,
        compiler_params=pltpu.CompilerParams(
            collective_id=0, has_side_effects=True, vmem_limit_bytes=60 * 1024 * 1024
        ),
    )(
        tile_rows.reshape(slots),
        tile_cols.reshape(slots),
        bounds,
        start_block,
        tiles.reshape(slots, tile, tile),
    )


def solution(mesh):
    placed = (
        P(("row", "col"), None),
        P("row", "col", None, None, None),
        P("row", "col", None),
        P("row", "col", None),
        P(),
    )
    return jax.shard_map(
        local, mesh=mesh, in_specs=placed, out_specs=P(("row", "col"), None), check_vma=False
    )
```

```python
import functools
import math

import jax
import jax.numpy as jnp
from jax import lax
from jax.experimental import pallas as pl
from jax.experimental.pallas import tpu as pltpu
from jax.sharding import PartitionSpec as P

DEGREE = 4
CHAINS = 2
LAG = 0
PARTS = 4
ROOM = 48 * 1024 * 1024
MESH = pl.DeviceIdType.MESH


def wide_kernel(
    far, near, slots, tile, width,
    rows_ref, cols_ref, bounds_ref, start_ref, tiles_ref, out_ref,
    placed, owned, mirror, window, diagonal, low, partial, arrived, mine, state,
    tile_send, tile_recv, low_send, low_recv, part_send, part_recv,
):
    chips = far // 2
    tall = far // 4
    count = far * near
    cut = width // CHAINS
    row = lax.axis_index("row")
    col = lax.axis_index("col")
    me = row * near + col
    core = row % 2
    mid = row // 2 % 2
    high = row // 4

    def spot(high_at, mid_at, core_at):
        return core_at * chips + high_at * 2 + mid_at

    def row_of(high_at, mid_at, core_at):
        return (high_at * 2 + mid_at) * 2 + core_at

    own_spot = spot(high, mid, core)

    barrier = pltpu.get_barrier_semaphore()

    def greet(step, carry):
        other = (me + step) % count
        pl.semaphore_signal(
            barrier, inc=1, device_id=(other // near, other % near), device_id_type=MESH
        )
        return carry

    lax.fori_loop(1, count, greet, 0)

    line = (1, cut)
    lowest = jnp.full(line, bounds_ref[0], jnp.float32)
    lower = jnp.full(line, bounds_ref[1], jnp.float32)
    upper = jnp.full(line, bounds_ref[2], jnp.float32)
    half_width = (upper - lower) * 0.5
    center = (upper + lower) * 0.5
    sigma_one = half_width / (lowest - center)

    def columns(chain):
        return slice(chain * cut, (chain + 1) * cut)

    for chain in range(CHAINS):
        low[0, chain, own_spot] = start_ref[:, columns(chain)].astype(jnp.bfloat16)

    for slot in range(slots):
        placed[slot] = tiles_ref[slot]
    placed[slots] = jnp.zeros((tile, tile), jnp.bfloat16)
    places = []
    for slot in range(slots):
        glob_row = rows_ref[slot]
        glob_col = cols_ref[slot]
        place = (glob_col // near) * near + (glob_row - row * near)
        places.append(jnp.where(glob_row >= 0, place, -1))

    def put(position, carry):
        chosen = jnp.int32(slots)
        for slot in range(slots):
            chosen = jnp.where(places[slot] == position, slot, chosen)
        owned[position] = placed[chosen]
        return carry

    lax.fori_loop(0, count, put, 0)
    diagonal[...] = owned[me]
    mirror[me] = diagonal[...]
    owned[me] = jnp.zeros((tile, tile), jnp.bfloat16)

    pl.semaphore_wait(barrier, count - 1)

    flip = high >= tall // 2
    near_end = jnp.where(flip, tall - 1 - high, high)

    def along(position):
        return jnp.where(flip, tall - 1 - position, position)

    def ranked(index):
        return index + jnp.where(index >= near_end, 1, 0)

    def send_low(step, chain, place, target_row):
        pltpu.make_async_remote_copy(
            src_ref=low.at[step, chain, place],
            dst_ref=low.at[step, chain, place],
            send_sem=low_send.at[step, chain],
            recv_sem=low_recv.at[step, chain, place],
            device_id=(target_row, col),
            device_id_type=MESH,
        ).start()

    def await_low(step, chain, place):
        here = low.at[step, chain, place]
        pltpu.make_async_copy(here, here, low_recv.at[step, chain, place]).wait()

    def begin(step, chain):
        send_low(step, chain, own_spot, row_of(high, 1 - mid, core))
        for index in range(tall - 1):
            send_low(step, chain, own_spot, row_of(along(ranked(index)), mid, core))
        send_low(step, chain, own_spot, row_of(high, mid, 1 - core))

    def forward_line(step, chain):
        for index in range(tall - 1):
            place = spot(along(ranked(index)), mid, core)
            await_low(step, chain, place)
            send_low(step, chain, place, row_of(high, 1 - mid, core))
            send_low(step, chain, place, row_of(high, mid, 1 - core))

    def forward_mid(step, chain):
        for index in range(tall):
            source = high if index == 0 else along(ranked(index - 1))
            place = spot(source, 1 - mid, core)
            await_low(step, chain, place)
            send_low(step, chain, place, row_of(high, mid, 1 - core))

    def await_core(step, chain):
        for offset in range(tall):
            for mid_at in range(2):
                await_low(step, chain, spot((high + offset) % tall, mid_at, 1 - core))

    def send_tiles(high_at):
        inner = me % (4 * near)

        def send_tile(offset, carry):
            other = high_at * (4 * near) + (inner + offset) % (4 * near)
            pltpu.make_async_remote_copy(
                src_ref=owned.at[other],
                dst_ref=mirror.at[me],
                send_sem=tile_send,
                recv_sem=tile_recv.at[row],
                device_id=(other // near, other % near),
                device_id_type=MESH,
            ).start()
            return carry

        return send_tile

    def send_group(index):
        if index < 0:
            lax.fori_loop(1, 4 * near, send_tiles(high), 0)
        else:
            lax.fori_loop(0, 4 * near, send_tiles(along(ranked(index))), 0)

    def build(step, carry):
        source = (row + far - step) % far
        base = source * near
        group = mirror.at[pl.ds(base, near)]
        pltpu.make_async_copy(group, group, tile_recv.at[source]).wait()
        fill(source)
        return carry

    def fill(source):
        lanes = (source % 2) * chips + source // 2
        lanes = pl.ds(pl.multiple_of(lanes * tile, tile), tile)
        for near_at in range(near):
            index = source * near + near_at
            window[near_at * tile : (near_at + 1) * tile, lanes] = (
                owned[index] + mirror[index].T
            )

    def multiply(step, chain, near_at):
        total = jnp.zeros((tile, cut), jnp.float32)
        matrix = window[pl.ds(pl.multiple_of(near_at * tile, tile), tile), :]
        vectors = low[step, chain].reshape(far * tile, cut)
        return total + jnp.dot(matrix, vectors, preferred_element_type=jnp.float32)

    def product(step, chain):
        for offset in range(1, near):
            other = (col + offset) % near
            partial[step, chain, other] = multiply(step, chain, other)
            pltpu.make_async_remote_copy(
                src_ref=partial.at[step, chain, other],
                dst_ref=arrived.at[step, chain, col],
                send_sem=part_send.at[step, chain],
                recv_sem=part_recv.at[step, chain, col],
                device_id=(row, other),
                device_id_type=MESH,
            ).start()
        mine[chain] = multiply(step, chain, col) + jnp.dot(
            diagonal[...], low[step, chain, own_spot], preferred_element_type=jnp.float32
        )

    def finish(step, chain, sigma):
        total = mine[chain]
        for offset in range(1, near):
            other = (col + offset) % near
            here = arrived.at[step, chain, other]
            pltpu.make_async_copy(here, here, part_recv.at[step, chain, other]).wait()
            total = total + arrived[step, chain, other]
        where = columns(chain)
        current = start_ref[:, where] if step == 0 else state[step - 1, :, where]
        if step == 0:
            following = (total - center * current) * (sigma_one / half_width)
            sigma_next = sigma_one
        else:
            before = start_ref[:, where] if step == 1 else state[step - 2, :, where]
            sigma_next = 1.0 / (2.0 / sigma_one - sigma)
            following = (total - center * current) * (
                2.0 * sigma_next / half_width
            ) - (sigma * sigma_next) * before
        if step == DEGREE - 1:
            out_ref[:, where] = following
        else:
            low[step + 1, chain, own_spot] = following.astype(jnp.bfloat16)
            begin(step + 1, chain)
            state[step, :, where] = following
        return sigma_next

    for chain in range(CHAINS):
        begin(0, chain)
    groups = list(range(tall - 2, -2, -1))
    for index in groups:
        send_group(index)
    for chain in range(CHAINS):
        forward_line(0, chain)
    for chain in range(CHAINS):
        forward_mid(0, chain)

    if near > 1:
        group = mirror.at[pl.ds(row * near, near - 1)]
        pltpu.make_async_copy(group, group, tile_recv.at[row]).wait()
    fill(row)
    lax.fori_loop(1, far, build, 0)

    sigmas = [sigma_one] * CHAINS

    def phase(chain, index):
        step, part = index // 4, index % 4
        if part == 0:
            forward_line(step, chain)
        elif part == 1:
            forward_mid(step, chain)
        elif part == 2:
            await_core(step, chain)
            product(step, chain)
        else:
            sigmas[chain] = finish(step, chain, sigmas[chain])

    for index in range(2, 4 * DEGREE + LAG * (CHAINS - 1)):
        for chain in range(CHAINS):
            own_index = index - LAG * chain
            if 2 <= own_index < 4 * DEGREE:
                phase(chain, own_index)

    group = owned.at[pl.ds(0, count - 1)]
    pltpu.make_async_copy(group, group, tile_send).wait()
    for step in range(DEGREE):
        for chain in range(CHAINS):
            group = low.at[step, chain, pl.ds(0, far - 1)]
            pltpu.make_async_copy(group, group, low_send.at[step, chain]).wait()
            if near > 1:
                group = partial.at[step, chain, pl.ds(0, near - 1)]
                pltpu.make_async_copy(group, group, part_send.at[step, chain]).wait()


def plane_kernel(
    tall, near, slots, tile, width,
    rows_ref, cols_ref, bounds_ref, start_ref, tiles_ref, out_ref,
    placed, owned, direct, mirror, forward, backward, give, take, low,
    part_out, part_in, mine, state, last, last_in, start, row_of, col_of, limits, load,
    near_tiles_send, far_tiles_send, core_tiles_send, core_far_send,
    near_tiles_recv, far_tiles_recv, core_tiles_recv, core_far_recv,
    give_send, give_recv, low_send, line_send, low_recv, line_recv,
    part_send, back_send, part_recv, back_recv, last_send, last_recv,
):
    far = 4 * tall
    plane = 2 * near
    line = tall // 2
    half = width // 2
    cut = half // PARTS
    pair = 2 * tile
    row = lax.axis_index("row")
    col = lax.axis_index("col")
    core = row % 2
    mid = row // 2 % 2
    high = row // 4

    def device(high_at, mid_at, core_at, col_at):
        return ((high_at * 2 + mid_at) * 2 + core_at, col_at)

    def beside(offset):
        return device(high, (mid + offset // near) % 2, core, (col + offset % near) % near)

    def opposite(offset):
        return offset // near * near + (near - offset % near) % near

    offsets = list(reversed(range(1, plane)))

    partner = device(high, mid, 1 - core, col)

    from_ok = [high != 2 * m for m in range(line)]
    from_at = [
        jnp.where(high < 2 * m, high + tall - 2 * m, high - 2 * m - 1) for m in range(line)
    ]
    into_ok = [high != tall - 1 - 2 * m for m in range(line)]
    into_at = [
        jnp.where(high >= tall - 2 * m, high - tall + 2 * m, high + 2 * m + 1)
        for m in range(line)
    ]

    def copy(src, dst, send, recv, to):
        pltpu.make_async_remote_copy(
            src_ref=src, dst_ref=dst, send_sem=send, recv_sem=recv,
            device_id=to, device_id_type=MESH,
        ).start()

    def wait(ref, sem):
        pltpu.make_async_copy(ref, ref, sem).wait()

    barrier = pltpu.get_barrier_semaphore()

    def greet(to):
        pl.semaphore_signal(barrier, inc=1, device_id=to, device_id_type=MESH)

    for step in reversed(range(1, tall)):
        for offset in range(near):
            greet(device((high + step) % tall, mid, core, (col + offset) % near))
    for offset in offsets:
        greet(beside(offset))
    greet(partner)

    loads = [
        pltpu.make_async_copy(src, dst, load.at[index])
        for index, (src, dst) in enumerate(
            [
                (rows_ref, row_of),
                (cols_ref, col_of),
                (bounds_ref, limits),
                (start_ref, start),
                (tiles_ref, placed.at[pl.ds(0, slots)]),
            ]
        )
    ]
    for item in loads:
        item.start()
    placed[slots] = jnp.zeros((tile, tile), jnp.bfloat16)
    loads[0].wait()
    loads[1].wait()

    def lanes(at, size):
        return pl.ds(pl.multiple_of(at * size, size), size)

    places = []
    for slot in range(slots):
        glob_row = row_of[slot]
        glob_col = col_of[slot]
        place = (glob_col // near) * near + (glob_row - row * near)
        places.append(jnp.where(glob_row >= 0, place, -1))

    def pick(high_at):
        def put(index, carry):
            at, other = high_at * 4 + index // near, index % near
            chosen = jnp.int32(slots)
            for slot in range(slots):
                chosen = jnp.where(places[slot] == at * near + other, slot, chosen)
            owned[at, other] = placed[chosen]
            return carry

        lax.fori_loop(0, 4 * near, put, 0, unroll=4)

    loads[4].wait()
    for m in reversed(range(line)):

        @pl.when(into_ok[m])
        def _(m=m):
            pick(into_at[m])

    def owned_at(high_at, mid_at):
        return pl.ds((high_at * 2 + mid_at) * 2, 2)

    pl.semaphore_wait(barrier, (tall - 1) * near + plane)

    for m in reversed(range(line)):

        @pl.when(into_ok[m])
        def _(m=m):
            for offset in range(near):
                other = (col + offset) % near
                copy(
                    owned.at[pl.ds(into_at[m] * 4, 4), other], mirror.at[m, core, col],
                    far_tiles_send.at[m], far_tiles_recv.at[m, col],
                    device(into_at[m], mid, core, other),
                )

    def each_slot(act):
        act(0, high)
        for m in reversed(range(line)):

            @pl.when(from_ok[m])
            def _(m=m):
                act(1 + m, from_at[m])

    def send_near(slot, high_at):
        copy(
            owned.at[owned_at(high_at, 1 - mid)], direct.at[slot, mid, core],
            near_tiles_send.at[slot], near_tiles_recv.at[slot],
            device(high, 1 - mid, core, col),
        )
        copy(
            owned.at[owned_at(high_at, mid)], direct.at[slot, mid, core],
            core_tiles_send.at[slot, 0], core_tiles_recv.at[slot, 0], partner,
        )

    each_slot(lambda slot, high_at: pick(high_at))
    each_slot(send_near)

    loads[3].wait()
    give[...] = start[:, lanes(1 - core, half)].T
    copy(give, take, give_send, give_recv, partner)
    kept = start[:, lanes(core, half)].T
    for chain in range(PARTS):
        state[0, chain, :, lanes(core, tile)] = kept[chain * cut : (chain + 1) * cut]


    loads[2].wait()
    span = (1, pair)
    lowest = jnp.full(span, limits[0], jnp.float32)
    lower = jnp.full(span, limits[1], jnp.float32)
    upper = jnp.full(span, limits[2], jnp.float32)
    half_width = (upper - lower) * 0.5
    center = (upper + lower) * 0.5
    sigma_one = half_width / (lowest - center)

    scales = [sigma_one / half_width]
    shares = [None]
    sigma = sigma_one
    for step in range(1, DEGREE):
        sigma_next = 1.0 / (2.0 / sigma_one - sigma)
        scales.append(2.0 * sigma_next / half_width)
        shares.append(sigma * sigma_next)
        sigma = sigma_next

    direct[0, mid, core] = owned[owned_at(high, mid)]
    for m in range(line):

        @pl.when(from_ok[m])
        def _(m=m):
            direct[1 + m, mid, core] = owned[owned_at(from_at[m], mid)]

        @pl.when(jnp.logical_not(from_ok[m]))
        def _(m=m):
            forward[:, (1 + m) * pair : (2 + m) * pair] = jnp.zeros(
                (plane * pair, pair), jnp.bfloat16
            )
            backward[(1 + m) * pair : (2 + m) * pair, :] = jnp.zeros(
                (pair, plane * pair), jnp.bfloat16
            )
            for step in range(DEGREE):
                for chain in range(PARTS):
                    low[step, chain, plane + m] = jnp.zeros((cut, pair), jnp.bfloat16)

        @pl.when(jnp.logical_not(into_ok[m]))
        def _(m=m):
            for step in range(DEGREE):
                for chain in range(PARTS):
                    part_in[step, chain, plane - 1 + m] = jnp.zeros((cut, pair), jnp.bfloat16)


    def begin(step, chain):
        own = low.at[step, chain, 0]
        for m in reversed(range(line)):

            @pl.when(into_ok[m])
            def _(m=m):
                copy(
                    own, low.at[step, chain, plane + m],
                    line_send.at[step, chain, m], line_recv.at[step, chain, m],
                    device(into_at[m], mid, core, col),
                )

        for offset in offsets:
            copy(
                own, low.at[step, chain, opposite(offset)],
                low_send.at[step, chain], low_recv.at[step, chain], beside(offset),
            )

    wait(take, give_recv)
    for chain in range(PARTS):
        state[0, chain, :, lanes(1 - core, tile)] = take[chain * cut : (chain + 1) * cut, :]
        low[0, chain, 0] = state[0, chain].astype(jnp.bfloat16)
        begin(0, chain)

    def pass_near(slot, high_at):
        block = direct.at[slot, 1 - mid, core]
        wait(block, near_tiles_recv.at[slot])
        copy(
            block, block, core_tiles_send.at[slot, 1], core_tiles_recv.at[slot, 1], partner
        )

    def pass_far(m, offset):
        other = (col + offset) % near
        block = mirror.at[m, core, other]
        wait(block, far_tiles_recv.at[m, other])
        copy(block, block, core_far_send.at[m, other], core_far_recv.at[m, other], partner)

    def spots(slot, mid_at, core_at, other_core, col_at):
        offset = (mid_at + mid) % 2 * near + (col_at + near - col) % near
        inner = pl.ds(pl.multiple_of((offset * 2 + core_at) * tile, tile), tile)
        outer = pl.ds(pl.multiple_of((slot * 2 + other_core) * tile, tile), tile)
        return inner, outer

    def fill_near(slot, mid_at, core_at):
        def fill(index, carry):
            other_core, col_at = index // near, index % near
            inner, outer = spots(slot, mid_at, core_at, other_core, col_at)
            block = direct[slot, mid_at, core_at, other_core, col_at]
            forward[inner, outer] = block
            backward[outer, inner] = block.T
            return carry

        lax.fori_loop(0, 2 * near, fill, 0, unroll=2)

    def fill_slot(slot, high_at):
        fill_near(slot, mid, core)
        fill_near(slot, 1 - mid, core)
        wait(direct.at[slot, mid, 1 - core], core_tiles_recv.at[slot, 0])
        fill_near(slot, mid, 1 - core)
        wait(direct.at[slot, 1 - mid, 1 - core], core_tiles_recv.at[slot, 1])
        fill_near(slot, 1 - mid, 1 - core)

    def fill_far(m, offset, other_core):
        col_at = (col + offset) % near

        def fill(index, carry):
            inner, outer = spots(1 + m, index // 2, index % 2, other_core, col_at)
            block = mirror[m, other_core, col_at, index]
            forward[inner, outer] += block.T
            backward[outer, inner] += block
            return carry

        lax.fori_loop(0, 4, fill, 0, unroll=2)

    def fill_pair(m, offset):
        fill_far(m, offset, core)
        other = (col + offset) % near
        wait(mirror.at[m, 1 - core, other], core_far_recv.at[m, other])
        fill_far(m, offset, 1 - core)

    def when_from(m, act):
        @pl.when(from_ok[m])
        def _():
            act()

    pass_near(0, high)
    order = list(reversed(range(line)))
    for place, m in enumerate(order):
        for offset in range(near):
            when_from(m, lambda m=m, offset=offset: pass_far(m, offset))
            if offset == 0:
                when_from(m, lambda m=m: pass_near(1 + m, from_at[m]))
                if place == 0:
                    fill_slot(0, high)
        if place + 1 < line:
            when_from(m, lambda m=m: fill_slot(1 + m, from_at[m]))
            for offset in range(near):
                when_from(m, lambda m=m, offset=offset: fill_pair(m, offset))
        else:
            when_from(m, lambda m=m: fill_slot(1 + m, from_at[m]))
    for offset in range(near):
        when_from(order[-1], lambda offset=offset: fill_pair(order[-1], offset))

    def product(step, chain):
        wait(low.at[step, chain, pl.ds(1, plane - 1)], low_recv.at[step, chain])
        vectors = jnp.concatenate([low[step, chain, at] for at in range(plane)], axis=1)
        total = jnp.dot(vectors, forward[...], preferred_element_type=jnp.float32)
        kept = total[:, :pair]
        for m in range(line):
            at = plane - 1 + m
            part_out[step, chain, at] = total[:, (1 + m) * pair : (2 + m) * pair].astype(
                jnp.bfloat16
            )
        for m in reversed(range(line)):

            @pl.when(from_ok[m])
            def _(m=m):
                at = plane - 1 + m
                copy(
                    part_out.at[step, chain, at], part_in.at[step, chain, at],
                    back_send.at[step, chain, m], back_recv.at[step, chain, m],
                    device(from_at[m], mid, core, col),
                )

        for m in range(line):

            @pl.when(from_ok[m])
            def _(m=m):
                wait(low.at[step, chain, plane + m], line_recv.at[step, chain, m])

        vectors = jnp.concatenate(
            [low[step, chain, at] for at in [0, *range(plane, plane + line)]], axis=1
        )
        total = jnp.dot(vectors, backward[...], preferred_element_type=jnp.float32)
        mine[chain] = kept + total[:, :pair]
        for offset in offsets:
            part_out[step, chain, offset - 1] = total[
                :, offset * pair : (offset + 1) * pair
            ].astype(jnp.bfloat16)
            copy(
                part_out.at[step, chain, offset - 1],
                part_in.at[step, chain, opposite(offset) - 1],
                part_send.at[step, chain], part_recv.at[step, chain], beside(offset),
            )

    def finish(step, chain):
        wait(part_in.at[step, chain, pl.ds(0, plane - 1)], part_recv.at[step, chain])
        for m in range(line):

            @pl.when(into_ok[m])
            def _(m=m):
                wait(part_in.at[step, chain, plane - 1 + m], back_recv.at[step, chain, m])

        total = mine[chain]
        for at in range(plane - 1 + line):
            total = total + part_in[step, chain, at].astype(jnp.float32)
        current = state[step, chain]
        following = (total - center * current) * scales[step]
        if step > 0:
            following = following - shares[step] * state[step - 1, chain]
        if step == DEGREE - 1:
            last[chain] = following
            copy(
                last.at[chain, :, lanes(1 - core, tile)], last_in.at[chain],
                last_send.at[chain], last_recv.at[chain], partner,
            )
        else:
            low[step + 1, chain, 0] = following.astype(jnp.bfloat16)
            begin(step + 1, chain)
            state[step + 1, chain] = following

    for step in range(DEGREE):
        for chain in range(PARTS):
            product(step, chain)
        for chain in range(PARTS):
            finish(step, chain)

    own = last[:, :, lanes(core, tile)].reshape(half, tile)
    out_ref[:, lanes(core, half)] = own.T
    for chain in range(PARTS):
        wait(last_in.at[chain], last_recv.at[chain])
    out_ref[:, lanes(1 - core, half)] = last_in[...].reshape(half, tile).T

    wait(give, give_send)
    for chain in range(PARTS):
        wait(last_in.at[chain], last_send.at[chain])

    def close_near(slot, high_at):
        block = direct.at[slot, mid, core]
        wait(block, near_tiles_send.at[slot])
        wait(block, core_tiles_send.at[slot, 0])
        wait(block, core_tiles_send.at[slot, 1])

    each_slot(close_near)
    for m in range(line):

        @pl.when(from_ok[m])
        def _(m=m):
            for other in range(near):
                wait(mirror.at[m, core, other], core_far_send.at[m, other])
            for step in range(DEGREE):
                for chain in range(PARTS):
                    wait(part_out.at[step, chain, plane - 1 + m], back_send.at[step, chain, m])

        @pl.when(into_ok[m])
        def _(m=m):
            wait(mirror.at[m, core], far_tiles_send.at[m])
            for step in range(DEGREE):
                for chain in range(PARTS):
                    wait(low.at[step, chain, 0], line_send.at[step, chain, m])

    for step in range(DEGREE):
        for chain in range(PARTS):
            wait(low.at[step, chain, pl.ds(1, plane - 1)], low_send.at[step, chain])
            wait(part_out.at[step, chain, pl.ds(0, plane - 1)], part_send.at[step, chain])


def plane_scratch(tall, near, slots, tile, width):
    far = 4 * tall
    plane = 2 * near
    line = tall // 2
    half = width // 2
    cut = half // PARTS
    pair = 2 * tile
    bf16, f32 = jnp.bfloat16, jnp.float32
    memory = [
        ((slots + 1, tile, tile), bf16),
        ((far, near, tile, tile), bf16),
        ((1 + line, 2, 2, 2, near, tile, tile), bf16),
        ((line, 2, near, 4, tile, tile), bf16),
        ((plane * pair, (1 + line) * pair), bf16),
        (((1 + line) * pair, plane * pair), bf16),
        ((half, tile), f32),
        ((half, tile), f32),
        ((DEGREE, PARTS, plane + line, cut, pair), bf16),
        ((DEGREE, PARTS, plane - 1 + line, cut, pair), bf16),
        ((DEGREE, PARTS, plane - 1 + line, cut, pair), bf16),
        ((PARTS, cut, pair), f32),
        ((DEGREE, PARTS, cut, pair), f32),
        ((PARTS, cut, pair), f32),
        ((PARTS, cut, tile), f32),
        ((tile, width), f32),
    ]
    chains = (DEGREE, PARTS)
    semaphores = [
        (1 + line,), (line,), (1 + line, 2), (line, near),
        (1 + line,), (line, near), (1 + line, 2), (line, near),
        (), (), chains, (*chains, line), chains, (*chains, line),
        chains, (*chains, line), chains, (*chains, line), (PARTS,), (PARTS,),
    ]
    size = sum(math.prod(shape) * jnp.dtype(kind).itemsize for shape, kind in memory)
    shapes = [pltpu.VMEM(shape, kind) for shape, kind in memory]
    shapes += [
        pltpu.SMEM((slots,), jnp.int32),
        pltpu.SMEM((slots,), jnp.int32),
        pltpu.SMEM((3,), jnp.float32),
        pltpu.SemaphoreType.DMA((5,)),
    ]
    return size, shapes + [pltpu.SemaphoreType.DMA(shape) for shape in semaphores]


def wide_scratch(far, near, slots, tile, width):
    count = far * near
    cut = width // CHAINS
    return [
        pltpu.VMEM((slots + 1, tile, tile), jnp.bfloat16),
        pltpu.VMEM((count, tile, tile), jnp.bfloat16),
        pltpu.VMEM((count, tile, tile), jnp.bfloat16),
        pltpu.VMEM((near * tile, far * tile), jnp.bfloat16),
        pltpu.VMEM((tile, tile), jnp.bfloat16),
        pltpu.VMEM((DEGREE, CHAINS, far, tile, cut), jnp.bfloat16),
        pltpu.VMEM((DEGREE, CHAINS, near, tile, cut), jnp.float32),
        pltpu.VMEM((DEGREE, CHAINS, near, tile, cut), jnp.float32),
        pltpu.VMEM((CHAINS, tile, cut), jnp.float32),
        pltpu.VMEM((DEGREE, tile, width), jnp.float32),
        pltpu.SemaphoreType.DMA(()),
        pltpu.SemaphoreType.DMA((far,)),
        pltpu.SemaphoreType.DMA((DEGREE, CHAINS)),
        pltpu.SemaphoreType.DMA((DEGREE, CHAINS, far)),
        pltpu.SemaphoreType.DMA((DEGREE, CHAINS)),
        pltpu.SemaphoreType.DMA((DEGREE, CHAINS, near)),
    ]


def local(start_block, tiles, tile_rows, tile_cols, bounds):
    tall, width = start_block.shape
    tile = tiles.shape[-1]
    slots = tiles.shape[2]
    far = lax.axis_size("row")
    near = lax.axis_size("col")
    assert tall == tile and far % 4 == 0
    smem = pl.BlockSpec(memory_space=pltpu.SMEM)
    vmem = pl.BlockSpec(memory_space=pltpu.VMEM)
    body = functools.partial(wide_kernel, far, near, slots, tile, width)
    scratch = wide_scratch(far, near, slots, tile, width)
    in_specs = [smem, smem, smem, vmem, vmem]
    if far % 8 == 0:
        size, shapes = plane_scratch(far // 4, near, slots, tile, width)
        if size <= ROOM:
            body = functools.partial(plane_kernel, far // 4, near, slots, tile, width)
            scratch = shapes
            in_specs = [pl.BlockSpec(memory_space=pl.ANY)] * 5
    return pl.pallas_call(
        body,
        out_shape=pltpu.VMEM((tall, width), jnp.float32),
        in_specs=in_specs,
        out_specs=vmem,
        scratch_shapes=scratch,
        compiler_params=pltpu.CompilerParams(
            collective_id=0, has_side_effects=True, vmem_limit_bytes=60 * 1024 * 1024
        ),
    )(
        tile_rows.reshape(slots),
        tile_cols.reshape(slots),
        bounds,
        start_block,
        tiles.reshape(slots, tile, tile),
    )


def solution(mesh):
    placed = (
        P(("row", "col"), None),
        P("row", "col", None, None, None),
        P("row", "col", None),
        P("row", "col", None),
        P(),
    )
    return jax.shard_map(
        local, mesh=mesh, in_specs=placed, out_specs=P(("row", "col"), None), check_vma=False
    )
```

```python
import functools
import math

import jax
import jax.numpy as jnp
from jax import lax
from jax.experimental import pallas as pl
from jax.experimental.pallas import tpu as pltpu
from jax.sharding import PartitionSpec as P

DEGREE = 4
CHAINS = 2
LAG = 0
PARTS = 4
ROOM = 48 * 1024 * 1024
MESH = pl.DeviceIdType.MESH


def wide_kernel(
    far, near, slots, tile, width,
    rows_ref, cols_ref, bounds_ref, start_ref, tiles_ref, out_ref,
    placed, owned, mirror, window, diagonal, low, partial, arrived, mine, state,
    tile_send, tile_recv, low_send, low_recv, part_send, part_recv,
):
    chips = far // 2
    tall = far // 4
    count = far * near
    cut = width // CHAINS
    row = lax.axis_index("row")
    col = lax.axis_index("col")
    me = row * near + col
    core = row % 2
    mid = row // 2 % 2
    high = row // 4

    def spot(high_at, mid_at, core_at):
        return core_at * chips + high_at * 2 + mid_at

    def row_of(high_at, mid_at, core_at):
        return (high_at * 2 + mid_at) * 2 + core_at

    own_spot = spot(high, mid, core)

    barrier = pltpu.get_barrier_semaphore()

    def greet(step, carry):
        other = (me + step) % count
        pl.semaphore_signal(
            barrier, inc=1, device_id=(other // near, other % near), device_id_type=MESH
        )
        return carry

    lax.fori_loop(1, count, greet, 0)

    line = (1, cut)
    lowest = jnp.full(line, bounds_ref[0], jnp.float32)
    lower = jnp.full(line, bounds_ref[1], jnp.float32)
    upper = jnp.full(line, bounds_ref[2], jnp.float32)
    half_width = (upper - lower) * 0.5
    center = (upper + lower) * 0.5
    sigma_one = half_width / (lowest - center)

    def columns(chain):
        return slice(chain * cut, (chain + 1) * cut)

    for chain in range(CHAINS):
        low[0, chain, own_spot] = start_ref[:, columns(chain)].astype(jnp.bfloat16)

    for slot in range(slots):
        placed[slot] = tiles_ref[slot]
    placed[slots] = jnp.zeros((tile, tile), jnp.bfloat16)
    places = []
    for slot in range(slots):
        glob_row = rows_ref[slot]
        glob_col = cols_ref[slot]
        place = (glob_col // near) * near + (glob_row - row * near)
        places.append(jnp.where(glob_row >= 0, place, -1))

    def put(position, carry):
        chosen = jnp.int32(slots)
        for slot in range(slots):
            chosen = jnp.where(places[slot] == position, slot, chosen)
        owned[position] = placed[chosen]
        return carry

    lax.fori_loop(0, count, put, 0)
    diagonal[...] = owned[me]
    mirror[me] = diagonal[...]
    owned[me] = jnp.zeros((tile, tile), jnp.bfloat16)

    pl.semaphore_wait(barrier, count - 1)

    flip = high >= tall // 2
    near_end = jnp.where(flip, tall - 1 - high, high)

    def along(position):
        return jnp.where(flip, tall - 1 - position, position)

    def ranked(index):
        return index + jnp.where(index >= near_end, 1, 0)

    def send_low(step, chain, place, target_row):
        pltpu.make_async_remote_copy(
            src_ref=low.at[step, chain, place],
            dst_ref=low.at[step, chain, place],
            send_sem=low_send.at[step, chain],
            recv_sem=low_recv.at[step, chain, place],
            device_id=(target_row, col),
            device_id_type=MESH,
        ).start()

    def await_low(step, chain, place):
        here = low.at[step, chain, place]
        pltpu.make_async_copy(here, here, low_recv.at[step, chain, place]).wait()

    def begin(step, chain):
        send_low(step, chain, own_spot, row_of(high, 1 - mid, core))
        for index in range(tall - 1):
            send_low(step, chain, own_spot, row_of(along(ranked(index)), mid, core))
        send_low(step, chain, own_spot, row_of(high, mid, 1 - core))

    def forward_line(step, chain):
        for index in range(tall - 1):
            place = spot(along(ranked(index)), mid, core)
            await_low(step, chain, place)
            send_low(step, chain, place, row_of(high, 1 - mid, core))
            send_low(step, chain, place, row_of(high, mid, 1 - core))

    def forward_mid(step, chain):
        for index in range(tall):
            source = high if index == 0 else along(ranked(index - 1))
            place = spot(source, 1 - mid, core)
            await_low(step, chain, place)
            send_low(step, chain, place, row_of(high, mid, 1 - core))

    def await_core(step, chain):
        for offset in range(tall):
            for mid_at in range(2):
                await_low(step, chain, spot((high + offset) % tall, mid_at, 1 - core))

    def send_tiles(high_at):
        inner = me % (4 * near)

        def send_tile(offset, carry):
            other = high_at * (4 * near) + (inner + offset) % (4 * near)
            pltpu.make_async_remote_copy(
                src_ref=owned.at[other],
                dst_ref=mirror.at[me],
                send_sem=tile_send,
                recv_sem=tile_recv.at[row],
                device_id=(other // near, other % near),
                device_id_type=MESH,
            ).start()
            return carry

        return send_tile

    def send_group(index):
        if index < 0:
            lax.fori_loop(1, 4 * near, send_tiles(high), 0)
        else:
            lax.fori_loop(0, 4 * near, send_tiles(along(ranked(index))), 0)

    def build(step, carry):
        source = (row + far - step) % far
        base = source * near
        group = mirror.at[pl.ds(base, near)]
        pltpu.make_async_copy(group, group, tile_recv.at[source]).wait()
        fill(source)
        return carry

    def fill(source):
        lanes = (source % 2) * chips + source // 2
        lanes = pl.ds(pl.multiple_of(lanes * tile, tile), tile)
        for near_at in range(near):
            index = source * near + near_at
            window[near_at * tile : (near_at + 1) * tile, lanes] = (
                owned[index] + mirror[index].T
            )

    def multiply(step, chain, near_at):
        total = jnp.zeros((tile, cut), jnp.float32)
        matrix = window[pl.ds(pl.multiple_of(near_at * tile, tile), tile), :]
        vectors = low[step, chain].reshape(far * tile, cut)
        return total + jnp.dot(matrix, vectors, preferred_element_type=jnp.float32)

    def product(step, chain):
        for offset in range(1, near):
            other = (col + offset) % near
            partial[step, chain, other] = multiply(step, chain, other)
            pltpu.make_async_remote_copy(
                src_ref=partial.at[step, chain, other],
                dst_ref=arrived.at[step, chain, col],
                send_sem=part_send.at[step, chain],
                recv_sem=part_recv.at[step, chain, col],
                device_id=(row, other),
                device_id_type=MESH,
            ).start()
        mine[chain] = multiply(step, chain, col) + jnp.dot(
            diagonal[...], low[step, chain, own_spot], preferred_element_type=jnp.float32
        )

    def finish(step, chain, sigma):
        total = mine[chain]
        for offset in range(1, near):
            other = (col + offset) % near
            here = arrived.at[step, chain, other]
            pltpu.make_async_copy(here, here, part_recv.at[step, chain, other]).wait()
            total = total + arrived[step, chain, other]
        where = columns(chain)
        current = start_ref[:, where] if step == 0 else state[step - 1, :, where]
        if step == 0:
            following = (total - center * current) * (sigma_one / half_width)
            sigma_next = sigma_one
        else:
            before = start_ref[:, where] if step == 1 else state[step - 2, :, where]
            sigma_next = 1.0 / (2.0 / sigma_one - sigma)
            following = (total - center * current) * (
                2.0 * sigma_next / half_width
            ) - (sigma * sigma_next) * before
        if step == DEGREE - 1:
            out_ref[:, where] = following
        else:
            low[step + 1, chain, own_spot] = following.astype(jnp.bfloat16)
            begin(step + 1, chain)
            state[step, :, where] = following
        return sigma_next

    for chain in range(CHAINS):
        begin(0, chain)
    groups = list(range(tall - 2, -2, -1))
    for index in groups:
        send_group(index)
    for chain in range(CHAINS):
        forward_line(0, chain)
    for chain in range(CHAINS):
        forward_mid(0, chain)

    if near > 1:
        group = mirror.at[pl.ds(row * near, near - 1)]
        pltpu.make_async_copy(group, group, tile_recv.at[row]).wait()
    fill(row)
    lax.fori_loop(1, far, build, 0)

    sigmas = [sigma_one] * CHAINS

    def phase(chain, index):
        step, part = index // 4, index % 4
        if part == 0:
            forward_line(step, chain)
        elif part == 1:
            forward_mid(step, chain)
        elif part == 2:
            await_core(step, chain)
            product(step, chain)
        else:
            sigmas[chain] = finish(step, chain, sigmas[chain])

    for index in range(2, 4 * DEGREE + LAG * (CHAINS - 1)):
        for chain in range(CHAINS):
            own_index = index - LAG * chain
            if 2 <= own_index < 4 * DEGREE:
                phase(chain, own_index)

    group = owned.at[pl.ds(0, count - 1)]
    pltpu.make_async_copy(group, group, tile_send).wait()
    for step in range(DEGREE):
        for chain in range(CHAINS):
            group = low.at[step, chain, pl.ds(0, far - 1)]
            pltpu.make_async_copy(group, group, low_send.at[step, chain]).wait()
            if near > 1:
                group = partial.at[step, chain, pl.ds(0, near - 1)]
                pltpu.make_async_copy(group, group, part_send.at[step, chain]).wait()


def plane_kernel(
    tall, near, slots, tile, width,
    rows_ref, cols_ref, bounds_ref, start_ref, tiles_ref, out_ref,
    placed, owned, direct, mirror, forward, backward, give, take, low,
    part_out, part_in, mine, state, last, end_in, mine_in, peer, start, row_of, col_of, limits, load,
    near_tiles_send, far_tiles_send, core_tiles_send, core_far_send,
    near_tiles_recv, far_tiles_recv, core_tiles_recv, core_far_recv,
    give_send, give_recv, low_send, line_send, low_recv, line_recv,
    part_send, back_send, part_recv, back_recv,
    end_recv, end_back_recv, mine_send, mine_recv, peer_send, peer_recv,
):
    far = 4 * tall
    plane = 2 * near
    line = tall // 2
    half = width // 2
    cut = half // PARTS
    pair = 2 * tile
    row = lax.axis_index("row")
    col = lax.axis_index("col")
    core = row % 2
    mid = row // 2 % 2
    high = row // 4

    def device(high_at, mid_at, core_at, col_at):
        return ((high_at * 2 + mid_at) * 2 + core_at, col_at)

    def beside(offset, core_at=core):
        return device(high, (mid + offset // near) % 2, core_at, (col + offset % near) % near)

    def opposite(offset):
        return offset // near * near + (near - offset % near) % near

    offsets = list(reversed(range(1, plane)))

    partner = device(high, mid, 1 - core, col)

    from_ok = [high != 2 * m for m in range(line)]
    from_at = [
        jnp.where(high < 2 * m, high + tall - 2 * m, high - 2 * m - 1) for m in range(line)
    ]
    into_ok = [high != tall - 1 - 2 * m for m in range(line)]
    into_at = [
        jnp.where(high >= tall - 2 * m, high - tall + 2 * m, high + 2 * m + 1)
        for m in range(line)
    ]

    def copy(src, dst, send, recv, to):
        pltpu.make_async_remote_copy(
            src_ref=src, dst_ref=dst, send_sem=send, recv_sem=recv,
            device_id=to, device_id_type=MESH,
        ).start()

    def wait(ref, sem):
        pltpu.make_async_copy(ref, ref, sem).wait()

    loads = [
        pltpu.make_async_copy(src, dst, load.at[index])
        for index, (src, dst) in enumerate(
            [
                (rows_ref, row_of),
                (cols_ref, col_of),
                (bounds_ref, limits),
                (start_ref, start),
                (tiles_ref, placed.at[pl.ds(0, slots)]),
            ]
        )
    ]
    for item in loads:
        item.start()

    barrier = pltpu.get_barrier_semaphore()

    def greet(to):
        pl.semaphore_signal(barrier, inc=1, device_id=to, device_id_type=MESH)

    for step in reversed(range(1, tall)):
        for offset in range(near):
            greet(device((high + step) % tall, mid, core, (col + offset) % near))
    for offset in offsets:
        greet(beside(offset))
    greet(partner)

    placed[slots] = jnp.zeros((tile, tile), jnp.bfloat16)
    loads[0].wait()
    loads[1].wait()

    def lanes(at, size):
        return pl.ds(pl.multiple_of(at * size, size), size)

    places = []
    for slot in range(slots):
        glob_row = row_of[slot]
        glob_col = col_of[slot]
        place = (glob_col // near) * near + (glob_row - row * near)
        places.append(jnp.where(glob_row >= 0, place, -1))

    def pick(high_at):
        def put(index, carry):
            at, other = high_at * 4 + index // near, index % near
            chosen = jnp.int32(slots)
            for slot in range(slots):
                chosen = jnp.where(places[slot] == at * near + other, slot, chosen)
            owned[at, other] = placed[chosen]
            return carry

        lax.fori_loop(0, 4 * near, put, 0, unroll=4)

    loads[4].wait()
    targets = list(reversed(range(line)))

    @pl.when(into_ok[targets[0]])
    def _():
        pick(into_at[targets[0]])

    def owned_at(high_at, mid_at):
        return pl.ds((high_at * 2 + mid_at) * 2, 2)

    pl.semaphore_wait(barrier, (tall - 1) * near + plane)

    for m in targets:

        @pl.when(into_ok[m])
        def _(m=m):
            if m != targets[0]:
                pick(into_at[m])
            for offset in range(near):
                other = (col + offset) % near
                copy(
                    owned.at[pl.ds(into_at[m] * 4, 4), other], mirror.at[m, core, col],
                    far_tiles_send.at[m], far_tiles_recv.at[m, col],
                    device(into_at[m], mid, core, other),
                )

    def each_slot(act):
        act(0, high)
        for m in reversed(range(line)):

            @pl.when(from_ok[m])
            def _(m=m):
                act(1 + m, from_at[m])

    def send_near(slot, high_at):
        copy(
            owned.at[owned_at(high_at, 1 - mid)], direct.at[slot, mid, core],
            near_tiles_send.at[slot], near_tiles_recv.at[slot],
            device(high, 1 - mid, core, col),
        )
        copy(
            owned.at[owned_at(high_at, mid)], direct.at[slot, mid, core],
            core_tiles_send.at[slot, 0], core_tiles_recv.at[slot, 0], partner,
        )

    each_slot(lambda slot, high_at: pick(high_at))
    each_slot(send_near)

    loads[3].wait()
    give[...] = start[:, lanes(1 - core, half)].T
    copy(give, take, give_send, give_recv, partner)
    kept = start[:, lanes(core, half)].T
    for chain in range(PARTS):
        state[0, chain, :, lanes(core, tile)] = kept[chain * cut : (chain + 1) * cut]


    loads[2].wait()
    span = (1, pair)
    lowest = jnp.full(span, limits[0], jnp.float32)
    lower = jnp.full(span, limits[1], jnp.float32)
    upper = jnp.full(span, limits[2], jnp.float32)
    half_width = (upper - lower) * 0.5
    center = (upper + lower) * 0.5
    sigma_one = half_width / (lowest - center)

    scales = [sigma_one / half_width]
    shares = [None]
    sigma = sigma_one
    for step in range(1, DEGREE):
        sigma_next = 1.0 / (2.0 / sigma_one - sigma)
        scales.append(2.0 * sigma_next / half_width)
        shares.append(sigma * sigma_next)
        sigma = sigma_next

    direct[0, mid, core] = owned[owned_at(high, mid)]
    for m in range(line):

        @pl.when(from_ok[m])
        def _(m=m):
            direct[1 + m, mid, core] = owned[owned_at(from_at[m], mid)]

        @pl.when(jnp.logical_not(from_ok[m]))
        def _(m=m):
            forward[:, (1 + m) * pair : (2 + m) * pair] = jnp.zeros(
                (plane * pair, pair), jnp.bfloat16
            )
            backward[(1 + m) * pair : (2 + m) * pair, :] = jnp.zeros(
                (pair, plane * pair), jnp.bfloat16
            )
            for step in range(DEGREE):
                for chain in range(PARTS):
                    low[step, chain, plane + m] = jnp.zeros((cut, pair), jnp.bfloat16)

        @pl.when(jnp.logical_not(into_ok[m]))
        def _(m=m):
            for chain in range(PARTS):
                for step in range(DEGREE - 1):
                    part_in[step, chain, plane - 1 + m] = jnp.zeros((cut, pair), jnp.bfloat16)
                for other in range(2):
                    end_in[chain, other, plane - 1 + m] = jnp.zeros((cut, tile), jnp.bfloat16)


    def begin(step, chain):
        own = low.at[step, chain, 0]
        for m in reversed(range(line)):

            @pl.when(into_ok[m])
            def _(m=m):
                copy(
                    own, low.at[step, chain, plane + m],
                    line_send.at[step, chain, m], line_recv.at[step, chain, m],
                    device(into_at[m], mid, core, col),
                )

        for offset in offsets:
            copy(
                own, low.at[step, chain, opposite(offset)],
                low_send.at[step, chain], low_recv.at[step, chain], beside(offset),
            )

    wait(take, give_recv)
    for chain in range(PARTS):
        state[0, chain, :, lanes(1 - core, tile)] = take[chain * cut : (chain + 1) * cut, :]
        low[0, chain, 0] = state[0, chain].astype(jnp.bfloat16)
        begin(0, chain)

    def pass_near(slot, high_at):
        block = direct.at[slot, 1 - mid, core]
        wait(block, near_tiles_recv.at[slot])
        copy(
            block, block, core_tiles_send.at[slot, 1], core_tiles_recv.at[slot, 1], partner
        )

    def pass_far(m, offset):
        other = (col + offset) % near
        block = mirror.at[m, core, other]
        wait(block, far_tiles_recv.at[m, other])
        copy(block, block, core_far_send.at[m, other], core_far_recv.at[m, other], partner)

    def spots(slot, mid_at, core_at, other_core, col_at):
        offset = (mid_at + mid) % 2 * near + (col_at + near - col) % near
        inner = pl.ds(pl.multiple_of((offset * 2 + core_at) * tile, tile), tile)
        outer = pl.ds(pl.multiple_of((slot * 2 + other_core) * tile, tile), tile)
        return inner, outer

    def fill_near(slot, mid_at, core_at):
        def fill(index, carry):
            other_core, col_at = index // near, index % near
            inner, outer = spots(slot, mid_at, core_at, other_core, col_at)
            block = direct[slot, mid_at, core_at, other_core, col_at]
            forward[inner, outer] = block
            backward[outer, inner] = block.T
            return carry

        lax.fori_loop(0, 2 * near, fill, 0, unroll=2)

    def fill_slot(slot, high_at):
        fill_near(slot, mid, core)
        fill_near(slot, 1 - mid, core)
        wait(direct.at[slot, mid, 1 - core], core_tiles_recv.at[slot, 0])
        fill_near(slot, mid, 1 - core)
        wait(direct.at[slot, 1 - mid, 1 - core], core_tiles_recv.at[slot, 1])
        fill_near(slot, 1 - mid, 1 - core)

    def fill_far(m, offset, other_core):
        col_at = (col + offset) % near

        def fill(index, carry):
            inner, outer = spots(1 + m, index // 2, index % 2, other_core, col_at)
            block = mirror[m, other_core, col_at, index]
            forward[inner, outer] += block.T
            backward[outer, inner] += block
            return carry

        lax.fori_loop(0, 4, fill, 0, unroll=2)

    def fill_pair(m, offset):
        fill_far(m, offset, core)
        other = (col + offset) % near
        wait(mirror.at[m, 1 - core, other], core_far_recv.at[m, other])
        fill_far(m, offset, 1 - core)

    def when_from(m, act):
        @pl.when(from_ok[m])
        def _():
            act()

    pass_near(0, high)
    order = list(reversed(range(line)))
    for place, m in enumerate(order):
        for offset in range(near):
            when_from(m, lambda m=m, offset=offset: pass_far(m, offset))
            if offset == 0:
                when_from(m, lambda m=m: pass_near(1 + m, from_at[m]))
                if place == 0:
                    fill_slot(0, high)
        if place + 1 < line:
            when_from(m, lambda m=m: fill_slot(1 + m, from_at[m]))
            for offset in range(near):
                when_from(m, lambda m=m, offset=offset: fill_pair(m, offset))
        else:
            when_from(m, lambda m=m: fill_slot(1 + m, from_at[m]))
    for offset in range(near):
        when_from(order[-1], lambda offset=offset: fill_pair(order[-1], offset))

    def product(step, chain):
        wait(low.at[step, chain, pl.ds(1, plane - 1)], low_recv.at[step, chain])
        vectors = jnp.concatenate([low[step, chain, at] for at in range(plane)], axis=1)
        total = jnp.dot(vectors, forward[...], preferred_element_type=jnp.float32)
        kept = total[:, :pair]
        for m in range(line):
            at = plane - 1 + m
            part_out[step, chain, at] = total[:, (1 + m) * pair : (2 + m) * pair].astype(
                jnp.bfloat16
            )
        for m in reversed(range(line)):

            @pl.when(from_ok[m])
            def _(m=m):
                at = plane - 1 + m
                if step < DEGREE - 1:
                    copy(
                        part_out.at[step, chain, at], part_in.at[step, chain, at],
                        back_send.at[step, chain, m], back_recv.at[step, chain, m],
                        device(from_at[m], mid, core, col),
                    )
                    return
                for owner in (core, 1 - core):
                    copy(
                        part_out.at[step, chain, at, :, lanes(owner, tile)],
                        end_in.at[chain, core, at],
                        back_send.at[step, chain, m], end_back_recv.at[chain, core, m],
                        device(from_at[m], mid, owner, col),
                    )

        for m in range(line):

            @pl.when(from_ok[m])
            def _(m=m):
                wait(low.at[step, chain, plane + m], line_recv.at[step, chain, m])

        vectors = jnp.concatenate(
            [low[step, chain, at] for at in [0, *range(plane, plane + line)]], axis=1
        )
        total = jnp.dot(vectors, backward[...], preferred_element_type=jnp.float32)
        mine[chain] = kept + total[:, :pair]
        for offset in offsets:
            part_out[step, chain, offset - 1] = total[
                :, offset * pair : (offset + 1) * pair
            ].astype(jnp.bfloat16)
            if step < DEGREE - 1:
                copy(
                    part_out.at[step, chain, offset - 1],
                    part_in.at[step, chain, opposite(offset) - 1],
                    part_send.at[step, chain], part_recv.at[step, chain], beside(offset),
                )
                continue
            for owner in (core, 1 - core):
                copy(
                    part_out.at[step, chain, offset - 1, :, lanes(owner, tile)],
                    end_in.at[chain, core, opposite(offset) - 1],
                    part_send.at[step, chain], end_recv.at[chain, core],
                    beside(offset, owner),
                )
        if step == DEGREE - 1:
            copy(
                mine.at[chain, :, lanes(1 - core, tile)], mine_in.at[chain],
                mine_send.at[chain], mine_recv.at[chain], partner,
            )

    def finish(step, chain):
        wait(part_in.at[step, chain, pl.ds(0, plane - 1)], part_recv.at[step, chain])
        for m in range(line):

            @pl.when(into_ok[m])
            def _(m=m):
                wait(part_in.at[step, chain, plane - 1 + m], back_recv.at[step, chain, m])

        total = mine[chain]
        for at in range(plane - 1 + line):
            total = total + part_in[step, chain, at].astype(jnp.float32)
        current = state[step, chain]
        following = (total - center * current) * scales[step]
        if step > 0:
            following = following - shares[step] * state[step - 1, chain]
        low[step + 1, chain, 0] = following.astype(jnp.bfloat16)
        begin(step + 1, chain)
        state[step + 1, chain] = following
        if step + 1 >= DEGREE - 2:
            at = step + 3 - DEGREE
            copy(
                state.at[step + 1, chain, :, lanes(1 - core, tile)], peer.at[at, chain],
                peer_send.at[at, chain], peer_recv.at[at, chain], partner,
            )

    def end(chain, owned_half):
        half_at = core if owned_half else 1 - core
        wait(end_in.at[chain, half_at, pl.ds(0, plane - 1)], end_recv.at[chain, half_at])
        for m in range(line):

            @pl.when(into_ok[m])
            def _(m=m):
                wait(end_in.at[chain, half_at, plane - 1 + m], end_back_recv.at[chain, half_at, m])

        if owned_half:
            where = lanes(core, tile)
            total = mine[chain, :, where]
            current = state[DEGREE - 1, chain, :, where]
            before = state[DEGREE - 2, chain, :, where]
        else:
            wait(mine_in.at[chain], mine_recv.at[chain])
            for at in range(2):
                wait(peer.at[at, chain], peer_recv.at[at, chain])
            total = mine_in[chain]
            current = peer[1, chain]
            before = peer[0, chain]
        for at in range(plane - 1 + line):
            total = total + end_in[chain, half_at, at].astype(jnp.float32)
        following = (total - center[:, :tile] * current) * scales[DEGREE - 1][:, :tile]
        last[0 if owned_half else 1, chain] = following - shares[DEGREE - 1][:, :tile] * before

    def close_near(slot, high_at):
        block = direct.at[slot, mid, core]
        wait(block, near_tiles_send.at[slot])
        wait(block, core_tiles_send.at[slot, 0])
        wait(block, core_tiles_send.at[slot, 1])

    def close_tiles():
        wait(give, give_send)
        each_slot(close_near)
        for m in range(line):

            @pl.when(from_ok[m])
            def _(m=m):
                for other in range(near):
                    wait(mirror.at[m, core, other], core_far_send.at[m, other])

            @pl.when(into_ok[m])
            def _(m=m):
                wait(mirror.at[m, core], far_tiles_send.at[m])

    def close_steps(steps):
        for m in range(line):

            @pl.when(from_ok[m])
            def _(m=m):
                for step in steps:
                    for chain in range(PARTS):
                        at = plane - 1 + m
                        wait(part_out.at[step, chain, at], back_send.at[step, chain, m])

            @pl.when(into_ok[m])
            def _(m=m):
                for step in steps:
                    for chain in range(PARTS):
                        wait(low.at[step, chain, 0], line_send.at[step, chain, m])

        for step in steps:
            for chain in range(PARTS):
                wait(low.at[step, chain, pl.ds(1, plane - 1)], low_send.at[step, chain])
                wait(part_out.at[step, chain, pl.ds(0, plane - 1)], part_send.at[step, chain])

    for step in range(DEGREE):
        for chain in range(PARTS):
            product(step, chain)
        if step == DEGREE - 1:
            close_tiles()
            close_steps(range(step))
            for chain in range(PARTS):
                end(chain, True)
                end(chain, False)
            break
        for chain in range(PARTS):
            finish(step, chain)

    out_ref[:, lanes(core, half)] = last[0].reshape(half, tile).T
    out_ref[:, lanes(1 - core, half)] = last[1].reshape(half, tile).T

    for chain in range(PARTS):
        wait(mine_in.at[chain], mine_send.at[chain])
        for at in range(2):
            wait(peer.at[at, chain], peer_send.at[at, chain])
    close_steps([DEGREE - 1])


def plane_scratch(tall, near, slots, tile, width):
    far = 4 * tall
    plane = 2 * near
    line = tall // 2
    half = width // 2
    cut = half // PARTS
    pair = 2 * tile
    bf16, f32 = jnp.bfloat16, jnp.float32
    memory = [
        ((slots + 1, tile, tile), bf16),
        ((far, near, tile, tile), bf16),
        ((1 + line, 2, 2, 2, near, tile, tile), bf16),
        ((line, 2, near, 4, tile, tile), bf16),
        ((plane * pair, (1 + line) * pair), bf16),
        (((1 + line) * pair, plane * pair), bf16),
        ((half, tile), f32),
        ((half, tile), f32),
        ((DEGREE, PARTS, plane + line, cut, pair), bf16),
        ((DEGREE, PARTS, plane - 1 + line, cut, pair), bf16),
        ((DEGREE, PARTS, plane - 1 + line, cut, pair), bf16),
        ((PARTS, cut, pair), f32),
        ((DEGREE, PARTS, cut, pair), f32),
        ((2, PARTS, cut, tile), f32),
        ((PARTS, 2, plane - 1 + line, cut, tile), bf16),
        ((PARTS, cut, tile), f32),
        ((2, PARTS, cut, tile), f32),
        ((tile, width), f32),
    ]
    chains = (DEGREE, PARTS)
    semaphores = [
        (1 + line,), (line,), (1 + line, 2), (line, near),
        (1 + line,), (line, near), (1 + line, 2), (line, near),
        (), (), chains, (*chains, line), chains, (*chains, line),
        chains, (*chains, line), chains, (*chains, line),
        (PARTS, 2), (PARTS, 2, line), (PARTS,), (PARTS,), (2, PARTS), (2, PARTS),
    ]
    size = sum(math.prod(shape) * jnp.dtype(kind).itemsize for shape, kind in memory)
    shapes = [pltpu.VMEM(shape, kind) for shape, kind in memory]
    shapes += [
        pltpu.SMEM((slots,), jnp.int32),
        pltpu.SMEM((slots,), jnp.int32),
        pltpu.SMEM((3,), jnp.float32),
        pltpu.SemaphoreType.DMA((5,)),
    ]
    return size, shapes + [pltpu.SemaphoreType.DMA(shape) for shape in semaphores]


def wide_scratch(far, near, slots, tile, width):
    count = far * near
    cut = width // CHAINS
    return [
        pltpu.VMEM((slots + 1, tile, tile), jnp.bfloat16),
        pltpu.VMEM((count, tile, tile), jnp.bfloat16),
        pltpu.VMEM((count, tile, tile), jnp.bfloat16),
        pltpu.VMEM((near * tile, far * tile), jnp.bfloat16),
        pltpu.VMEM((tile, tile), jnp.bfloat16),
        pltpu.VMEM((DEGREE, CHAINS, far, tile, cut), jnp.bfloat16),
        pltpu.VMEM((DEGREE, CHAINS, near, tile, cut), jnp.float32),
        pltpu.VMEM((DEGREE, CHAINS, near, tile, cut), jnp.float32),
        pltpu.VMEM((CHAINS, tile, cut), jnp.float32),
        pltpu.VMEM((DEGREE, tile, width), jnp.float32),
        pltpu.SemaphoreType.DMA(()),
        pltpu.SemaphoreType.DMA((far,)),
        pltpu.SemaphoreType.DMA((DEGREE, CHAINS)),
        pltpu.SemaphoreType.DMA((DEGREE, CHAINS, far)),
        pltpu.SemaphoreType.DMA((DEGREE, CHAINS)),
        pltpu.SemaphoreType.DMA((DEGREE, CHAINS, near)),
    ]


def local(start_block, tiles, tile_rows, tile_cols, bounds):
    tall, width = start_block.shape
    tile = tiles.shape[-1]
    slots = tiles.shape[2]
    far = lax.axis_size("row")
    near = lax.axis_size("col")
    assert tall == tile and far % 4 == 0
    smem = pl.BlockSpec(memory_space=pltpu.SMEM)
    vmem = pl.BlockSpec(memory_space=pltpu.VMEM)
    body = functools.partial(wide_kernel, far, near, slots, tile, width)
    scratch = wide_scratch(far, near, slots, tile, width)
    in_specs = [smem, smem, smem, vmem, vmem]
    if far % 8 == 0:
        size, shapes = plane_scratch(far // 4, near, slots, tile, width)
        if size <= ROOM:
            body = functools.partial(plane_kernel, far // 4, near, slots, tile, width)
            scratch = shapes
            in_specs = [pl.BlockSpec(memory_space=pl.ANY)] * 5
    return pl.pallas_call(
        body,
        out_shape=pltpu.VMEM((tall, width), jnp.float32),
        in_specs=in_specs,
        out_specs=vmem,
        scratch_shapes=scratch,
        compiler_params=pltpu.CompilerParams(
            collective_id=0, has_side_effects=True, vmem_limit_bytes=60 * 1024 * 1024
        ),
    )(
        tile_rows.reshape(slots),
        tile_cols.reshape(slots),
        bounds,
        start_block,
        tiles.reshape(slots, tile, tile),
    )


def solution(mesh):
    placed = (
        P(("row", "col"), None),
        P("row", "col", None, None, None),
        P("row", "col", None),
        P("row", "col", None),
        P(),
    )
    return jax.shard_map(
        local, mesh=mesh, in_specs=placed, out_specs=P(("row", "col"), None), check_vma=False
    )
```

```python
import functools
import math

import jax
import jax.numpy as jnp
from jax import lax
from jax.experimental import pallas as pl
from jax.experimental.pallas import tpu as pltpu
from jax.sharding import PartitionSpec as P

DEGREE = 4
CHAINS = 2
LAG = 0
PARTS = 4
ROOM = 48 * 1024 * 1024
MESH = pl.DeviceIdType.MESH


def wide_kernel(
    far, near, slots, tile, width,
    rows_ref, cols_ref, bounds_ref, start_ref, tiles_ref, out_ref,
    placed, owned, mirror, window, diagonal, low, partial, arrived, mine, state,
    tile_send, tile_recv, low_send, low_recv, part_send, part_recv,
):
    chips = far // 2
    tall = far // 4
    count = far * near
    cut = width // CHAINS
    row = lax.axis_index("row")
    col = lax.axis_index("col")
    me = row * near + col
    core = row % 2
    mid = row // 2 % 2
    high = row // 4

    def spot(high_at, mid_at, core_at):
        return core_at * chips + high_at * 2 + mid_at

    def row_of(high_at, mid_at, core_at):
        return (high_at * 2 + mid_at) * 2 + core_at

    own_spot = spot(high, mid, core)

    barrier = pltpu.get_barrier_semaphore()

    def greet(step, carry):
        other = (me + step) % count
        pl.semaphore_signal(
            barrier, inc=1, device_id=(other // near, other % near), device_id_type=MESH
        )
        return carry

    lax.fori_loop(1, count, greet, 0)

    line = (1, cut)
    lowest = jnp.full(line, bounds_ref[0], jnp.float32)
    lower = jnp.full(line, bounds_ref[1], jnp.float32)
    upper = jnp.full(line, bounds_ref[2], jnp.float32)
    half_width = (upper - lower) * 0.5
    center = (upper + lower) * 0.5
    sigma_one = half_width / (lowest - center)

    def columns(chain):
        return slice(chain * cut, (chain + 1) * cut)

    for chain in range(CHAINS):
        low[0, chain, own_spot] = start_ref[:, columns(chain)].astype(jnp.bfloat16)

    for slot in range(slots):
        placed[slot] = tiles_ref[slot]
    placed[slots] = jnp.zeros((tile, tile), jnp.bfloat16)
    places = []
    for slot in range(slots):
        glob_row = rows_ref[slot]
        glob_col = cols_ref[slot]
        place = (glob_col // near) * near + (glob_row - row * near)
        places.append(jnp.where(glob_row >= 0, place, -1))

    def put(position, carry):
        chosen = jnp.int32(slots)
        for slot in range(slots):
            chosen = jnp.where(places[slot] == position, slot, chosen)
        owned[position] = placed[chosen]
        return carry

    lax.fori_loop(0, count, put, 0)
    diagonal[...] = owned[me]
    mirror[me] = diagonal[...]
    owned[me] = jnp.zeros((tile, tile), jnp.bfloat16)

    pl.semaphore_wait(barrier, count - 1)

    flip = high >= tall // 2
    near_end = jnp.where(flip, tall - 1 - high, high)

    def along(position):
        return jnp.where(flip, tall - 1 - position, position)

    def ranked(index):
        return index + jnp.where(index >= near_end, 1, 0)

    def send_low(step, chain, place, target_row):
        pltpu.make_async_remote_copy(
            src_ref=low.at[step, chain, place],
            dst_ref=low.at[step, chain, place],
            send_sem=low_send.at[step, chain],
            recv_sem=low_recv.at[step, chain, place],
            device_id=(target_row, col),
            device_id_type=MESH,
        ).start()

    def await_low(step, chain, place):
        here = low.at[step, chain, place]
        pltpu.make_async_copy(here, here, low_recv.at[step, chain, place]).wait()

    def begin(step, chain):
        send_low(step, chain, own_spot, row_of(high, 1 - mid, core))
        for index in range(tall - 1):
            send_low(step, chain, own_spot, row_of(along(ranked(index)), mid, core))
        send_low(step, chain, own_spot, row_of(high, mid, 1 - core))

    def forward_line(step, chain):
        for index in range(tall - 1):
            place = spot(along(ranked(index)), mid, core)
            await_low(step, chain, place)
            send_low(step, chain, place, row_of(high, 1 - mid, core))
            send_low(step, chain, place, row_of(high, mid, 1 - core))

    def forward_mid(step, chain):
        for index in range(tall):
            source = high if index == 0 else along(ranked(index - 1))
            place = spot(source, 1 - mid, core)
            await_low(step, chain, place)
            send_low(step, chain, place, row_of(high, mid, 1 - core))

    def await_core(step, chain):
        for offset in range(tall):
            for mid_at in range(2):
                await_low(step, chain, spot((high + offset) % tall, mid_at, 1 - core))

    def send_tiles(high_at):
        inner = me % (4 * near)

        def send_tile(offset, carry):
            other = high_at * (4 * near) + (inner + offset) % (4 * near)
            pltpu.make_async_remote_copy(
                src_ref=owned.at[other],
                dst_ref=mirror.at[me],
                send_sem=tile_send,
                recv_sem=tile_recv.at[row],
                device_id=(other // near, other % near),
                device_id_type=MESH,
            ).start()
            return carry

        return send_tile

    def send_group(index):
        if index < 0:
            lax.fori_loop(1, 4 * near, send_tiles(high), 0)
        else:
            lax.fori_loop(0, 4 * near, send_tiles(along(ranked(index))), 0)

    def build(step, carry):
        source = (row + far - step) % far
        base = source * near
        group = mirror.at[pl.ds(base, near)]
        pltpu.make_async_copy(group, group, tile_recv.at[source]).wait()
        fill(source)
        return carry

    def fill(source):
        lanes = (source % 2) * chips + source // 2
        lanes = pl.ds(pl.multiple_of(lanes * tile, tile), tile)
        for near_at in range(near):
            index = source * near + near_at
            window[near_at * tile : (near_at + 1) * tile, lanes] = (
                owned[index] + mirror[index].T
            )

    def multiply(step, chain, near_at):
        total = jnp.zeros((tile, cut), jnp.float32)
        matrix = window[pl.ds(pl.multiple_of(near_at * tile, tile), tile), :]
        vectors = low[step, chain].reshape(far * tile, cut)
        return total + jnp.dot(matrix, vectors, preferred_element_type=jnp.float32)

    def product(step, chain):
        for offset in range(1, near):
            other = (col + offset) % near
            partial[step, chain, other] = multiply(step, chain, other)
            pltpu.make_async_remote_copy(
                src_ref=partial.at[step, chain, other],
                dst_ref=arrived.at[step, chain, col],
                send_sem=part_send.at[step, chain],
                recv_sem=part_recv.at[step, chain, col],
                device_id=(row, other),
                device_id_type=MESH,
            ).start()
        mine[chain] = multiply(step, chain, col) + jnp.dot(
            diagonal[...], low[step, chain, own_spot], preferred_element_type=jnp.float32
        )

    def finish(step, chain, sigma):
        total = mine[chain]
        for offset in range(1, near):
            other = (col + offset) % near
            here = arrived.at[step, chain, other]
            pltpu.make_async_copy(here, here, part_recv.at[step, chain, other]).wait()
            total = total + arrived[step, chain, other]
        where = columns(chain)
        current = start_ref[:, where] if step == 0 else state[step - 1, :, where]
        if step == 0:
            following = (total - center * current) * (sigma_one / half_width)
            sigma_next = sigma_one
        else:
            before = start_ref[:, where] if step == 1 else state[step - 2, :, where]
            sigma_next = 1.0 / (2.0 / sigma_one - sigma)
            following = (total - center * current) * (
                2.0 * sigma_next / half_width
            ) - (sigma * sigma_next) * before
        if step == DEGREE - 1:
            out_ref[:, where] = following
        else:
            low[step + 1, chain, own_spot] = following.astype(jnp.bfloat16)
            begin(step + 1, chain)
            state[step, :, where] = following
        return sigma_next

    for chain in range(CHAINS):
        begin(0, chain)
    groups = list(range(tall - 2, -2, -1))
    for index in groups:
        send_group(index)
    for chain in range(CHAINS):
        forward_line(0, chain)
    for chain in range(CHAINS):
        forward_mid(0, chain)

    if near > 1:
        group = mirror.at[pl.ds(row * near, near - 1)]
        pltpu.make_async_copy(group, group, tile_recv.at[row]).wait()
    fill(row)
    lax.fori_loop(1, far, build, 0)

    sigmas = [sigma_one] * CHAINS

    def phase(chain, index):
        step, part = index // 4, index % 4
        if part == 0:
            forward_line(step, chain)
        elif part == 1:
            forward_mid(step, chain)
        elif part == 2:
            await_core(step, chain)
            product(step, chain)
        else:
            sigmas[chain] = finish(step, chain, sigmas[chain])

    for index in range(2, 4 * DEGREE + LAG * (CHAINS - 1)):
        for chain in range(CHAINS):
            own_index = index - LAG * chain
            if 2 <= own_index < 4 * DEGREE:
                phase(chain, own_index)

    group = owned.at[pl.ds(0, count - 1)]
    pltpu.make_async_copy(group, group, tile_send).wait()
    for step in range(DEGREE):
        for chain in range(CHAINS):
            group = low.at[step, chain, pl.ds(0, far - 1)]
            pltpu.make_async_copy(group, group, low_send.at[step, chain]).wait()
            if near > 1:
                group = partial.at[step, chain, pl.ds(0, near - 1)]
                pltpu.make_async_copy(group, group, part_send.at[step, chain]).wait()


def plane_kernel(
    tall, near, slots, tile, width,
    rows_ref, cols_ref, bounds_ref, start_ref, tiles_ref, out_ref,
    placed, owned, direct, mirror, forward, backward, give, take, low,
    part_out, part_in, mine, state, last, end_in, mine_in, peer, start, row_of, col_of, limits, load,
    near_tiles_send, far_tiles_send, core_tiles_send, core_far_send,
    near_tiles_recv, far_tiles_recv, core_tiles_recv, core_far_recv,
    give_send, give_recv, low_send, line_send, low_recv, line_recv,
    part_send, back_send, part_recv, back_recv,
    end_recv, end_back_recv, mine_send, mine_recv, peer_send, peer_recv,
):
    far = 4 * tall
    plane = 2 * near
    line = tall // 2
    half = width // 2
    cut = half // PARTS
    pair = 2 * tile
    row = lax.axis_index("row")
    col = lax.axis_index("col")
    core = row % 2
    mid = row // 2 % 2
    high = row // 4

    def device(high_at, mid_at, core_at, col_at):
        return ((high_at * 2 + mid_at) * 2 + core_at, col_at)

    def beside(offset, core_at=core):
        return device(high, (mid + offset // near) % 2, core_at, (col + offset % near) % near)

    def opposite(offset):
        return offset // near * near + (near - offset % near) % near

    offsets = list(reversed(range(1, plane)))

    partner = device(high, mid, 1 - core, col)

    from_ok = [high != 2 * m for m in range(line)]
    from_at = [
        jnp.where(high < 2 * m, high + tall - 2 * m, high - 2 * m - 1) for m in range(line)
    ]
    into_ok = [high != tall - 1 - 2 * m for m in range(line)]
    into_at = [
        jnp.where(high >= tall - 2 * m, high - tall + 2 * m, high + 2 * m + 1)
        for m in range(line)
    ]

    def copy(src, dst, send, recv, to):
        pltpu.make_async_remote_copy(
            src_ref=src, dst_ref=dst, send_sem=send, recv_sem=recv,
            device_id=to, device_id_type=MESH,
        ).start()

    def wait(ref, sem):
        pltpu.make_async_copy(ref, ref, sem).wait()

    loads = [
        pltpu.make_async_copy(src, dst, load.at[index])
        for index, (src, dst) in enumerate(
            [
                (rows_ref, row_of),
                (cols_ref, col_of),
                (bounds_ref, limits),
                (start_ref, start),
                (tiles_ref, placed.at[pl.ds(0, slots)]),
            ]
        )
    ]
    for item in loads:
        item.start()

    barrier = pltpu.get_barrier_semaphore()

    def greet(to):
        pl.semaphore_signal(barrier, inc=1, device_id=to, device_id_type=MESH)

    for step in reversed(range(1, tall)):
        for offset in range(near):
            greet(device((high + step) % tall, mid, core, (col + offset) % near))
    for offset in offsets:
        greet(beside(offset))
    greet(partner)

    placed[slots] = jnp.zeros((tile, tile), jnp.bfloat16)
    loads[0].wait()
    loads[1].wait()

    def lanes(at, size):
        return pl.ds(pl.multiple_of(at * size, size), size)

    places = []
    for slot in range(slots):
        glob_row = row_of[slot]
        glob_col = col_of[slot]
        place = (glob_col // near) * near + (glob_row - row * near)
        places.append(jnp.where(glob_row >= 0, place, -1))

    def pick(high_at):
        def put(index, carry):
            at, other = high_at * 4 + index // near, index % near
            chosen = jnp.int32(slots)
            for slot in range(slots):
                chosen = jnp.where(places[slot] == at * near + other, slot, chosen)
            owned[at, other] = placed[chosen]
            return carry

        lax.fori_loop(0, 4 * near, put, 0, unroll=4)

    loads[4].wait()
    targets = list(reversed(range(line)))

    @pl.when(into_ok[targets[0]])
    def _():
        pick(into_at[targets[0]])

    def owned_at(high_at, mid_at):
        return pl.ds((high_at * 2 + mid_at) * 2, 2)

    pl.semaphore_wait(barrier, (tall - 1) * near + plane)

    for m in targets:

        @pl.when(into_ok[m])
        def _(m=m):
            if m != targets[0]:
                pick(into_at[m])
            for offset in range(near):
                other = (col + offset) % near
                copy(
                    owned.at[pl.ds(into_at[m] * 4, 4), other], mirror.at[m, core, col],
                    far_tiles_send.at[m], far_tiles_recv.at[m, col],
                    device(into_at[m], mid, core, other),
                )

    def each_slot(act):
        act(0, high)
        for m in reversed(range(line)):

            @pl.when(from_ok[m])
            def _(m=m):
                act(1 + m, from_at[m])

    def send_near(slot, high_at):
        copy(
            owned.at[owned_at(high_at, 1 - mid)], direct.at[slot, mid, core],
            near_tiles_send.at[slot], near_tiles_recv.at[slot],
            device(high, 1 - mid, core, col),
        )
        copy(
            owned.at[owned_at(high_at, mid)], direct.at[slot, mid, core],
            core_tiles_send.at[slot, 0], core_tiles_recv.at[slot, 0], partner,
        )

    each_slot(lambda slot, high_at: pick(high_at))
    each_slot(send_near)

    loads[3].wait()
    give[...] = start[:, lanes(1 - core, half)].T
    copy(give, take, give_send, give_recv, partner)
    kept = start[:, lanes(core, half)].T
    for chain in range(PARTS):
        state[0, chain, :, lanes(core, tile)] = kept[chain * cut : (chain + 1) * cut]


    loads[2].wait()
    span = (1, pair)
    lowest = jnp.full(span, limits[0], jnp.float32)
    lower = jnp.full(span, limits[1], jnp.float32)
    upper = jnp.full(span, limits[2], jnp.float32)
    half_width = (upper - lower) * 0.5
    center = (upper + lower) * 0.5
    sigma_one = half_width / (lowest - center)

    scales = [sigma_one / half_width]
    shares = [None]
    sigma = sigma_one
    for step in range(1, DEGREE):
        sigma_next = 1.0 / (2.0 / sigma_one - sigma)
        scales.append(2.0 * sigma_next / half_width)
        shares.append(sigma * sigma_next)
        sigma = sigma_next

    direct[0, mid, core] = owned[owned_at(high, mid)]
    for m in range(line):

        @pl.when(from_ok[m])
        def _(m=m):
            direct[1 + m, mid, core] = owned[owned_at(from_at[m], mid)]

        @pl.when(jnp.logical_not(from_ok[m]))
        def _(m=m):
            forward[:, (1 + m) * pair : (2 + m) * pair] = jnp.zeros(
                (plane * pair, pair), jnp.bfloat16
            )
            backward[(1 + m) * pair : (2 + m) * pair, :] = jnp.zeros(
                (pair, plane * pair), jnp.bfloat16
            )
            for step in range(DEGREE):
                for chain in range(PARTS):
                    low[step, chain, plane + m] = jnp.zeros((cut, pair), jnp.bfloat16)

        @pl.when(jnp.logical_not(into_ok[m]))
        def _(m=m):
            for chain in range(PARTS):
                for step in range(DEGREE - 1):
                    part_in[step, chain, plane - 1 + m] = jnp.zeros((cut, pair), jnp.bfloat16)
                for other in range(2):
                    end_in[chain, other, plane - 1 + m] = jnp.zeros((cut, tile), jnp.bfloat16)


    def begin(step, chain):
        own = low.at[step, chain, 0]
        for m in reversed(range(line)):

            @pl.when(into_ok[m])
            def _(m=m):
                copy(
                    own, low.at[step, chain, plane + m],
                    line_send.at[step, chain, m], line_recv.at[step, chain, m],
                    device(into_at[m], mid, core, col),
                )

        for offset in offsets:
            copy(
                own, low.at[step, chain, opposite(offset)],
                low_send.at[step, chain], low_recv.at[step, chain], beside(offset),
            )

    wait(take, give_recv)
    for chain in range(PARTS):
        state[0, chain, :, lanes(1 - core, tile)] = take[chain * cut : (chain + 1) * cut, :]
        low[0, chain, 0] = state[0, chain].astype(jnp.bfloat16)
        begin(0, chain)

    def pass_near(slot, high_at):
        block = direct.at[slot, 1 - mid, core]
        wait(block, near_tiles_recv.at[slot])
        copy(
            block, block, core_tiles_send.at[slot, 1], core_tiles_recv.at[slot, 1], partner
        )

    def pass_far(m, offset):
        other = (col + offset) % near
        block = mirror.at[m, core, other]
        wait(block, far_tiles_recv.at[m, other])
        copy(block, block, core_far_send.at[m, other], core_far_recv.at[m, other], partner)

    def spots(slot, mid_at, core_at, other_core, col_at):
        offset = (mid_at + mid) % 2 * near + (col_at + near - col) % near
        inner = pl.ds(pl.multiple_of((offset * 2 + core_at) * tile, tile), tile)
        outer = pl.ds(pl.multiple_of((slot * 2 + other_core) * tile, tile), tile)
        return inner, outer

    def fill_near(slot, mid_at, core_at):
        def fill(index, carry):
            other_core, col_at = index // near, index % near
            inner, outer = spots(slot, mid_at, core_at, other_core, col_at)
            block = direct[slot, mid_at, core_at, other_core, col_at]
            forward[inner, outer] = block
            backward[outer, inner] = block.T
            return carry

        lax.fori_loop(0, 2 * near, fill, 0, unroll=4)

    def fill_slot(slot, high_at):
        fill_near(slot, mid, core)
        fill_near(slot, 1 - mid, core)
        wait(direct.at[slot, mid, 1 - core], core_tiles_recv.at[slot, 0])
        fill_near(slot, mid, 1 - core)
        wait(direct.at[slot, 1 - mid, 1 - core], core_tiles_recv.at[slot, 1])
        fill_near(slot, 1 - mid, 1 - core)

    def fill_far(m, offset, other_core):
        col_at = (col + offset) % near

        def fill(index, carry):
            inner, outer = spots(1 + m, index // 2, index % 2, other_core, col_at)
            block = mirror[m, other_core, col_at, index]
            forward[inner, outer] += block.T
            backward[outer, inner] += block
            return carry

        lax.fori_loop(0, 4, fill, 0, unroll=4)

    def fill_pair(m, offset):
        fill_far(m, offset, core)
        other = (col + offset) % near
        wait(mirror.at[m, 1 - core, other], core_far_recv.at[m, other])
        fill_far(m, offset, 1 - core)

    def when_from(m, act):
        @pl.when(from_ok[m])
        def _():
            act()

    pass_near(0, high)
    order = list(reversed(range(line)))
    for place, m in enumerate(order):
        for offset in range(near):
            when_from(m, lambda m=m, offset=offset: pass_far(m, offset))
            if offset == 0:
                when_from(m, lambda m=m: pass_near(1 + m, from_at[m]))
                if place == 0:
                    fill_slot(0, high)
        if place + 1 < line:
            when_from(m, lambda m=m: fill_slot(1 + m, from_at[m]))
            for offset in range(near):
                when_from(m, lambda m=m, offset=offset: fill_pair(m, offset))
        else:
            when_from(m, lambda m=m: fill_slot(1 + m, from_at[m]))
    for offset in range(near):
        when_from(order[-1], lambda offset=offset: fill_pair(order[-1], offset))

    def product(step, chain):
        wait(low.at[step, chain, pl.ds(1, plane - 1)], low_recv.at[step, chain])
        vectors = jnp.concatenate([low[step, chain, at] for at in range(plane)], axis=1)
        total = jnp.dot(vectors, forward[...], preferred_element_type=jnp.float32)
        kept = total[:, :pair]
        for m in range(line):
            at = plane - 1 + m
            part_out[step, chain, at] = total[:, (1 + m) * pair : (2 + m) * pair].astype(
                jnp.bfloat16
            )
        for m in reversed(range(line)):

            @pl.when(from_ok[m])
            def _(m=m):
                at = plane - 1 + m
                if step < DEGREE - 1:
                    copy(
                        part_out.at[step, chain, at], part_in.at[step, chain, at],
                        back_send.at[step, chain, m], back_recv.at[step, chain, m],
                        device(from_at[m], mid, core, col),
                    )
                    return
                for owner in (core, 1 - core):
                    copy(
                        part_out.at[step, chain, at, :, lanes(owner, tile)],
                        end_in.at[chain, core, at],
                        back_send.at[step, chain, m], end_back_recv.at[chain, core, m],
                        device(from_at[m], mid, owner, col),
                    )

        for m in range(line):

            @pl.when(from_ok[m])
            def _(m=m):
                wait(low.at[step, chain, plane + m], line_recv.at[step, chain, m])

        vectors = jnp.concatenate(
            [low[step, chain, at] for at in [0, *range(plane, plane + line)]], axis=1
        )
        total = jnp.dot(vectors, backward[...], preferred_element_type=jnp.float32)
        mine[chain] = kept + total[:, :pair]
        for offset in offsets:
            part_out[step, chain, offset - 1] = total[
                :, offset * pair : (offset + 1) * pair
            ].astype(jnp.bfloat16)
            if step < DEGREE - 1:
                copy(
                    part_out.at[step, chain, offset - 1],
                    part_in.at[step, chain, opposite(offset) - 1],
                    part_send.at[step, chain], part_recv.at[step, chain], beside(offset),
                )
                continue
            for owner in (core, 1 - core):
                copy(
                    part_out.at[step, chain, offset - 1, :, lanes(owner, tile)],
                    end_in.at[chain, core, opposite(offset) - 1],
                    part_send.at[step, chain], end_recv.at[chain, core],
                    beside(offset, owner),
                )
        if step == DEGREE - 1:
            copy(
                mine.at[chain, :, lanes(1 - core, tile)], mine_in.at[chain],
                mine_send.at[chain], mine_recv.at[chain], partner,
            )

    def finish(step, chain):
        wait(part_in.at[step, chain, pl.ds(0, plane - 1)], part_recv.at[step, chain])
        for m in range(line):

            @pl.when(into_ok[m])
            def _(m=m):
                wait(part_in.at[step, chain, plane - 1 + m], back_recv.at[step, chain, m])

        total = mine[chain]
        for at in range(plane - 1 + line):
            total = total + part_in[step, chain, at].astype(jnp.float32)
        current = state[step, chain]
        following = (total - center * current) * scales[step]
        if step > 0:
            following = following - shares[step] * state[step - 1, chain]
        low[step + 1, chain, 0] = following.astype(jnp.bfloat16)
        begin(step + 1, chain)
        state[step + 1, chain] = following
        if step + 1 >= DEGREE - 2:
            at = step + 3 - DEGREE
            copy(
                state.at[step + 1, chain, :, lanes(1 - core, tile)], peer.at[at, chain],
                peer_send.at[at, chain], peer_recv.at[at, chain], partner,
            )

    def end(chain, owned_half):
        half_at = core if owned_half else 1 - core
        wait(end_in.at[chain, half_at, pl.ds(0, plane - 1)], end_recv.at[chain, half_at])
        for m in range(line):

            @pl.when(into_ok[m])
            def _(m=m):
                wait(end_in.at[chain, half_at, plane - 1 + m], end_back_recv.at[chain, half_at, m])

        if owned_half:
            where = lanes(core, tile)
            total = mine[chain, :, where]
            current = state[DEGREE - 1, chain, :, where]
            before = state[DEGREE - 2, chain, :, where]
        else:
            wait(mine_in.at[chain], mine_recv.at[chain])
            for at in range(2):
                wait(peer.at[at, chain], peer_recv.at[at, chain])
            total = mine_in[chain]
            current = peer[1, chain]
            before = peer[0, chain]
        for at in range(plane - 1 + line):
            total = total + end_in[chain, half_at, at].astype(jnp.float32)
        following = (total - center[:, :tile] * current) * scales[DEGREE - 1][:, :tile]
        last[0 if owned_half else 1, chain] = following - shares[DEGREE - 1][:, :tile] * before

    def close_near(slot, high_at):
        block = direct.at[slot, mid, core]
        wait(block, near_tiles_send.at[slot])
        wait(block, core_tiles_send.at[slot, 0])
        wait(block, core_tiles_send.at[slot, 1])

    def close_tiles():
        wait(give, give_send)
        each_slot(close_near)
        for m in range(line):

            @pl.when(from_ok[m])
            def _(m=m):
                for other in range(near):
                    wait(mirror.at[m, core, other], core_far_send.at[m, other])

            @pl.when(into_ok[m])
            def _(m=m):
                wait(mirror.at[m, core], far_tiles_send.at[m])

    def close_steps(steps):
        for m in range(line):

            @pl.when(from_ok[m])
            def _(m=m):
                for step in steps:
                    for chain in range(PARTS):
                        at = plane - 1 + m
                        wait(part_out.at[step, chain, at], back_send.at[step, chain, m])

            @pl.when(into_ok[m])
            def _(m=m):
                for step in steps:
                    for chain in range(PARTS):
                        wait(low.at[step, chain, 0], line_send.at[step, chain, m])

        for step in steps:
            for chain in range(PARTS):
                wait(low.at[step, chain, pl.ds(1, plane - 1)], low_send.at[step, chain])
                wait(part_out.at[step, chain, pl.ds(0, plane - 1)], part_send.at[step, chain])

    for step in range(DEGREE):
        for chain in range(PARTS):
            product(step, chain)
        if step == DEGREE - 1:
            close_tiles()
            close_steps(range(step))
            for chain in range(PARTS):
                end(chain, True)
                end(chain, False)
            break
        for chain in range(PARTS):
            finish(step, chain)

    out_ref[:, lanes(core, half)] = last[0].reshape(half, tile).T
    out_ref[:, lanes(1 - core, half)] = last[1].reshape(half, tile).T

    for chain in range(PARTS):
        wait(mine_in.at[chain], mine_send.at[chain])
        for at in range(2):
            wait(peer.at[at, chain], peer_send.at[at, chain])
    close_steps([DEGREE - 1])


def plane_scratch(tall, near, slots, tile, width):
    far = 4 * tall
    plane = 2 * near
    line = tall // 2
    half = width // 2
    cut = half // PARTS
    pair = 2 * tile
    bf16, f32 = jnp.bfloat16, jnp.float32
    memory = [
        ((slots + 1, tile, tile), bf16),
        ((far, near, tile, tile), bf16),
        ((1 + line, 2, 2, 2, near, tile, tile), bf16),
        ((line, 2, near, 4, tile, tile), bf16),
        ((plane * pair, (1 + line) * pair), bf16),
        (((1 + line) * pair, plane * pair), bf16),
        ((half, tile), f32),
        ((half, tile), f32),
        ((DEGREE, PARTS, plane + line, cut, pair), bf16),
        ((DEGREE, PARTS, plane - 1 + line, cut, pair), bf16),
        ((DEGREE, PARTS, plane - 1 + line, cut, pair), bf16),
        ((PARTS, cut, pair), f32),
        ((DEGREE, PARTS, cut, pair), f32),
        ((2, PARTS, cut, tile), f32),
        ((PARTS, 2, plane - 1 + line, cut, tile), bf16),
        ((PARTS, cut, tile), f32),
        ((2, PARTS, cut, tile), f32),
        ((tile, width), f32),
    ]
    chains = (DEGREE, PARTS)
    semaphores = [
        (1 + line,), (line,), (1 + line, 2), (line, near),
        (1 + line,), (line, near), (1 + line, 2), (line, near),
        (), (), chains, (*chains, line), chains, (*chains, line),
        chains, (*chains, line), chains, (*chains, line),
        (PARTS, 2), (PARTS, 2, line), (PARTS,), (PARTS,), (2, PARTS), (2, PARTS),
    ]
    size = sum(math.prod(shape) * jnp.dtype(kind).itemsize for shape, kind in memory)
    shapes = [pltpu.VMEM(shape, kind) for shape, kind in memory]
    shapes += [
        pltpu.SMEM((slots,), jnp.int32),
        pltpu.SMEM((slots,), jnp.int32),
        pltpu.SMEM((3,), jnp.float32),
        pltpu.SemaphoreType.DMA((5,)),
    ]
    return size, shapes + [pltpu.SemaphoreType.DMA(shape) for shape in semaphores]


def wide_scratch(far, near, slots, tile, width):
    count = far * near
    cut = width // CHAINS
    return [
        pltpu.VMEM((slots + 1, tile, tile), jnp.bfloat16),
        pltpu.VMEM((count, tile, tile), jnp.bfloat16),
        pltpu.VMEM((count, tile, tile), jnp.bfloat16),
        pltpu.VMEM((near * tile, far * tile), jnp.bfloat16),
        pltpu.VMEM((tile, tile), jnp.bfloat16),
        pltpu.VMEM((DEGREE, CHAINS, far, tile, cut), jnp.bfloat16),
        pltpu.VMEM((DEGREE, CHAINS, near, tile, cut), jnp.float32),
        pltpu.VMEM((DEGREE, CHAINS, near, tile, cut), jnp.float32),
        pltpu.VMEM((CHAINS, tile, cut), jnp.float32),
        pltpu.VMEM((DEGREE, tile, width), jnp.float32),
        pltpu.SemaphoreType.DMA(()),
        pltpu.SemaphoreType.DMA((far,)),
        pltpu.SemaphoreType.DMA((DEGREE, CHAINS)),
        pltpu.SemaphoreType.DMA((DEGREE, CHAINS, far)),
        pltpu.SemaphoreType.DMA((DEGREE, CHAINS)),
        pltpu.SemaphoreType.DMA((DEGREE, CHAINS, near)),
    ]


def local(start_block, tiles, tile_rows, tile_cols, bounds):
    tall, width = start_block.shape
    tile = tiles.shape[-1]
    slots = tiles.shape[2]
    far = lax.axis_size("row")
    near = lax.axis_size("col")
    assert tall == tile and far % 4 == 0
    smem = pl.BlockSpec(memory_space=pltpu.SMEM)
    vmem = pl.BlockSpec(memory_space=pltpu.VMEM)
    body = functools.partial(wide_kernel, far, near, slots, tile, width)
    scratch = wide_scratch(far, near, slots, tile, width)
    in_specs = [smem, smem, smem, vmem, vmem]
    if far % 8 == 0:
        size, shapes = plane_scratch(far // 4, near, slots, tile, width)
        if size <= ROOM:
            body = functools.partial(plane_kernel, far // 4, near, slots, tile, width)
            scratch = shapes
            in_specs = [pl.BlockSpec(memory_space=pl.ANY)] * 5
    return pl.pallas_call(
        body,
        out_shape=pltpu.VMEM((tall, width), jnp.float32),
        in_specs=in_specs,
        out_specs=vmem,
        scratch_shapes=scratch,
        compiler_params=pltpu.CompilerParams(
            collective_id=0, has_side_effects=True, vmem_limit_bytes=60 * 1024 * 1024
        ),
    )(
        tile_rows.reshape(slots),
        tile_cols.reshape(slots),
        bounds,
        start_block,
        tiles.reshape(slots, tile, tile),
    )


def solution(mesh):
    placed = (
        P(("row", "col"), None),
        P("row", "col", None, None, None),
        P("row", "col", None),
        P("row", "col", None),
        P(),
    )
    return jax.shard_map(
        local, mesh=mesh, in_specs=placed, out_specs=P(("row", "col"), None), check_vma=False
    )
```

```python
import functools
import math

import jax
import jax.numpy as jnp
from jax import lax
from jax.experimental import pallas as pl
from jax.experimental.pallas import tpu as pltpu
from jax.sharding import PartitionSpec as P

DEGREE = 4
CHAINS = 2
LAG = 0
PARTS = 4
ROOM = 48 * 1024 * 1024
MESH = pl.DeviceIdType.MESH


def wide_kernel(
    far, near, slots, tile, width,
    rows_ref, cols_ref, bounds_ref, start_ref, tiles_ref, out_ref,
    placed, owned, mirror, window, diagonal, low, partial, arrived, mine, state,
    tile_send, tile_recv, low_send, low_recv, part_send, part_recv,
):
    chips = far // 2
    tall = far // 4
    count = far * near
    cut = width // CHAINS
    row = lax.axis_index("row")
    col = lax.axis_index("col")
    me = row * near + col
    core = row % 2
    mid = row // 2 % 2
    high = row // 4

    def spot(high_at, mid_at, core_at):
        return core_at * chips + high_at * 2 + mid_at

    def row_of(high_at, mid_at, core_at):
        return (high_at * 2 + mid_at) * 2 + core_at

    own_spot = spot(high, mid, core)

    barrier = pltpu.get_barrier_semaphore()

    def greet(step, carry):
        other = (me + step) % count
        pl.semaphore_signal(
            barrier, inc=1, device_id=(other // near, other % near), device_id_type=MESH
        )
        return carry

    lax.fori_loop(1, count, greet, 0)

    line = (1, cut)
    lowest = jnp.full(line, bounds_ref[0], jnp.float32)
    lower = jnp.full(line, bounds_ref[1], jnp.float32)
    upper = jnp.full(line, bounds_ref[2], jnp.float32)
    half_width = (upper - lower) * 0.5
    center = (upper + lower) * 0.5
    sigma_one = half_width / (lowest - center)

    def columns(chain):
        return slice(chain * cut, (chain + 1) * cut)

    for chain in range(CHAINS):
        low[0, chain, own_spot] = start_ref[:, columns(chain)].astype(jnp.bfloat16)

    for slot in range(slots):
        placed[slot] = tiles_ref[slot]
    placed[slots] = jnp.zeros((tile, tile), jnp.bfloat16)
    places = []
    for slot in range(slots):
        glob_row = rows_ref[slot]
        glob_col = cols_ref[slot]
        place = (glob_col // near) * near + (glob_row - row * near)
        places.append(jnp.where(glob_row >= 0, place, -1))

    def put(position, carry):
        chosen = jnp.int32(slots)
        for slot in range(slots):
            chosen = jnp.where(places[slot] == position, slot, chosen)
        owned[position] = placed[chosen]
        return carry

    lax.fori_loop(0, count, put, 0)
    diagonal[...] = owned[me]
    mirror[me] = diagonal[...]
    owned[me] = jnp.zeros((tile, tile), jnp.bfloat16)

    pl.semaphore_wait(barrier, count - 1)

    flip = high >= tall // 2
    near_end = jnp.where(flip, tall - 1 - high, high)

    def along(position):
        return jnp.where(flip, tall - 1 - position, position)

    def ranked(index):
        return index + jnp.where(index >= near_end, 1, 0)

    def send_low(step, chain, place, target_row):
        pltpu.make_async_remote_copy(
            src_ref=low.at[step, chain, place],
            dst_ref=low.at[step, chain, place],
            send_sem=low_send.at[step, chain],
            recv_sem=low_recv.at[step, chain, place],
            device_id=(target_row, col),
            device_id_type=MESH,
        ).start()

    def await_low(step, chain, place):
        here = low.at[step, chain, place]
        pltpu.make_async_copy(here, here, low_recv.at[step, chain, place]).wait()

    def begin(step, chain):
        send_low(step, chain, own_spot, row_of(high, 1 - mid, core))
        for index in range(tall - 1):
            send_low(step, chain, own_spot, row_of(along(ranked(index)), mid, core))
        send_low(step, chain, own_spot, row_of(high, mid, 1 - core))

    def forward_line(step, chain):
        for index in range(tall - 1):
            place = spot(along(ranked(index)), mid, core)
            await_low(step, chain, place)
            send_low(step, chain, place, row_of(high, 1 - mid, core))
            send_low(step, chain, place, row_of(high, mid, 1 - core))

    def forward_mid(step, chain):
        for index in range(tall):
            source = high if index == 0 else along(ranked(index - 1))
            place = spot(source, 1 - mid, core)
            await_low(step, chain, place)
            send_low(step, chain, place, row_of(high, mid, 1 - core))

    def await_core(step, chain):
        for offset in range(tall):
            for mid_at in range(2):
                await_low(step, chain, spot((high + offset) % tall, mid_at, 1 - core))

    def send_tiles(high_at):
        inner = me % (4 * near)

        def send_tile(offset, carry):
            other = high_at * (4 * near) + (inner + offset) % (4 * near)
            pltpu.make_async_remote_copy(
                src_ref=owned.at[other],
                dst_ref=mirror.at[me],
                send_sem=tile_send,
                recv_sem=tile_recv.at[row],
                device_id=(other // near, other % near),
                device_id_type=MESH,
            ).start()
            return carry

        return send_tile

    def send_group(index):
        if index < 0:
            lax.fori_loop(1, 4 * near, send_tiles(high), 0)
        else:
            lax.fori_loop(0, 4 * near, send_tiles(along(ranked(index))), 0)

    def build(step, carry):
        source = (row + far - step) % far
        base = source * near
        group = mirror.at[pl.ds(base, near)]
        pltpu.make_async_copy(group, group, tile_recv.at[source]).wait()
        fill(source)
        return carry

    def fill(source):
        lanes = (source % 2) * chips + source // 2
        lanes = pl.ds(pl.multiple_of(lanes * tile, tile), tile)
        for near_at in range(near):
            index = source * near + near_at
            window[near_at * tile : (near_at + 1) * tile, lanes] = (
                owned[index] + mirror[index].T
            )

    def multiply(step, chain, near_at):
        total = jnp.zeros((tile, cut), jnp.float32)
        matrix = window[pl.ds(pl.multiple_of(near_at * tile, tile), tile), :]
        vectors = low[step, chain].reshape(far * tile, cut)
        return total + jnp.dot(matrix, vectors, preferred_element_type=jnp.float32)

    def product(step, chain):
        for offset in range(1, near):
            other = (col + offset) % near
            partial[step, chain, other] = multiply(step, chain, other)
            pltpu.make_async_remote_copy(
                src_ref=partial.at[step, chain, other],
                dst_ref=arrived.at[step, chain, col],
                send_sem=part_send.at[step, chain],
                recv_sem=part_recv.at[step, chain, col],
                device_id=(row, other),
                device_id_type=MESH,
            ).start()
        mine[chain] = multiply(step, chain, col) + jnp.dot(
            diagonal[...], low[step, chain, own_spot], preferred_element_type=jnp.float32
        )

    def finish(step, chain, sigma):
        total = mine[chain]
        for offset in range(1, near):
            other = (col + offset) % near
            here = arrived.at[step, chain, other]
            pltpu.make_async_copy(here, here, part_recv.at[step, chain, other]).wait()
            total = total + arrived[step, chain, other]
        where = columns(chain)
        current = start_ref[:, where] if step == 0 else state[step - 1, :, where]
        if step == 0:
            following = (total - center * current) * (sigma_one / half_width)
            sigma_next = sigma_one
        else:
            before = start_ref[:, where] if step == 1 else state[step - 2, :, where]
            sigma_next = 1.0 / (2.0 / sigma_one - sigma)
            following = (total - center * current) * (
                2.0 * sigma_next / half_width
            ) - (sigma * sigma_next) * before
        if step == DEGREE - 1:
            out_ref[:, where] = following
        else:
            low[step + 1, chain, own_spot] = following.astype(jnp.bfloat16)
            begin(step + 1, chain)
            state[step, :, where] = following
        return sigma_next

    for chain in range(CHAINS):
        begin(0, chain)
    groups = list(range(tall - 2, -2, -1))
    for index in groups:
        send_group(index)
    for chain in range(CHAINS):
        forward_line(0, chain)
    for chain in range(CHAINS):
        forward_mid(0, chain)

    if near > 1:
        group = mirror.at[pl.ds(row * near, near - 1)]
        pltpu.make_async_copy(group, group, tile_recv.at[row]).wait()
    fill(row)
    lax.fori_loop(1, far, build, 0)

    sigmas = [sigma_one] * CHAINS

    def phase(chain, index):
        step, part = index // 4, index % 4
        if part == 0:
            forward_line(step, chain)
        elif part == 1:
            forward_mid(step, chain)
        elif part == 2:
            await_core(step, chain)
            product(step, chain)
        else:
            sigmas[chain] = finish(step, chain, sigmas[chain])

    for index in range(2, 4 * DEGREE + LAG * (CHAINS - 1)):
        for chain in range(CHAINS):
            own_index = index - LAG * chain
            if 2 <= own_index < 4 * DEGREE:
                phase(chain, own_index)

    group = owned.at[pl.ds(0, count - 1)]
    pltpu.make_async_copy(group, group, tile_send).wait()
    for step in range(DEGREE):
        for chain in range(CHAINS):
            group = low.at[step, chain, pl.ds(0, far - 1)]
            pltpu.make_async_copy(group, group, low_send.at[step, chain]).wait()
            if near > 1:
                group = partial.at[step, chain, pl.ds(0, near - 1)]
                pltpu.make_async_copy(group, group, part_send.at[step, chain]).wait()


def plane_kernel(
    tall, near, slots, tile, width,
    rows_ref, cols_ref, bounds_ref, start_ref, tiles_ref, out_ref,
    placed, owned, direct, mirror, forward, backward, give, take, low,
    part_out, part_in, mine, state, last, end_in, mine_in, peer, start, row_of, col_of, limits, load,
    near_tiles_send, far_tiles_send, core_tiles_send, core_far_send,
    near_tiles_recv, far_tiles_recv, core_tiles_recv, core_far_recv,
    give_send, give_recv, low_send, line_send, low_recv, line_recv,
    part_send, back_send, part_recv, back_recv,
    end_recv, end_back_recv, mine_send, mine_recv, peer_send, peer_recv,
):
    far = 4 * tall
    plane = 2 * near
    line = tall // 2
    half = width // 2
    cut = half // PARTS
    pair = 2 * tile
    row = lax.axis_index("row")
    col = lax.axis_index("col")
    core = row % 2
    mid = row // 2 % 2
    high = row // 4

    def device(high_at, mid_at, core_at, col_at):
        return ((high_at * 2 + mid_at) * 2 + core_at, col_at)

    def beside(offset, core_at=core):
        return device(high, (mid + offset // near) % 2, core_at, (col + offset % near) % near)

    def opposite(offset):
        return offset // near * near + (near - offset % near) % near

    offsets = list(reversed(range(1, plane)))

    partner = device(high, mid, 1 - core, col)

    from_ok = [high != 2 * m for m in range(line)]
    from_at = [
        jnp.where(high < 2 * m, high + tall - 2 * m, high - 2 * m - 1) for m in range(line)
    ]
    into_ok = [high != tall - 1 - 2 * m for m in range(line)]
    into_at = [
        jnp.where(high >= tall - 2 * m, high - tall + 2 * m, high + 2 * m + 1)
        for m in range(line)
    ]

    def copy(src, dst, send, recv, to):
        pltpu.make_async_remote_copy(
            src_ref=src, dst_ref=dst, send_sem=send, recv_sem=recv,
            device_id=to, device_id_type=MESH,
        ).start()

    def wait(ref, sem):
        pltpu.make_async_copy(ref, ref, sem).wait()

    loads = [
        pltpu.make_async_copy(src, dst, load.at[index])
        for index, (src, dst) in enumerate(
            [
                (rows_ref, row_of),
                (cols_ref, col_of),
                (bounds_ref, limits),
                (start_ref, start),
                (tiles_ref, placed.at[pl.ds(0, slots)]),
            ]
        )
    ]
    for item in loads:
        item.start()

    barrier = pltpu.get_barrier_semaphore()

    def greet(to):
        pl.semaphore_signal(barrier, inc=1, device_id=to, device_id_type=MESH)

    for step in reversed(range(1, tall)):
        for offset in range(near):
            greet(device((high + step) % tall, mid, core, (col + offset) % near))
    for offset in offsets:
        greet(beside(offset))
    greet(partner)

    placed[slots] = jnp.zeros((tile, tile), jnp.bfloat16)
    loads[0].wait()
    loads[1].wait()

    def lanes(at, size):
        return pl.ds(pl.multiple_of(at * size, size), size)

    places = []
    for slot in range(slots):
        glob_row = row_of[slot]
        glob_col = col_of[slot]
        place = (glob_col // near) * near + (glob_row - row * near)
        places.append(jnp.where(glob_row >= 0, place, -1))

    def pick(high_at):
        def put(index, carry):
            at, other = high_at * 4 + index // near, index % near
            chosen = jnp.int32(slots)
            for slot in range(slots):
                chosen = jnp.where(places[slot] == at * near + other, slot, chosen)
            owned[at, other] = placed[chosen]
            return carry

        lax.fori_loop(0, 4 * near, put, 0, unroll=4)

    loads[4].wait()
    targets = list(reversed(range(line)))

    @pl.when(into_ok[targets[0]])
    def _():
        pick(into_at[targets[0]])

    def owned_at(high_at, mid_at):
        return pl.ds((high_at * 2 + mid_at) * 2, 2)

    pl.semaphore_wait(barrier, (tall - 1) * near + plane)

    for m in targets:

        @pl.when(into_ok[m])
        def _(m=m):
            if m != targets[0]:
                pick(into_at[m])
            for offset in range(near):
                other = (col + offset) % near
                copy(
                    owned.at[pl.ds(into_at[m] * 4, 4), other], mirror.at[m, core, col],
                    far_tiles_send.at[m], far_tiles_recv.at[m, col],
                    device(into_at[m], mid, core, other),
                )

    def each_slot(act):
        act(0, high)
        for m in reversed(range(line)):

            @pl.when(from_ok[m])
            def _(m=m):
                act(1 + m, from_at[m])

    def send_near(slot, high_at):
        copy(
            owned.at[owned_at(high_at, 1 - mid)], direct.at[slot, mid, core],
            near_tiles_send.at[slot], near_tiles_recv.at[slot],
            device(high, 1 - mid, core, col),
        )
        copy(
            owned.at[owned_at(high_at, mid)], direct.at[slot, mid, core],
            core_tiles_send.at[slot, 0], core_tiles_recv.at[slot, 0], partner,
        )

    each_slot(lambda slot, high_at: pick(high_at))
    each_slot(send_near)

    loads[3].wait()
    give[...] = start[:, lanes(1 - core, half)].T
    copy(give, take, give_send, give_recv, partner)
    kept = start[:, lanes(core, half)].T
    for chain in range(PARTS):
        state[0, chain, :, lanes(core, tile)] = kept[chain * cut : (chain + 1) * cut]


    loads[2].wait()
    span = (1, pair)
    lowest = jnp.full(span, limits[0], jnp.float32)
    lower = jnp.full(span, limits[1], jnp.float32)
    upper = jnp.full(span, limits[2], jnp.float32)
    half_width = (upper - lower) * 0.5
    center = (upper + lower) * 0.5
    sigma_one = half_width / (lowest - center)

    scales = [sigma_one / half_width]
    shares = [None]
    sigma = sigma_one
    for step in range(1, DEGREE):
        sigma_next = 1.0 / (2.0 / sigma_one - sigma)
        scales.append(2.0 * sigma_next / half_width)
        shares.append(sigma * sigma_next)
        sigma = sigma_next

    direct[0, mid, core] = owned[owned_at(high, mid)]
    for m in range(line):

        @pl.when(from_ok[m])
        def _(m=m):
            direct[1 + m, mid, core] = owned[owned_at(from_at[m], mid)]

        @pl.when(jnp.logical_not(from_ok[m]))
        def _(m=m):
            forward[:, (1 + m) * pair : (2 + m) * pair] = jnp.zeros(
                (plane * pair, pair), jnp.bfloat16
            )
            backward[(1 + m) * pair : (2 + m) * pair, :] = jnp.zeros(
                (pair, plane * pair), jnp.bfloat16
            )
            for step in range(DEGREE):
                for chain in range(PARTS):
                    low[step, chain, plane + m] = jnp.zeros((cut, pair), jnp.bfloat16)

        @pl.when(jnp.logical_not(into_ok[m]))
        def _(m=m):
            for chain in range(PARTS):
                for step in range(DEGREE - 1):
                    part_in[step, chain, plane - 1 + m] = jnp.zeros((cut, pair), jnp.bfloat16)
                for other in range(2):
                    end_in[chain, other, plane - 1 + m] = jnp.zeros((cut, tile), jnp.bfloat16)


    def begin(step, chain):
        own = low.at[step, chain, 0]
        for m in reversed(range(line)):

            @pl.when(into_ok[m])
            def _(m=m):
                copy(
                    own, low.at[step, chain, plane + m],
                    line_send.at[step, chain, m], line_recv.at[step, chain, m],
                    device(into_at[m], mid, core, col),
                )

        for offset in offsets:
            copy(
                own, low.at[step, chain, opposite(offset)],
                low_send.at[step, chain], low_recv.at[step, chain], beside(offset),
            )

    wait(take, give_recv)
    for chain in range(PARTS):
        state[0, chain, :, lanes(1 - core, tile)] = take[chain * cut : (chain + 1) * cut, :]
        low[0, chain, 0] = state[0, chain].astype(jnp.bfloat16)
        begin(0, chain)

    def pass_near(slot, high_at):
        block = direct.at[slot, 1 - mid, core]
        wait(block, near_tiles_recv.at[slot])
        copy(
            block, block, core_tiles_send.at[slot, 1], core_tiles_recv.at[slot, 1], partner
        )

    def pass_far(m, offset):
        other = (col + offset) % near
        block = mirror.at[m, core, other]
        wait(block, far_tiles_recv.at[m, other])
        copy(block, block, core_far_send.at[m, other], core_far_recv.at[m, other], partner)

    def spots(slot, mid_at, core_at, other_core, col_at):
        offset = (mid_at + mid) % 2 * near + (col_at + near - col) % near
        inner = pl.ds(pl.multiple_of((offset * 2 + core_at) * tile, tile), tile)
        outer = pl.ds(pl.multiple_of((slot * 2 + other_core) * tile, tile), tile)
        return inner, outer

    def fill_near(slot, mid_at, core_at):
        def fill(index, carry):
            other_core, col_at = index // near, index % near
            inner, outer = spots(slot, mid_at, core_at, other_core, col_at)
            block = direct[slot, mid_at, core_at, other_core, col_at]
            forward[inner, outer] = block
            backward[outer, inner] = block.T
            return carry

        lax.fori_loop(0, 2 * near, fill, 0, unroll=4)

    def fill_slot(slot, high_at):
        fill_near(slot, mid, core)
        fill_near(slot, 1 - mid, core)
        wait(direct.at[slot, mid, 1 - core], core_tiles_recv.at[slot, 0])
        fill_near(slot, mid, 1 - core)
        wait(direct.at[slot, 1 - mid, 1 - core], core_tiles_recv.at[slot, 1])
        fill_near(slot, 1 - mid, 1 - core)

    def fill_far(m, offset, other_core):
        col_at = (col + offset) % near

        def fill(index, carry):
            inner, outer = spots(1 + m, index // 2, index % 2, other_core, col_at)
            block = mirror[m, other_core, col_at, index]
            forward[inner, outer] += block.T
            backward[outer, inner] += block
            return carry

        lax.fori_loop(0, 4, fill, 0, unroll=4)

    def fill_pair(m, offset):
        fill_far(m, offset, core)
        other = (col + offset) % near
        wait(mirror.at[m, 1 - core, other], core_far_recv.at[m, other])
        fill_far(m, offset, 1 - core)

    def when_from(m, act):
        @pl.when(from_ok[m])
        def _():
            act()

    pass_near(0, high)
    order = list(reversed(range(line)))
    for place, m in enumerate(order):
        for offset in range(near):
            when_from(m, lambda m=m, offset=offset: pass_far(m, offset))
            if offset == 0:
                when_from(m, lambda m=m: pass_near(1 + m, from_at[m]))
                if place == 0:
                    fill_slot(0, high)
        if place + 1 < line:
            when_from(m, lambda m=m: fill_slot(1 + m, from_at[m]))
            for offset in range(near):
                when_from(m, lambda m=m, offset=offset: fill_pair(m, offset))
        else:
            when_from(m, lambda m=m: fill_slot(1 + m, from_at[m]))
    for offset in range(near):
        when_from(order[-1], lambda offset=offset: fill_pair(order[-1], offset))

    def product(step, chain):
        wait(low.at[step, chain, pl.ds(1, plane - 1)], low_recv.at[step, chain])
        vectors = jnp.concatenate([low[step, chain, at] for at in range(plane)], axis=1)
        total = jnp.dot(vectors, forward[...], preferred_element_type=jnp.float32)
        kept = total[:, :pair]
        for m in range(line):
            at = plane - 1 + m
            part_out[step, chain, at] = total[:, (1 + m) * pair : (2 + m) * pair].astype(
                jnp.bfloat16
            )
        for m in reversed(range(line)):

            @pl.when(from_ok[m])
            def _(m=m):
                at = plane - 1 + m
                if step < DEGREE - 1:
                    copy(
                        part_out.at[step, chain, at], part_in.at[step, chain, at],
                        back_send.at[step, chain, m], back_recv.at[step, chain, m],
                        device(from_at[m], mid, core, col),
                    )
                    return
                for owner in (core, 1 - core):
                    copy(
                        part_out.at[step, chain, at, :, lanes(owner, tile)],
                        end_in.at[chain, core, at],
                        back_send.at[step, chain, m], end_back_recv.at[chain, core, m],
                        device(from_at[m], mid, owner, col),
                    )

        for m in range(line):

            @pl.when(from_ok[m])
            def _(m=m):
                wait(low.at[step, chain, plane + m], line_recv.at[step, chain, m])

        vectors = jnp.concatenate(
            [low[step, chain, at] for at in [0, *range(plane, plane + line)]], axis=1
        )
        total = jnp.dot(vectors, backward[...], preferred_element_type=jnp.float32)
        mine[chain] = kept + total[:, :pair]
        for offset in offsets:
            part_out[step, chain, offset - 1] = total[
                :, offset * pair : (offset + 1) * pair
            ].astype(jnp.bfloat16)
            if step < DEGREE - 1:
                copy(
                    part_out.at[step, chain, offset - 1],
                    part_in.at[step, chain, opposite(offset) - 1],
                    part_send.at[step, chain], part_recv.at[step, chain], beside(offset),
                )
                continue
            for owner in (core, 1 - core):
                copy(
                    part_out.at[step, chain, offset - 1, :, lanes(owner, tile)],
                    end_in.at[chain, core, opposite(offset) - 1],
                    part_send.at[step, chain], end_recv.at[chain, core],
                    beside(offset, owner),
                )
        if step == DEGREE - 1:
            copy(
                mine.at[chain, :, lanes(1 - core, tile)], mine_in.at[chain],
                mine_send.at[chain], mine_recv.at[chain], partner,
            )

    def finish(step, chain):
        wait(part_in.at[step, chain, pl.ds(0, plane - 1)], part_recv.at[step, chain])
        for m in range(line):

            @pl.when(into_ok[m])
            def _(m=m):
                wait(part_in.at[step, chain, plane - 1 + m], back_recv.at[step, chain, m])

        total = mine[chain]
        for at in range(plane - 1 + line):
            total = total + part_in[step, chain, at].astype(jnp.float32)
        current = state[step, chain]
        following = (total - center * current) * scales[step]
        if step > 0:
            following = following - shares[step] * state[step - 1, chain]
        low[step + 1, chain, 0] = following.astype(jnp.bfloat16)
        begin(step + 1, chain)
        state[step + 1, chain] = following
        if step + 1 >= DEGREE - 2:
            at = step + 3 - DEGREE
            copy(
                state.at[step + 1, chain, :, lanes(1 - core, tile)], peer.at[at, chain],
                peer_send.at[at, chain], peer_recv.at[at, chain], partner,
            )

    def end(chain, owned_half):
        half_at = core if owned_half else 1 - core
        wait(end_in.at[chain, half_at, pl.ds(0, plane - 1)], end_recv.at[chain, half_at])
        for m in range(line):

            @pl.when(into_ok[m])
            def _(m=m):
                wait(end_in.at[chain, half_at, plane - 1 + m], end_back_recv.at[chain, half_at, m])

        if owned_half:
            where = lanes(core, tile)
            total = mine[chain, :, where]
            current = state[DEGREE - 1, chain, :, where]
            before = state[DEGREE - 2, chain, :, where]
        else:
            wait(mine_in.at[chain], mine_recv.at[chain])
            for at in range(2):
                wait(peer.at[at, chain], peer_recv.at[at, chain])
            total = mine_in[chain]
            current = peer[1, chain]
            before = peer[0, chain]
        for at in range(plane - 1 + line):
            total = total + end_in[chain, half_at, at].astype(jnp.float32)
        following = (total - center[:, :tile] * current) * scales[DEGREE - 1][:, :tile]
        last[0 if owned_half else 1, chain] = following - shares[DEGREE - 1][:, :tile] * before

    def close_near(slot, high_at):
        block = direct.at[slot, mid, core]
        wait(block, near_tiles_send.at[slot])
        wait(block, core_tiles_send.at[slot, 0])
        wait(block, core_tiles_send.at[slot, 1])

    def close_tiles():
        wait(give, give_send)
        each_slot(close_near)
        for m in range(line):

            @pl.when(from_ok[m])
            def _(m=m):
                for other in range(near):
                    wait(mirror.at[m, core, other], core_far_send.at[m, other])

            @pl.when(into_ok[m])
            def _(m=m):
                wait(mirror.at[m, core], far_tiles_send.at[m])

    def close_steps(steps):
        for m in range(line):

            @pl.when(from_ok[m])
            def _(m=m):
                for step in steps:
                    for chain in range(PARTS):
                        at = plane - 1 + m
                        wait(part_out.at[step, chain, at], back_send.at[step, chain, m])

            @pl.when(into_ok[m])
            def _(m=m):
                for step in steps:
                    for chain in range(PARTS):
                        wait(low.at[step, chain, 0], line_send.at[step, chain, m])

        for step in steps:
            for chain in range(PARTS):
                wait(low.at[step, chain, pl.ds(1, plane - 1)], low_send.at[step, chain])
                wait(part_out.at[step, chain, pl.ds(0, plane - 1)], part_send.at[step, chain])

    for step in range(DEGREE):
        for chain in range(PARTS):
            product(step, chain)
        if step == DEGREE - 1:
            close_tiles()
            close_steps(range(step))
            for chain in range(PARTS):
                end(chain, True)
            out_ref[:, lanes(core, half)] = last[0].reshape(half, tile).T
            for chain in range(PARTS):
                end(chain, False)
            break
        for chain in range(PARTS):
            finish(step, chain)

    out_ref[:, lanes(1 - core, half)] = last[1].reshape(half, tile).T

    for chain in range(PARTS):
        wait(mine_in.at[chain], mine_send.at[chain])
        for at in range(2):
            wait(peer.at[at, chain], peer_send.at[at, chain])
    close_steps([DEGREE - 1])


def plane_scratch(tall, near, slots, tile, width):
    far = 4 * tall
    plane = 2 * near
    line = tall // 2
    half = width // 2
    cut = half // PARTS
    pair = 2 * tile
    bf16, f32 = jnp.bfloat16, jnp.float32
    memory = [
        ((slots + 1, tile, tile), bf16),
        ((far, near, tile, tile), bf16),
        ((1 + line, 2, 2, 2, near, tile, tile), bf16),
        ((line, 2, near, 4, tile, tile), bf16),
        ((plane * pair, (1 + line) * pair), bf16),
        (((1 + line) * pair, plane * pair), bf16),
        ((half, tile), f32),
        ((half, tile), f32),
        ((DEGREE, PARTS, plane + line, cut, pair), bf16),
        ((DEGREE, PARTS, plane - 1 + line, cut, pair), bf16),
        ((DEGREE, PARTS, plane - 1 + line, cut, pair), bf16),
        ((PARTS, cut, pair), f32),
        ((DEGREE, PARTS, cut, pair), f32),
        ((2, PARTS, cut, tile), f32),
        ((PARTS, 2, plane - 1 + line, cut, tile), bf16),
        ((PARTS, cut, tile), f32),
        ((2, PARTS, cut, tile), f32),
        ((tile, width), f32),
    ]
    chains = (DEGREE, PARTS)
    semaphores = [
        (1 + line,), (line,), (1 + line, 2), (line, near),
        (1 + line,), (line, near), (1 + line, 2), (line, near),
        (), (), chains, (*chains, line), chains, (*chains, line),
        chains, (*chains, line), chains, (*chains, line),
        (PARTS, 2), (PARTS, 2, line), (PARTS,), (PARTS,), (2, PARTS), (2, PARTS),
    ]
    size = sum(math.prod(shape) * jnp.dtype(kind).itemsize for shape, kind in memory)
    shapes = [pltpu.VMEM(shape, kind) for shape, kind in memory]
    shapes += [
        pltpu.SMEM((slots,), jnp.int32),
        pltpu.SMEM((slots,), jnp.int32),
        pltpu.SMEM((3,), jnp.float32),
        pltpu.SemaphoreType.DMA((5,)),
    ]
    return size, shapes + [pltpu.SemaphoreType.DMA(shape) for shape in semaphores]


def wide_scratch(far, near, slots, tile, width):
    count = far * near
    cut = width // CHAINS
    return [
        pltpu.VMEM((slots + 1, tile, tile), jnp.bfloat16),
        pltpu.VMEM((count, tile, tile), jnp.bfloat16),
        pltpu.VMEM((count, tile, tile), jnp.bfloat16),
        pltpu.VMEM((near * tile, far * tile), jnp.bfloat16),
        pltpu.VMEM((tile, tile), jnp.bfloat16),
        pltpu.VMEM((DEGREE, CHAINS, far, tile, cut), jnp.bfloat16),
        pltpu.VMEM((DEGREE, CHAINS, near, tile, cut), jnp.float32),
        pltpu.VMEM((DEGREE, CHAINS, near, tile, cut), jnp.float32),
        pltpu.VMEM((CHAINS, tile, cut), jnp.float32),
        pltpu.VMEM((DEGREE, tile, width), jnp.float32),
        pltpu.SemaphoreType.DMA(()),
        pltpu.SemaphoreType.DMA((far,)),
        pltpu.SemaphoreType.DMA((DEGREE, CHAINS)),
        pltpu.SemaphoreType.DMA((DEGREE, CHAINS, far)),
        pltpu.SemaphoreType.DMA((DEGREE, CHAINS)),
        pltpu.SemaphoreType.DMA((DEGREE, CHAINS, near)),
    ]


def local(start_block, tiles, tile_rows, tile_cols, bounds):
    tall, width = start_block.shape
    tile = tiles.shape[-1]
    slots = tiles.shape[2]
    far = lax.axis_size("row")
    near = lax.axis_size("col")
    assert tall == tile and far % 4 == 0
    smem = pl.BlockSpec(memory_space=pltpu.SMEM)
    vmem = pl.BlockSpec(memory_space=pltpu.VMEM)
    body = functools.partial(wide_kernel, far, near, slots, tile, width)
    scratch = wide_scratch(far, near, slots, tile, width)
    in_specs = [smem, smem, smem, vmem, vmem]
    if far % 8 == 0:
        size, shapes = plane_scratch(far // 4, near, slots, tile, width)
        if size <= ROOM:
            body = functools.partial(plane_kernel, far // 4, near, slots, tile, width)
            scratch = shapes
            in_specs = [pl.BlockSpec(memory_space=pl.ANY)] * 5
    return pl.pallas_call(
        body,
        out_shape=pltpu.VMEM((tall, width), jnp.float32),
        in_specs=in_specs,
        out_specs=vmem,
        scratch_shapes=scratch,
        compiler_params=pltpu.CompilerParams(
            collective_id=0, has_side_effects=True, vmem_limit_bytes=60 * 1024 * 1024
        ),
    )(
        tile_rows.reshape(slots),
        tile_cols.reshape(slots),
        bounds,
        start_block,
        tiles.reshape(slots, tile, tile),
    )


def solution(mesh):
    placed = (
        P(("row", "col"), None),
        P("row", "col", None, None, None),
        P("row", "col", None),
        P("row", "col", None),
        P(),
    )
    return jax.shard_map(
        local, mesh=mesh, in_specs=placed, out_specs=P(("row", "col"), None), check_vma=False
    )
```
